32 devices in a mesh: shard: 8 (over y, x, core), context: 2 (over z_hi), tensor: 2 (over z_lo).
Axes of the slice: x: 2, y: 2, z: 4 (z_hi: 2, z_lo: 2; z = z_hi * 2 + z_lo), core: 2. Of those that a mesh axis runs over, the one named last changes fastest.
Arguments:
- inputs: bfloat16 [8, 1024, 2048], P('shard', 'context'), may hold values from -6 to 6
- cotangent: bfloat16 [8, 1024, 2048], P('shard', 'context'), may hold values from -6 to 6
- qkv_weight: bfloat16 [2048, 8, 768], P(('shard', 'context'), 'tensor'), may hold values from -0.125 to 0.125
- dense_weight: bfloat16 [2048, 2048], P(('shard', 'context'), 'tensor'), may hold values from -0.25 to 0.25
- up_weight: bfloat16 [2048, 8192], P(('shard', 'context'), 'tensor'), may hold values from -0.125 to 0.125
- down_weight: bfloat16 [2048, 8192], P(('shard', 'context'), 'tensor'), may hold values from -0.0625 to 0.0625
- unit_biases: bfloat16 [8, 1792], P('tensor'), may hold values from -3 to 3
- vectors: bfloat16 [6, 2048], replicated, as said below
- qkv_moments: float32 [2, 2048, 8, 768], P(None, ('shard', 'context'), 'tensor'), as said below
- dense_moments: float32 [2, 2048, 2048], P(None, ('shard', 'context'), 'tensor'), as said below
- up_moments: float32 [2, 2048, 8192], P(None, ('shard', 'context'), 'tensor'), as said below
- down_moments: float32 [2, 2048, 8192], P(None, ('shard', 'context'), 'tensor'), as said below
- unit_moments: float32 [2, 8, 1792], P(None, 'tensor'), as said below
- vector_moments: float32 [2, 6, 2048], replicated, as said below
- step_count: int32 [], replicated, may hold values from 1 to 20
Outputs:
- outputs: bfloat16 [8, 1024, 2048], P('shard', 'context')
- input_grad: float32 [8, 1024, 2048], P('shard', 'context')
- qkv_grad: float32 [2048, 8, 768], P(('shard', 'context'), 'tensor')
- dense_grad: float32 [2048, 2048], P(('shard', 'context'), 'tensor')
- up_grad: float32 [2048, 8192], P(('shard', 'context'), 'tensor')
- down_grad: float32 [2048, 8192], P(('shard', 'context'), 'tensor')
- unit_grad: float32 [8, 1792], P('tensor')
- vector_grad: float32 [6, 2048], replicated
- qkv_moments_new: float32 [2, 2048, 8, 768], P(None, ('shard', 'context'), 'tensor')
- dense_moments_new: float32 [2, 2048, 2048], P(None, ('shard', 'context'), 'tensor')
- up_moments_new: float32 [2, 2048, 8192], P(None, ('shard', 'context'), 'tensor')
- down_moments_new: float32 [2, 2048, 8192], P(None, ('shard', 'context'), 'tensor')
- unit_moments_new: float32 [2, 8, 1792], P(None, 'tensor')
- vector_moments_new: float32 [2, 6, 2048], replicated
- qkv_update: float32 [2048, 8, 768], P(('shard', 'context'), 'tensor')
- dense_update: float32 [2048, 2048], P(('shard', 'context'), 'tensor')
- up_update: float32 [2048, 8192], P(('shard', 'context'), 'tensor')
- down_update: float32 [2048, 8192], P(('shard', 'context'), 'tensor')
- unit_update: float32 [8, 1792], P('tensor')
- vector_update: float32 [6, 2048], replicated
The draws below stay inside these ranges and needn't reach their ends.
Inputs may be any that keep to these rules, and one draw needn't show every extreme that they name: `vectors`: rows 0 and 2 lie between 0.5 and 1.5; the other rows are of order one half. `qkv_moments`: the root mean square states are positive. `dense_moments`: the root mean square states are positive. `up_moments`: the root mean square states are positive. `down_moments`: the root mean square states are positive. `unit_moments`: the root mean square states are positive. `vector_moments`: the root mean square states are positive.
All inputs are finite; a program needn't handle non-finite values.
Results may differ from the reference program's by a relative error of at most 0.009.
Values may be sent and summed in bfloat16 or wider, within the bound.
No kernel may reach another device: no remote copies, remote signals or barrier semaphores. Data moves between devices by JAX's collectives and lax.ppermute only.
A program may use at most 256 MiB of HBM per device.

```python
import math
import jax
import jax.numpy as jnp
from jax import lax

D = 2048
HEADS = 8
HEAD_DIM = 256
FF = 8192
ROTARY = 64
LEN = 1024
SEQUENCES = 8
TOKENS = 8192


def make_moments(key, shape):
    first_key, second_key = jax.random.split(key)
    grad_scale = math.sqrt(TOKENS)
    first_moment = 0.03 * grad_scale * jax.random.normal(first_key, shape, jnp.float32)
    root_state = math.sqrt(0.005 * TOKENS) * jnp.exp(jax.random.uniform(second_key, shape, jnp.float32, -0.75, 0.75))
    return jnp.stack([first_moment, root_state])


def draw_vectors(key, part):
    gain_key, shift_key = jax.random.split(jax.random.fold_in(key, 11))
    gains = jax.random.uniform(gain_key, (6, D), jnp.float32, 0.5, 1.5)
    shifts = 0.5 * jax.random.normal(shift_key, (6, D), jnp.float32)
    row_ids = jnp.arange(6)[:, None]
    chosen = jnp.where((row_ids == 0) | (row_ids == 2), gains, shifts)
    return chosen.astype(jnp.bfloat16)


def draw_qkv_moments(key, part):
    return make_moments(jax.random.fold_in(key, 21), (D, HEADS, 3 * HEAD_DIM))


def draw_dense_moments(key, part):
    return make_moments(jax.random.fold_in(key, 22), (D, HEADS * HEAD_DIM))


def draw_up_moments(key, part):
    return make_moments(jax.random.fold_in(key, 23), (D, FF))


def draw_down_moments(key, part):
    return make_moments(jax.random.fold_in(key, 24), (D, FF))


def draw_unit_moments(key, part):
    return make_moments(jax.random.fold_in(key, 25), (HEADS, 3 * HEAD_DIM + FF // HEADS))


def draw_vector_moments(key, part):
    return make_moments(jax.random.fold_in(key, 26), (6, D))


def shard_levels(rng, dims, cuts, low, top_value):
    level = 1.0
    for dim, shards_of in cuts:
        draws = jax.random.uniform(jax.random.fold_in(jax.random.fold_in(rng, 6), dim), (shards_of,), jnp.float32, low / len(cuts), top_value / len(cuts))
        level = level * jnp.repeat(jnp.exp(draws), dims[dim] // shards_of).reshape((-1,) + (1,) * (len(dims) - 1 - dim))
    return level


def centred(rng, extent, width, most, cuts=(), kind=jnp.bfloat16):
    entries = jax.random.normal(rng, extent, jnp.float32) * width
    if len(cuts) > 0:
        entries = shard_levels(rng, extent, cuts, -0.22, 0.18) * entries
    return jnp.clip(entries, min=-most, max=most).astype(kind)


def setup_inputs(seed: int = 0) -> dict:
    seeds = jax.random.split(jax.random.key(seed), 16)
    inputs = centred(seeds[0], (SEQUENCES, LEN, D), 1.0, 6.0, ((0, 8), (1, 2)))
    cotangent = centred(seeds[1], (SEQUENCES, LEN, D), 1.0, 6.0, ((0, 8), (1, 2)))
    qkv_weight = centred(seeds[2], (D, HEADS, 3 * HEAD_DIM), D ** -0.5, 0.125, ((0, 16), (1, 2)))
    dense_weight = centred(seeds[3], (D, HEADS * HEAD_DIM), (D // 4) ** -0.5, 0.25, ((0, 16), (1, 2)))
    up_weight = centred(seeds[4], (D, FF), D ** -0.5, 0.125, ((0, 16), (1, 2)))
    down_weight = centred(seeds[5], (D, FF), FF ** -0.5, 0.0625, ((0, 16), (1, 2)))
    unit_biases = centred(seeds[6], (HEADS, 3 * HEAD_DIM + FF // HEADS), 0.5, 3.0, ((0, 2),))
    vectors = draw_vectors(jax.random.fold_in(seeds[15], 71), 0)
    qkv_moments = draw_qkv_moments(jax.random.fold_in(seeds[15], 71), 0)
    dense_moments = draw_dense_moments(jax.random.fold_in(seeds[15], 71), 0)
    up_moments = draw_up_moments(jax.random.fold_in(seeds[15], 71), 0)
    down_moments = draw_down_moments(jax.random.fold_in(seeds[15], 71), 0)
    unit_moments = draw_unit_moments(jax.random.fold_in(seeds[15], 71), 0)
    vector_moments = draw_vector_moments(jax.random.fold_in(seeds[15], 71), 0)
    step_count = jax.random.randint(seeds[14], (), 1, 21).astype(jnp.int32)
    return dict(inputs=inputs, cotangent=cotangent, qkv_weight=qkv_weight, dense_weight=dense_weight, up_weight=up_weight, down_weight=down_weight, unit_biases=unit_biases, vectors=vectors, qkv_moments=qkv_moments, dense_moments=dense_moments, up_moments=up_moments, down_moments=down_moments, unit_moments=unit_moments, vector_moments=vector_moments, step_count=step_count)


@jax.custom_vjp
def low(v):
    return lax.optimization_barrier(v.astype(jnp.bfloat16)).astype(jnp.float32)

@jax.custom_vjp
def low_back(v):
    return v

def low_keep(v):
    return (low(v), None)

def low_pass(kept, grad):
    return (grad,)

def back_keep(v):
    return (v, None)

def back_low(kept, grad):
    return (low(grad),)
low.defvjp(low_keep, low_pass)
low_back.defvjp(back_keep, back_low)
EPSILON = 1e-05
BETA_ONE = 0.9
BETA_TWO = 0.95
LEARN_RATE = 0.02
WEIGHT_DECAY = 0.01
ROOT_HALF = 0.7071067811865476
MASKED = -1000000000.0

def normalize(token_rows):
    center = token_rows - lax.optimization_barrier(jnp.mean(token_rows, -1, keepdims=True))
    inv_std = lax.rsqrt(lax.optimization_barrier(jnp.mean(center * center, -1, keepdims=True)) + EPSILON)
    return center * inv_std

def gelu_value(hidden):
    return 0.5 * hidden * (1.0 + lax.erf(hidden * ROOT_HALF))

def angle_table(positions):
    half_index = jnp.arange(ROTARY // 2, dtype=jnp.float32)
    inverse = jnp.exp(half_index * (-2.0 / ROTARY) * math.log(10000.0))
    angles = positions.astype(jnp.float32)[:, None] * inverse[None, :]
    return (jnp.cos(angles), jnp.sin(angles))

def turn(block_data, cosine, sine_table, sign_flip):
    half_width = ROTARY // 2
    first_half = block_data[..., :half_width]
    second_half = block_data[..., half_width:ROTARY]
    cos_part = cosine[None, :, None, :]
    sin_part = sign_flip * sine_table[None, :, None, :]
    return jnp.concatenate([first_half * cos_part - second_half * sin_part, second_half * cos_part + first_half * sin_part, block_data[..., ROTARY:]], -1)

def attend(packed):
    queries = packed[..., :HEAD_DIM]
    key_rows = packed[..., HEAD_DIM:2 * HEAD_DIM]
    value_rows = packed[..., 2 * HEAD_DIM:]
    scores = jnp.einsum('qhe,khe->hqk', queries, key_rows, precision=lax.Precision.HIGHEST) * HEAD_DIM ** (-0.5)
    positions = jnp.arange(LEN)
    scores = jnp.where(positions[:, None] >= positions[None, :], scores, MASKED)
    scores = low_back(scores)
    maximum = lax.optimization_barrier(jnp.max(scores, -1, keepdims=True))
    exponent = jnp.exp(scores - maximum)
    probs = exponent / lax.optimization_barrier(jnp.sum(exponent, -1, keepdims=True))
    mixed = jnp.einsum('hqk,khe->qhe', low(probs), value_rows, precision=lax.Precision.HIGHEST)
    return low(low_back(mixed))

def layer(params, group_inputs):
    qkv_w, dense_w, up_w, down_w, unit_vals, vector_vals = params
    normed = normalize(group_inputs)
    a_attn = low(normed * vector_vals[0] + vector_vals[1])
    a_mlp = low(normed * vector_vals[2] + vector_vals[3])
    linear = low_back(jnp.einsum('gtd,dhe->gthe', a_attn, qkv_w, precision=lax.Precision.HIGHEST))
    linear = linear + unit_vals[:, :3 * HEAD_DIM]
    cosine, sine_table = angle_table(jnp.arange(LEN))
    rotated_q = turn(linear[..., :HEAD_DIM], cosine, sine_table, 1.0)
    rotated_k = turn(linear[..., HEAD_DIM:2 * HEAD_DIM], cosine, sine_table, 1.0)
    packed = low(low_back(jnp.concatenate([rotated_q, rotated_k, linear[..., 2 * HEAD_DIM:]], -1)))
    mixed = lax.map(jax.checkpoint(attend), packed)
    context_flat = mixed.reshape(mixed.shape[0], LEN, HEADS * HEAD_DIM)
    hidden = low_back(jnp.einsum('gtd,df->gtf', a_mlp, up_w, precision=lax.Precision.HIGHEST))
    hidden = hidden + unit_vals[:, 3 * HEAD_DIM:].reshape(FF)
    active = low(gelu_value(hidden))
    branch = jnp.einsum('gtc,dc->gtd', context_flat, dense_w, precision=lax.Precision.HIGHEST)
    branch = branch + jnp.einsum('gtf,df->gtd', active, down_w, precision=lax.Precision.HIGHEST)
    return group_inputs + branch + vector_vals[4] + vector_vals[5]

def adam_step(weight, moments, gradient, count_value, decay_rate):
    first_new = BETA_ONE * moments[0] + (1.0 - BETA_ONE) * gradient
    root_new = jnp.sqrt(BETA_TWO * moments[1] * moments[1] + (1.0 - BETA_TWO) * gradient * gradient)
    fix_one = 1.0 - jnp.power(BETA_ONE, count_value)
    fix_two = 1.0 - jnp.power(BETA_TWO, count_value)
    change = -LEARN_RATE * (first_new / fix_one / (root_new / jnp.sqrt(fix_two) + 1e-08) + decay_rate * weight)
    return (jnp.stack([first_new, root_new]), change)

def reference(inputs, cotangent, qkv_weight, dense_weight, up_weight, down_weight, unit_biases, vectors, qkv_moments, dense_moments, up_moments, down_moments, unit_moments, vector_moments, step_count):
    params = (qkv_weight.astype(jnp.float32), dense_weight.astype(jnp.float32), up_weight.astype(jnp.float32), down_weight.astype(jnp.float32), unit_biases.astype(jnp.float32), vectors.astype(jnp.float32))
    group_size = math.gcd(SEQUENCES, max(1, 4096 // LEN))
    group_count = SEQUENCES // group_size
    input_groups = inputs.astype(jnp.float32).reshape(group_count, group_size, LEN, D)
    cot_groups = cotangent.astype(jnp.float32).reshape(group_count, group_size, LEN, D)

    def one_group(totals, pair):
        group_inputs, group_cot = pair
        result, pullback = jax.vjp(layer, params, group_inputs)
        param_grads, group_grad = pullback(group_cot)
        totals = jax.tree.map(lambda running, extra: running + extra, totals, param_grads)
        return (totals, (result.astype(jnp.bfloat16), group_grad))
    zero_grads = jax.tree.map(jnp.zeros_like, params)
    grads, (result_groups, grad_groups) = lax.scan(one_group, zero_grads, (input_groups, cot_groups))
    outputs = result_groups.reshape(SEQUENCES, LEN, D)
    input_grad = grad_groups.reshape(SEQUENCES, LEN, D)
    count_value = step_count.astype(jnp.float32)
    qkv_new, qkv_change = adam_step(params[0], qkv_moments, grads[0], count_value, WEIGHT_DECAY)
    dense_new, dense_change = adam_step(params[1], dense_moments, grads[1], count_value, WEIGHT_DECAY)
    up_new, up_change = adam_step(params[2], up_moments, grads[2], count_value, WEIGHT_DECAY)
    down_new, down_change = adam_step(params[3], down_moments, grads[3], count_value, WEIGHT_DECAY)
    unit_new, unit_change = adam_step(params[4], unit_moments, grads[4], count_value, 0.0)
    vector_new, vector_change = adam_step(params[5], vector_moments, grads[5], count_value, 0.0)
    return (outputs, input_grad, grads[0], grads[1], grads[2], grads[3], grads[4], grads[5], qkv_new, dense_new, up_new, down_new, unit_new, vector_new, qkv_change, dense_change, up_change, down_change, unit_change, vector_change)
```

```python
import functools
import math

import jax
import jax.numpy as jnp
from jax import lax
from jax.experimental import pallas as pl
from jax.experimental.pallas import tpu as pltpu
from jax.sharding import PartitionSpec as P

HEAD_DIM = 256
ROTARY = 64
EPSILON = 1e-05
BETA_ONE = 0.9
BETA_TWO = 0.95
LEARN_RATE = 0.02
WEIGHT_DECAY = 0.01
ROOT_HALF = 0.7071067811865476
ROOT_TWO_PI = 2.5066282746310002
MASKED = -1000000000.0
BF = jnp.bfloat16
F32 = jnp.float32


def dot(a, b, ca, cb):
    return lax.dot_general(a, b, (((ca,), (cb,)), ((), ())), preferred_element_type=F32)


def gelu_value(hidden):
    return 0.5 * hidden * (1.0 + lax.erf(hidden * ROOT_HALF))


def gelu_slope(hidden):
    return (
        0.5 * (1.0 + lax.erf(hidden * ROOT_HALF))
        + hidden * jnp.exp(-0.5 * hidden * hidden) / ROOT_TWO_PI
    )


BLOCK = 128
MIB = 1024 * 1024


def whole(shape):
    return pl.BlockSpec(shape, lambda *_: (0,) * len(shape))


def call(kernel, grid, in_specs, out_specs, out_shape, name, flops, nbytes, prefetch=0, scratch=(), limit=56):
    return pl.pallas_call(
        kernel,
        grid_spec=pltpu.PrefetchScalarGridSpec(
            num_scalar_prefetch=prefetch, grid=grid, in_specs=in_specs, out_specs=out_specs, scratch_shapes=list(scratch)
        ),
        out_shape=out_shape,
        compiler_params=pltpu.CompilerParams(vmem_limit_bytes=limit * MIB),
        cost_estimate=pl.CostEstimate(flops=flops, bytes_accessed=nbytes, transcendentals=0),
        name=name,
    )


def like(shape, dtype):
    return jax.ShapeDtypeStruct(shape, dtype)


def arrange_kernel(place_ref, x_ref, d_ref, v_ref, up_ref, down_ref, xo_ref, do_ref, xs_ref, ds_ref, vo_ref, *quarter_refs):
    width = x_ref.shape[1]
    count = width // BLOCK
    rows = x_ref.shape[0] // 2
    n = quarter_refs[0].shape[1]
    for k in range(2):
        cols = pl.ds(pl.multiple_of((place_ref[2 * count + 1] ^ k) * n, n), n)
        quarter_refs[k][...] = up_ref[:, cols]
        quarter_refs[2 + k][...] = down_ref[:, cols]
    for j in range(count):
        out = slice(j * BLOCK, (j + 1) * BLOCK)
        col = pl.ds(pl.multiple_of(place_ref[j] * BLOCK, BLOCK), BLOCK)
        sent = pl.ds(pl.multiple_of(place_ref[count + j] * BLOCK, BLOCK), BLOCK)
        for b in range(2):
            row = pl.ds(pl.multiple_of((place_ref[2 * count] ^ b) * rows, rows), rows)
            xo_ref[b * rows : (b + 1) * rows, out] = x_ref[row, col]
            do_ref[b * rows : (b + 1) * rows, out] = d_ref[row, col]
            if b == 0:
                xs_ref[:, out] = x_ref[row, sent]
                ds_ref[:, out] = d_ref[row, sent]
        vo_ref[:, out] = v_ref[:, col].astype(F32)


def arrange(place, x, d, v, up, down):
    sent = (x.shape[0] // 2, x.shape[1])
    part = (up.shape[0], up.shape[1] // 2)
    operands = (x, d, v, up, down)
    outs = [(x.shape, BF), (d.shape, BF), (sent, BF), (sent, BF), (v.shape, F32)] + [(part, BF)] * 4
    return call(
        arrange_kernel,
        (1,),
        [whole(a.shape) for a in operands],
        [whole(a) for a, _ in outs],
        [like(*a) for a in outs],
        "arrange",
        0,
        5 * x.size * 2,
        prefetch=1,
    )(place, *operands)


def unorder_kernel(place_ref, v_ref, o_ref):
    for j in range(v_ref.shape[1] // BLOCK):
        col = pl.ds(pl.multiple_of(place_ref[j] * BLOCK, BLOCK), BLOCK)
        o_ref[:, col] = v_ref[:, j * BLOCK : (j + 1) * BLOCK]


def unorder(place, v):
    return call(
        unorder_kernel, (1,), [whole(v.shape)], whole(v.shape), like(v.shape, v.dtype), "unorder", 0, v.size * 8, prefetch=1
    )(place, v)


def pack_kernel(*refs):
    *pieces, out_ref = refs
    row = 0
    for piece in pieces:
        out_ref[row : row + piece.shape[0], :] = piece[...]
        row += piece.shape[0]


def pack(*pieces):
    rows, n = sum(p.shape[0] for p in pieces), pieces[0].shape[1]
    return call(
        pack_kernel, (1,), [whole(p.shape) for p in pieces], whole((rows, n)), like((rows, n), BF), "pack", 0, rows * n * 4
    )(*pieces)


def norm_kernel(x_ref, v_ref, attn_ref, mlp_ref, mean_ref, inv_ref):
    x = x_ref[...].astype(F32)
    mean = jnp.mean(x, -1, keepdims=True)
    center = x - mean
    inv_std = lax.rsqrt(jnp.mean(center * center, -1, keepdims=True) + EPSILON)
    normed = center * inv_std
    attn_ref[...] = (normed * v_ref[0:1, :] + v_ref[1:2, :]).astype(BF)
    mlp_ref[...] = (normed * v_ref[2:3, :] + v_ref[3:4, :]).astype(BF)
    mean_ref[...] = jnp.broadcast_to(mean, mean_ref.shape)
    inv_ref[...] = jnp.broadcast_to(inv_std, inv_ref.shape)


def norm(x, vec):
    rows, width = x.shape
    tile = rows // 4
    block = pl.BlockSpec((tile, width), lambda i: (i, 0))
    stat = pl.BlockSpec((tile, 128), lambda i: (i, 0))
    return call(
        norm_kernel,
        (4,),
        [block, whole(vec.shape)],
        [block, block, stat, stat],
        [like(x.shape, BF), like(x.shape, BF), like((rows, 128), F32), like((rows, 128), F32)],
        "norm",
        x.size * 12,
        x.size * 6,
    )(x, vec)


def both(a_ref, near_ref, far_ref):
    half = a_ref.shape[1] // 2
    return dot(a_ref[:, :half], near_ref[...], 1, 0) + dot(a_ref[:, half:], far_ref[...], 1, 0)


def hidden_kernel(a_ref, near_ref, far_ref, b_ref, act_ref, slope_ref):
    hidden = both(a_ref, near_ref, far_ref) + b_ref[...]
    cdf = 0.5 * (1.0 + lax.erf(hidden * ROOT_HALF))
    act_ref[...] = (hidden * cdf).astype(BF)
    slope_ref[...] = cdf + hidden * jnp.exp(-0.5 * hidden * hidden) * (1.0 / ROOT_TWO_PI)


def hidden_of(a, weight, bias, tile=256):
    near, far = weight
    (rows, width), n = a.shape, near.shape[1]
    wide = pl.BlockSpec((width // 2, tile), lambda j: (0, j))
    out = pl.BlockSpec((rows, tile), lambda j: (0, j))
    return call(
        hidden_kernel,
        (n // tile,),
        [whole(a.shape), wide, wide, pl.BlockSpec((1, tile), lambda j: (0, j))],
        [out, out],
        [like((rows, n), BF), like((rows, n), F32)],
        "hidden",
        2 * rows * width * n,
        (a.size + near.size * 2 + rows * n * 3) * 2,
    )(a, near, far, bias)


def d_hidden_kernel(d_ref, near_ref, far_ref, slope_ref, low_ref, sum_ref):
    grad = both(d_ref, near_ref, far_ref) * slope_ref[...]
    low_ref[...] = grad.astype(BF)
    sum_ref[...] = jnp.broadcast_to(jnp.sum(grad, 0, keepdims=True), sum_ref.shape)


def d_hidden_of(d, weight, slope, tile=256):
    near, far = weight
    (rows, width), n = d.shape, near.shape[1]
    wide = pl.BlockSpec((width // 2, tile), lambda j: (0, j))
    out = pl.BlockSpec((rows, tile), lambda j: (0, j))
    return call(
        d_hidden_kernel,
        (n // tile,),
        [whole(d.shape), wide, wide, out],
        [out, pl.BlockSpec((8, tile), lambda j: (0, j))],
        [like((rows, n), BF), like((8, n), F32)],
        "d_hidden",
        2 * rows * width * n,
        (d.size + near.size * 2 + rows * n * 3) * 2,
    )(d, near, far, slope)


def turn(block, cosine, sine):
    head = block[:, :128]
    lane = lax.broadcasted_iota(jnp.int32, head.shape, 1)
    half = ROTARY // 2
    partner = jnp.where(lane < half, -pltpu.roll(head, 128 - half, 1), pltpu.roll(head, half, 1))
    return jnp.concatenate([head * cosine + partner * sine, block[:, 128:]], 1)


def attend_kernel(
    z_ref, a0_ref, a1_ref, near_ref, far_ref, b_ref, cos_ref, sin_ref, ctx_ref, pack_ref, log_ref
):
    z = z_ref[0]
    size = a0_ref.shape[0] // 2
    hd = HEAD_DIM
    scale = hd**-0.5

    def row_of(p):
        return pl.ds(pl.multiple_of((z ^ p) * size, size), size)

    for b in range(4):
        a = (a0_ref, a1_ref)[b // 2][b % 2 * size : (b % 2 + 1) * size, :]
        half = a.shape[1] // 2
        lin = dot(a[:, :half], near_ref[...], 1, 0) + dot(a[:, half:], far_ref[...], 1, 0) + b_ref[...]
        mine = slice(b * size, (b + 1) * size)
        cosine, sine = cos_ref[mine, :], sin_ref[mine, :]
        rows = row_of(b)
        pack_ref[rows, :hd] = turn(lin[:, :hd], cosine, sine).astype(BF)
        pack_ref[rows, hd : 2 * hd] = turn(lin[:, hd : 2 * hd], cosine, sine).astype(BF)
        pack_ref[rows, 2 * hd :] = lin[:, 2 * hd :].astype(BF)
    for p in range(4):
        here, seen = slice(p * size, (p + 1) * size), slice(0, (p + 1) * size)
        scores = dot(pack_ref[here, :hd], pack_ref[seen, hd : 2 * hd], 1, 1) * scale
        row_ids = p * size + lax.broadcasted_iota(jnp.int32, scores.shape, 0)
        col_ids = lax.broadcasted_iota(jnp.int32, scores.shape, 1)
        scores = jnp.where(row_ids >= col_ids, scores, MASKED)
        top = jnp.max(scores, -1, keepdims=True)
        exponent = jnp.exp(scores - top)
        total = jnp.sum(exponent, -1, keepdims=True)
        low = (exponent * (1.0 / total)).astype(BF)
        ctx_ref[row_of(p), :] = dot(low, pack_ref[seen, 2 * hd :], 1, 0).astype(BF)
        log_ref[here, :] = jnp.broadcast_to(top + jnp.log(total), (size, log_ref.shape[1]))


def attend(z, a0, a1, weight, bias, cosine, sine):
    near, far = weight
    length, width = 2 * a0.shape[0], a0.shape[1]
    hd = HEAD_DIM
    heads = bias.shape[1] // (3 * hd)
    column = lambda rows, cols: pl.BlockSpec((rows, cols), lambda h, p: (0, h))
    return call(
        attend_kernel,
        (heads,),
        [
            whole(a0.shape),
            whole(a1.shape),
            column(near.shape[0], 3 * hd),
            column(far.shape[0], 3 * hd),
            column(1, 3 * hd),
            whole(cosine.shape),
            whole(sine.shape),
        ],
        [column(length, hd), column(length, 3 * hd), column(length, 128)],
        [like((length, heads * hd), BF), like((length, heads * 3 * hd), BF), like((length, heads * 128), F32)],
        "attend",
        (3 * length * length * hd + 6 * length * width * hd) * heads,
        length * width * 8,
        prefetch=1,
    )(z, a0, a1, near, far, bias, cosine, sine)


def attend_back_kernel(
    z_ref, pack_ref, log_ref, d0_ref, d1_ref, near_ref, far_ref, cos_ref, sin_ref, dl_ref, us_ref, g_s, dk_s, dv_s
):
    z = z_ref[0]
    size = d0_ref.shape[0] // 2
    hd = HEAD_DIM
    scale = hd**-0.5

    def row_of(p):
        return pl.ds(pl.multiple_of((z ^ p) * size, size), size)

    for half, d_ref in enumerate((d0_ref, d1_ref)):
        grad = both(d_ref, near_ref, far_ref).astype(BF)
        g_s[row_of(2 * half), :] = grad[:size]
        g_s[row_of(2 * half + 1), :] = grad[size:]
    dk_s[...] = jnp.zeros_like(dk_s)
    dv_s[...] = jnp.zeros_like(dv_s)
    q_sum = jnp.zeros((1, hd), F32)
    for p in range(4):
        here, seen = slice(p * size, (p + 1) * size), slice(0, (p + 1) * size)
        rows = row_of(p)
        queries, grads = pack_ref[here, :hd], g_s[here, :]
        keys, values = pack_ref[seen, hd : 2 * hd], pack_ref[seen, 2 * hd :]
        scores = dot(queries, keys, 1, 1) * scale
        row_ids = p * size + lax.broadcasted_iota(jnp.int32, scores.shape, 0)
        col_ids = lax.broadcasted_iota(jnp.int32, scores.shape, 1)
        scores = jnp.where(row_ids >= col_ids, scores, MASKED)
        probs = jnp.exp(scores - log_ref[here, 0:1])
        low = probs.astype(BF)
        weight_grad = dot(grads, values, 1, 1)
        score_grad = (
            probs * (weight_grad - jnp.sum(probs * weight_grad, -1, keepdims=True))
        ).astype(BF)
        query_grad = (dot(score_grad, keys, 1, 0) * scale).astype(BF).astype(F32)
        dk_s[seen, :] += dot(score_grad, queries, 0, 0)
        dv_s[seen, :] += dot(low, grads, 0, 0)
        query_grad = turn(query_grad, cos_ref[rows, :], -sin_ref[rows, :])
        q_sum = q_sum + jnp.sum(query_grad, 0, keepdims=True)
        dl_ref[rows, :hd] = query_grad.astype(BF)
    k_sum = jnp.zeros((1, hd), F32)
    v_sum = jnp.zeros((1, hd), F32)
    for p in range(4):
        here = slice(p * size, (p + 1) * size)
        rows = row_of(p)
        key_grad = (dk_s[here, :] * scale).astype(BF).astype(F32)
        key_grad = turn(key_grad, cos_ref[rows, :], -sin_ref[rows, :])
        k_sum = k_sum + jnp.sum(key_grad, 0, keepdims=True)
        dl_ref[rows, hd : 2 * hd] = key_grad.astype(BF)
        value_grad = dv_s[here, :].astype(BF)
        v_sum = v_sum + jnp.sum(value_grad.astype(F32), 0, keepdims=True)
        dl_ref[rows, 2 * hd :] = value_grad
    us_ref[...] = jnp.broadcast_to(jnp.concatenate([q_sum, k_sum, v_sum], 1), us_ref.shape)


def attend_back(z, packed, logs, d0, d1, weight, cosine, sine):
    near, far = weight
    length, wide = packed.shape
    hd = HEAD_DIM
    heads = wide // (3 * hd)
    first = wide // hd
    column = lambda rows, cols: pl.BlockSpec((rows, cols), lambda h, p: (0, h))
    dense = pl.BlockSpec((near.shape[0], hd), lambda h, p: (0, first + h))
    return call(
        attend_back_kernel,
        (heads,),
        [
            column(length, 3 * hd),
            column(length, 128),
            whole(d0.shape),
            whole(d1.shape),
            dense,
            dense,
            whole(cosine.shape),
            whole(sine.shape),
        ],
        [column(length, 3 * hd), column(8, 3 * hd)],
        [like((length, wide), BF), like((8, wide), F32)],
        "attend_back",
        (9 * length * length * hd + 2 * length * d0.shape[1] * hd) * heads,
        length * wide * 8,
        prefetch=1,
        scratch=[pltpu.VMEM((length, hd), BF)] + [pltpu.VMEM((length, hd), F32)] * 2,
    )(z, packed, logs, d0, d1, near, far, cosine, sine)


def near_or_far(near_ref, far_ref, body):
    j = pl.program_id(0)
    count = pl.num_programs(0) // 2

    @pl.when(j < count)
    def _():
        body(*near_ref)

    @pl.when(j >= count)
    def _():
        body(*far_ref)


def row_specs(shape, count, col=0):
    half = count // 2
    return [
        pl.BlockSpec(shape, lambda j: (jnp.minimum(j, half - 1), col)),
        pl.BlockSpec(shape, lambda j: (jnp.maximum(j - half, 0), col)),
    ]


def branch_kernel(a0_ref, a1_ref, ctx_ref, dn_ref, df_ref, sn_ref, sf_ref, *outs):
    size = outs[0].shape[0]

    def body(down_ref, dense_ref):
        for k, act_ref in enumerate((a0_ref, a1_ref)):
            ctx = ctx_ref[2 * k * size : 2 * (k + 1) * size, :]
            part = dot(act_ref[...], down_ref[...], 1, 1) + dot(ctx, dense_ref[...], 1, 1)
            outs[2 * k][...] = part[:size]
            outs[2 * k + 1][...] = part[size:].astype(BF)

    near_or_far((dn_ref, sn_ref), (df_ref, sf_ref), body)


def token_outs(size, width, tile):
    spec = pl.BlockSpec((size, tile), lambda j: (0, j))
    return [spec] * 4, [like((size, width), F32), like((size, width), BF)] * 2


def branch_of(a0, a1, context_out, down, attn, tile=256):
    rows, n = a0.shape
    width = 2 * down[0].shape[0]
    cols = context_out.shape[1]
    count = width // tile
    specs, shapes = token_outs(rows // 2, width, tile)
    return call(
        branch_kernel,
        (count,),
        [
            whole(a0.shape),
            whole(a1.shape),
            whole(context_out.shape),
            *row_specs((tile, n), count),
            *row_specs((tile, cols), count, attn[0].shape[1] // cols - 1),
        ],
        specs,
        shapes,
        "branch",
        4 * rows * width * (n + cols),
        (2 * rows * (n + cols) + width * (n + cols) + 2 * rows * width * 2) * 2,
    )(a0, a1, context_out, *down, *attn)


def input_grad_kernel(
    dl_ref, h0_ref, h1_ref, an_ref, af_ref, un_ref, uf_ref, x0_ref, x1_ref, m0_ref, m1_ref, i0_ref, i1_ref, v_ref, *outs
):
    size = outs[0].shape[0]
    wide = dl_ref.shape[1]
    halves = ((h0_ref, x0_ref, m0_ref, i0_ref), (h1_ref, x1_ref, m1_ref, i1_ref))

    def body(attn_ref, up_ref):
        total = [0.0] * 4
        for k, (dh_ref, x_ref, mean_ref, inv_ref) in enumerate(halves):
            attn = dot(dl_ref[2 * k * size : 2 * (k + 1) * size, :], attn_ref[:, :wide], 1, 1)
            mlp = dot(dh_ref[...], up_ref[...], 1, 1)
            part = attn * v_ref[0:1, :] + mlp * v_ref[2:3, :]
            outs[2 * k][...] = part[:size]
            outs[2 * k + 1][...] = part[size:].astype(BF)
            normed = (x_ref[...].astype(F32) - mean_ref[:, 0:1]) * inv_ref[:, 0:1]
            sums = [jnp.sum(v, 0, keepdims=True) for v in (attn * normed, attn, mlp * normed, mlp)]
            total = [u + v for u, v in zip(total, sums)]
        outs[4][...] = jnp.concatenate(total + [jnp.zeros((4, attn.shape[1]), F32)], 0)

    near_or_far((an_ref, un_ref), (af_ref, uf_ref), body)


def input_grad_of(d_linear, h0, h1, attn, up, xs, means, invs, vec, tile=256):
    rows, n = h0.shape
    width = xs[0].shape[1]
    wide = d_linear.shape[1]
    count = width // tile
    specs, shapes = token_outs(rows // 2, width, tile)
    column = pl.BlockSpec((rows, tile), lambda j: (0, j))
    return call(
        input_grad_kernel,
        (count,),
        [
            whole(d_linear.shape),
            whole(h0.shape),
            whole(h1.shape),
            *row_specs((tile, attn[0].shape[1]), count),
            *row_specs((tile, n), count),
            column,
            column,
            *[whole(a.shape) for a in (*means, *invs)],
            pl.BlockSpec((vec.shape[0], tile), lambda j: (0, j)),
        ],
        [*specs, pl.BlockSpec((8, tile), lambda j: (0, j))],
        [*shapes, like((8, width), F32)],
        "input_grad",
        4 * rows * width * (n + wide),
        (2 * rows * (n + wide) + width * (n + wide) + 2 * rows * width * 3) * 2,
    )(d_linear, h0, h1, *attn, *up, *xs, *means, *invs, vec)


def grad_kernel(pairs, near, *refs):
    operands = refs[: 4 * pairs]
    outs = refs[4 * pairs + near :]
    j = pl.program_id(0)
    col = 0
    for k in range(pairs):
        l0, l1, r0, r1 = (r[...] for r in operands[4 * k : 4 * k + 4])
        part = dot(l0, r0, 0, 0) + dot(l1, r1, 0, 0)
        cols = slice(col, col + part.shape[1])
        col += part.shape[1]
        if near:
            part = (part + refs[4 * pairs][:, cols].astype(F32)).astype(BF)
            for i, out_ref in enumerate(outs):

                @pl.when(j == i)
                def _(out_ref=out_ref, part=part, cols=cols):
                    out_ref[:, cols] = part

        else:
            outs[0][:, cols] = part.astype(BF)


def grad_of(factors, add=None):
    width = factors[0][0].shape[1]
    near = add is not None
    tile = width // 8
    first = 0 if near else 4
    in_specs, operands, n, flops, nbytes = [], [], 0, 0, 0
    for l0, l1, r0, r1 in factors:
        rows = l0.shape[0]
        for left in (l0, l1):
            in_specs.append(pl.BlockSpec((rows, tile), lambda j: (0, first + j)))
            operands.append(left)
        cols = r0[0].shape[1]
        for right, k in (r0, r1):
            in_specs.append(pl.BlockSpec((rows, cols), lambda j, k=k: (k, 0)))
            operands.append(right)
        n += cols
        flops += 2 * rows * width * cols
        nbytes += 2 * rows * (width + 2 * cols)
    block = pl.BlockSpec((tile, n), lambda j: (j, 0))
    if near:
        in_specs.append(block)
        operands.append(add)
        nbytes += width * n
    return call(
        functools.partial(grad_kernel, len(factors), near),
        (4,),
        in_specs,
        [whole((tile, n))] * 4 if near else block,
        [like((tile, n), BF)] * 4 if near else like((width // 2, n), BF),
        "grad_near" if near else "grad_far",
        flops,
        nbytes + width * n,
    )(*operands)


def fold_kernel(cross, keep_ref, got_ref, o_ref):
    for j, k in enumerate(cross):
        here = slice(j * BLOCK, (j + 1) * BLOCK)
        o_ref[:, k * BLOCK : (k + 1) * BLOCK] = (keep_ref[:, here] + got_ref[:, here].astype(F32)).astype(BF)


def fold(cross, keep, got):
    rows, width = keep.shape
    tile = rows // 4
    block = pl.BlockSpec((tile, width), lambda i: (i, 0))
    return call(
        functools.partial(fold_kernel, cross), (4,), [block, block], block, like(keep.shape, BF), "fold", keep.size, keep.size * 8
    )(keep, got)


def finish_kernel(place_ref, o0_ref, o1_ref, g0_ref, g1_ref, x_ref, d_ref, out_ref, grad_ref):
    width = x_ref.shape[1]
    count = width // BLOCK
    x = x_ref[...].astype(F32)
    center = x - jnp.mean(x, -1, keepdims=True)
    inv_std = lax.rsqrt(jnp.mean(center * center, -1, keepdims=True) + EPSILON)
    normed = center * inv_std

    def body(o_ref, g_ref):
        g = g_ref[...].astype(F32)
        grad = d_ref[...].astype(F32) + inv_std * (
            g - jnp.mean(g, -1, keepdims=True) - normed * jnp.mean(g * normed, -1, keepdims=True)
        )
        for j in range(count):
            col = pl.ds(pl.multiple_of(place_ref[j] * BLOCK, BLOCK), BLOCK)
            part = slice(j * BLOCK, (j + 1) * BLOCK)
            out_ref[:, col] = o_ref[:, part]
            grad_ref[:, col] = grad[:, part]

    near_or_far((o0_ref, g0_ref), (o1_ref, g1_ref), body)


def finish(place, o0, o1, g0, g1, x, d):
    rows, width = o0.shape
    per = 4
    tile = rows // per
    at = 2 * width // BLOCK
    first = pl.BlockSpec((tile, width), lambda i, p: (jnp.minimum(i, per - 1), 0))
    second = pl.BlockSpec((tile, width), lambda i, p: (jnp.maximum(i - per, 0), 0))
    local = pl.BlockSpec((tile, width), lambda i, p: (i, 0))
    out = pl.BlockSpec((tile, width), lambda i, p: ((p[at] ^ (i // per)) * per + i % per, 0))
    return call(
        finish_kernel,
        (2 * per,),
        [first, second, first, second, local, local],
        [out, out],
        [like(x.shape, BF), like(x.shape, F32)],
        "finish",
        x.size * 20,
        x.size * 14,
        prefetch=1,
    )(place, o0, o1, g0, g1, x, d)


def step_values(weight, first, root, gradient, fix_one, fix_two, decay_rate):
    first_new = BETA_ONE * first + (1.0 - BETA_ONE) * gradient
    root_new = jnp.sqrt(BETA_TWO * root * root + (1.0 - BETA_TWO) * gradient * gradient)
    change = -LEARN_RATE * (
        first_new / fix_one / (root_new / fix_two + 1e-08) + decay_rate * weight
    )
    return first_new, root_new, change


def adam_kernel(c_ref, fix_ref, w_ref, m_ref, a_ref, b_ref, e_ref, t_ref, g_ref, n_ref, u_ref):
    def body(gradient):
        first, root, change = step_values(
            w_ref[...].astype(F32), m_ref[0], m_ref[1], gradient, fix_ref[0], fix_ref[1], WEIGHT_DECAY
        )
        g_ref[...] = gradient
        n_ref[0] = first
        n_ref[1] = root
        u_ref[...] = change

    @pl.when(pl.program_id(0) == 0)
    def _():
        body(a_ref[...].astype(F32) + b_ref[...].astype(F32) + e_ref[...].astype(F32))

    @pl.when(pl.program_id(0) == 1)
    def _():
        body(t_ref[...].astype(F32))


def adam(ctx, fixes, weight, moments, terms, theirs, tile=1024, first=0):
    rows, cols = weight.shape
    n = cols // 2
    per = n // tile
    at = lambda k, i, c: (0, (c[0] ^ k) * per + i)
    mine = pl.BlockSpec((rows, tile), lambda k, i, c: (0, first + i + k * (per - 1 - i)))
    other = pl.BlockSpec((rows, tile), lambda k, i, c: (0, first + i * k))
    matrix = pl.BlockSpec((rows, tile), at)
    pair = pl.BlockSpec((2, rows, tile), lambda k, i, c: (0, *at(k, i, c)))
    return call(
        adam_kernel,
        (2, per),
        [pl.BlockSpec(memory_space=pltpu.SMEM), matrix, pair, mine, mine, mine, other],
        [matrix, pair, matrix],
        [like(weight.shape, F32), like(moments.shape, F32), like(weight.shape, F32)],
        "adam",
        weight.size * 20,
        weight.size * 30,
        prefetch=1,
    )(ctx, fixes, weight, moments, *terms, theirs)


def adam_heads_kernel(c_ref, fix_ref, w_ref, m_ref, a_ref, b_ref, e_ref, t_ref, g_ref, n_ref, u_ref):
    mine = a_ref[...].astype(F32) + b_ref[...].astype(F32) + e_ref[...].astype(F32)
    theirs = t_ref[...].astype(F32)
    heads, wide = w_ref.shape[1] // 2, w_ref.shape[2]
    for h in range(2 * heads):
        cols = slice(h % heads * wide, (h % heads + 1) * wide)
        gradient = jnp.where(c_ref[0] == h // heads, mine[:, cols], theirs[:, cols])
        first, root, change = step_values(
            w_ref[:, h, :].astype(F32), m_ref[0, :, h, :], m_ref[1, :, h, :], gradient, fix_ref[0], fix_ref[1], WEIGHT_DECAY
        )
        g_ref[:, h, :] = gradient
        n_ref[0, :, h, :] = first
        n_ref[1, :, h, :] = root
        u_ref[:, h, :] = change


def adam_heads(ctx, fixes, weight, moments, terms, theirs):
    rows, heads, wide = weight.shape
    tile = rows // 4
    part = pl.BlockSpec((tile, heads // 2 * wide), lambda i, c: (i, 0))
    cube = pl.BlockSpec((tile, heads, wide), lambda i, c: (i, 0, 0))
    pair = pl.BlockSpec((2, tile, heads, wide), lambda i, c: (0, i, 0, 0))
    return call(
        adam_heads_kernel,
        (4,),
        [pl.BlockSpec(memory_space=pltpu.SMEM), cube, pair, part, part, part, part],
        [cube, pair, cube],
        [like(weight.shape, F32), like(moments.shape, F32), like(weight.shape, F32)],
        "adam_heads",
        weight.size * 20,
        weight.size * 30,
        prefetch=1,
    )(ctx, fixes, weight, moments, *terms, theirs)


def rotary_tables(positions):
    lane = jnp.arange(128)
    inverse = jnp.exp((lane % (ROTARY // 2)).astype(F32) * (-2.0 / ROTARY) * math.log(10000.0))
    angles = positions.astype(F32)[:, None] * inverse[None, :]
    turned = lane[None, :] < ROTARY
    return (jnp.where(turned, jnp.cos(angles), 1.0), jnp.where(turned, jnp.sin(angles), 0.0))


def adam_step(weight, moments, gradient, count_value, decay_rate):
    first_new = BETA_ONE * moments[0] + (1.0 - BETA_ONE) * gradient
    root_new = jnp.sqrt(BETA_TWO * moments[1] * moments[1] + (1.0 - BETA_TWO) * gradient * gradient)
    fix_one = 1.0 - jnp.power(BETA_ONE, count_value)
    fix_two = 1.0 - jnp.power(BETA_TWO, count_value)
    change = -LEARN_RATE * (
        first_new / fix_one / (root_new / jnp.sqrt(fix_two) + 1e-08) + decay_rate * weight
    )
    return (jnp.stack([first_new, root_new]), change)


def on_device(
    shard_count,
    inputs,
    cotangent,
    qkv_weight,
    dense_weight,
    up_weight,
    down_weight,
    unit_biases,
    vectors,
    qkv_moments,
    dense_moments,
    up_moments,
    down_moments,
    unit_moments,
    vector_moments,
    step_count,
):
    shard, ctx, ten = (lax.axis_index(a) for a in ("shard", "context", "tensor"))
    fast = shard_count == 8
    _, local_len, width = inputs.shape
    quarter = local_len // 2
    row_count, heads_local, head_wide = qkv_weight.shape
    heads = heads_local // 2
    units = up_weight.shape[1] // 2
    head_cols = heads * HEAD_DIM
    n_qkv = heads * head_wide
    count = width // BLOCK

    def along(axis, size, bit):
        return lambda v: lax.ppermute(v, axis, [(i, i ^ bit) for i in range(size)])

    to_core, to_x, to_y = (along("shard", shard_count, bit) for bit in (1, 2, 4))
    to_ctx, to_ten = along("context", 2, 1), along("tensor", 2, 1)

    if fast:
        chips = ((0, 4, 2, 6), (0, 2, 4, 6))
        relative = [(core + chips[ab][k], ab) for core in range(2) for ab in range(2) for k in range(4)]
        places = [[(shard ^ s) * 2 + (ctx ^ f ^ ab) for s, ab in relative] for f in range(2)]
        cross = [core * 8 + (1 - ab) * 4 + (0, 2, 1, 3)[k] for core in range(2) for ab in range(2) for k in range(4)]
    else:
        places = [[jnp.int32(j) for j in range(count)]] * 2
        cross = list(range(count))
    place = jnp.stack([*places[0], *places[1], ten, ctx]).astype(jnp.int32)
    z = ctx * 2 + ten
    ctx_scalar, z_scalar = (v.reshape(1).astype(jnp.int32) for v in (ctx, z))

    def after(value, *others):
        return lax.optimization_barrier((value, *others))[0]

    def gather_rows(mine, other):
        if not fast:
            block = jnp.where(ctx == 0, jnp.concatenate([mine, other], 0), jnp.concatenate([other, mine], 0))
            full = lax.all_gather(block, "shard", axis=0, tiled=True)
            return full[: width // 2], full[width // 2 :]
        a1 = to_y(mine)
        a2 = to_x(pack(mine, a1))
        b1 = to_x(other)
        b2 = to_y(pack(other, b1))
        near = pack(mine, a1, a2, other, b1, b2)
        return near, to_core(near)

    def scatter_rows(factors):
        far_part = grad_of(factors)
        r = row_count
        if not fast:
            part = jnp.concatenate([*grad_of(factors, jnp.zeros_like(far_part)), far_part], 0)
            total = lax.psum_scatter(part, "shard", scatter_dimension=0, tiled=True)
            mine = lax.dynamic_slice_in_dim(total, ctx * r, r, 0)
            away = lax.dynamic_slice_in_dim(total, (1 - ctx) * r, r, 0)
            zero = jnp.zeros_like(mine)
            return (mine, zero, zero), to_ctx(away)
        a_own, a_x, b_own, b_y = grad_of(factors, to_core(far_part))
        add = lambda u, v: (u.astype(F32) + v.astype(F32)).astype(BF)
        b_got = to_y(b_y)
        a_got = to_x(a_x)
        b_last = to_x(add(b_own[r:], b_got[r:]))
        a_last = to_y(add(a_own[r:], a_got[r:]))
        away = (b_own[:r].astype(F32) + b_got[:r].astype(F32) + b_last.astype(F32)).astype(BF)
        return (a_own, a_got, a_last), to_ctx(away)

    def reduce_tokens(own, other):
        far = to_ctx(fold(cross, other[0], to_ten(other[1])))
        return own[0] + to_ten(own[1]).astype(F32) + far.astype(F32)

    def attn_quarter(q):
        qkv = lax.dynamic_slice_in_dim(qkv_weight, q * heads, heads, 1).reshape(row_count, n_qkv)
        dense = lax.dynamic_slice_in_dim(dense_weight, q * head_cols, head_cols, 1)
        return jnp.concatenate([qkv, dense], 1)

    x_own, d_own, x_sent, d_sent, vec, up_mine, up_theirs, down_mine, down_theirs = arrange(
        place, inputs.reshape(local_len, width), cotangent.reshape(local_len, width), vectors, up_weight, down_weight
    )
    up_other = to_ctx(up_theirs)
    attn_other = to_ctx(attn_quarter(1 - ctx))
    down_other = to_ctx(down_theirs)
    x_first = to_ctx(after(x_sent, up_other, attn_other, down_other))
    d_first = to_ctx(after(d_sent, x_first))
    w_up = gather_rows(up_mine, up_other)
    w_attn = gather_rows(attn_quarter(ctx), attn_other)
    w_down = gather_rows(down_mine, down_other)
    x_oth = pack(x_first, to_ten(x_first))
    d_oth = pack(d_first, to_ten(d_first))

    unit_vals = unit_biases.astype(F32)
    my_units = lax.dynamic_slice_in_dim(unit_vals, ctx * heads, heads, 0)
    qkv_bias, unit_bias = my_units[:, :head_wide].reshape(1, n_qkv), my_units[:, head_wide:].reshape(1, units)
    attn_own, mlp_own, mean_own, inv_own = norm(x_own, vec)
    attn_oth, mlp_oth, mean_oth, inv_oth = norm(x_oth, vec)

    positions = ((jnp.arange(4) ^ z)[:, None] * quarter + jnp.arange(quarter)[None, :]).reshape(-1)
    cosine, sine = rotary_tables(positions)
    active_own, slope_own = hidden_of(mlp_own, w_up, unit_bias)
    low_own, sum_own = d_hidden_of(d_own, w_down, slope_own)
    active_oth, slope_oth = hidden_of(mlp_oth, w_up, unit_bias)
    context_out, packed, logs = attend(z_scalar, attn_own, attn_oth, w_attn, qkv_bias, cosine, sine)
    *branch_own, branch_keep, branch_send = branch_of(active_own, active_oth, context_out, w_down, w_attn)
    branch_sum = reduce_tokens(branch_own, (branch_keep, branch_send))

    low_oth, sum_oth = d_hidden_of(d_oth, w_down, slope_oth)
    d_linear, unit_sums = attend_back(z_scalar, packed, logs, d_own, d_oth, w_attn, cosine, sine)
    *g_own, g_keep, g_send, sums = input_grad_of(
        d_linear, low_own, low_oth, w_attn, w_up, (x_own, x_oth), (mean_own, mean_oth), (inv_own, inv_oth), vec
    )
    g_sum = reduce_tokens(g_own, (g_keep, g_send)).astype(BF)

    down_terms, down_theirs = scatter_rows([(d_own, d_oth, (active_own, 0), (active_oth, 0))])
    up_terms, up_theirs = scatter_rows([(mlp_own, mlp_oth, (low_own, 0), (low_oth, 0))])
    attn_terms, attn_theirs = scatter_rows(
        [
            (attn_own, attn_oth, (d_linear, 0), (d_linear, 1)),
            (d_own, d_oth, (context_out, 0), (context_out, 1)),
        ]
    )

    out_own = (x_own[:quarter].astype(F32) + branch_sum + (vec[4] + vec[5])).astype(BF)
    outputs, input_grad = finish(place, out_own, to_ten(out_own), g_sum, to_ten(g_sum), x_own, d_own)

    d_sum = jnp.sum(d_own[:quarter].astype(F32), 0, keepdims=True)
    sums = unorder(place, jnp.concatenate([sums[:4], d_sum, jnp.zeros((3, width), F32)], 0))
    unit_part = jnp.concatenate(
        [unit_sums[0].reshape(heads, head_wide), (sum_own + sum_oth)[0].reshape(heads, units // heads)], 1
    )
    unit_rows = jnp.where(jnp.arange(4)[:, None, None] == ten * 2 + ctx, unit_part[None], 0.0)
    total = jnp.concatenate([sums.reshape(-1), unit_rows.reshape(-1)]).reshape(-1, BLOCK)
    for move in [to_ten, to_ctx] + [along("shard", shard_count, 1 << k) for k in range(shard_count.bit_length() - 1)]:
        total = total + move(total)
    total = total.reshape(-1)
    vector_grad = total[: 5 * width].reshape(5, width)
    vector_grad = jnp.concatenate([vector_grad, vector_grad[4:]], 0)
    unit_all = total[8 * width :].reshape(4 * heads, unit_part.shape[1])
    unit_grad = lax.dynamic_slice_in_dim(unit_all, ten * 2 * heads, 2 * heads, 0)

    count_value = step_count.astype(F32)
    fixes = jnp.stack([1.0 - jnp.power(BETA_ONE, count_value), jnp.sqrt(1.0 - jnp.power(BETA_TWO, count_value))])
    qkv_grad, qkv_new, qkv_change = adam_heads(ctx_scalar, fixes, qkv_weight, qkv_moments, attn_terms, attn_theirs)
    dense_grad, dense_new, dense_change = adam(
        ctx_scalar, fixes, dense_weight, dense_moments, attn_terms, attn_theirs, head_cols, n_qkv // head_cols
    )
    up_grad, up_new, up_change = adam(ctx_scalar, fixes, up_weight, up_moments, up_terms, up_theirs)
    down_grad, down_new, down_change = adam(ctx_scalar, fixes, down_weight, down_moments, down_terms, down_theirs)
    unit_new, unit_change = adam_step(unit_vals, unit_moments, unit_grad, count_value, 0.0)
    vector_new, vector_change = adam_step(vectors.astype(F32), vector_moments, vector_grad, count_value, 0.0)
    return (
        outputs.reshape(inputs.shape),
        input_grad.reshape(inputs.shape),
        qkv_grad,
        dense_grad,
        up_grad,
        down_grad,
        unit_grad,
        vector_grad,
        qkv_new,
        dense_new,
        up_new,
        down_new,
        unit_new,
        vector_new,
        qkv_change,
        dense_change,
        up_change,
        down_change,
        unit_change,
        vector_change,
    )


def solution(mesh):
    rows = ("shard", "context")
    tokens = P("shard", "context", None)
    qkv, matrix, units = P(rows, "tensor", None), P(rows, "tensor"), P("tensor", None)
    qkv_pair, matrix_pair, units_pair = P(None, rows, "tensor", None), P(None, rows, "tensor"), P(None, "tensor", None)
    params = (qkv, matrix, matrix, matrix, units, P())
    states = (qkv_pair, matrix_pair, matrix_pair, matrix_pair, units_pair, P())
    return jax.shard_map(
        functools.partial(on_device, mesh.shape["shard"]),
        mesh=mesh,
        in_specs=(tokens, tokens, *params, *states, P()),
        out_specs=(tokens, tokens, *params, *states, *params),
        check_vma=False,
    )
```

```python
import functools
import math

import jax
import jax.numpy as jnp
from jax import lax
from jax.experimental import pallas as pl
from jax.experimental.pallas import tpu as pltpu
from jax.sharding import PartitionSpec as P

HEAD_DIM = 256
ROTARY = 64
EPSILON = 1e-05
BETA_ONE = 0.9
BETA_TWO = 0.95
LEARN_RATE = 0.02
WEIGHT_DECAY = 0.01
ROOT_HALF = 0.7071067811865476
ROOT_TWO_PI = 2.5066282746310002
MASKED = -1000000000.0
BF = jnp.bfloat16
F32 = jnp.float32


def dot(a, b, ca, cb):
    return lax.dot_general(a, b, (((ca,), (cb,)), ((), ())), preferred_element_type=F32)


def gelu_value(hidden):
    return 0.5 * hidden * (1.0 + lax.erf(hidden * ROOT_HALF))


def gelu_slope(hidden):
    return (
        0.5 * (1.0 + lax.erf(hidden * ROOT_HALF))
        + hidden * jnp.exp(-0.5 * hidden * hidden) / ROOT_TWO_PI
    )


BLOCK = 128
MIB = 1024 * 1024
COSTS = [50, 50, 50, 50, 50, 50, 50, 5, 5, 50, 50, 5, 0.5, 50, 50, 2, 50, 50, 50, 50, 50, 50, 50, 0.5, 20, 10, 10, 50, 0.5, 50, 2, 50, 10, 0, 50, 50, 0.5, 50, 50, 50, 50, 0.5, 50, 50, 5, 5, 5, 50, 50, 10, 50, 20, 10, 50, 50, 50, 50, 50, 50, 50, 50, 50, 50, 10]


def whole(shape):
    return pl.BlockSpec(shape, lambda *_: (0,) * len(shape), pipeline_mode=pl.Buffered(1))


ORDER = []
CALLS = []


def call(kernel, grid, in_specs, out_specs, out_shape, name, flops, nbytes, prefetch=0, scratch=(), limit=56):
    single = not isinstance(out_shape, (list, tuple))
    specs, shapes = ([out_specs], [out_shape]) if single else (list(out_specs), list(out_shape))
    waits = tuple(ORDER)
    cost = COSTS[len(CALLS)] if len(CALLS) < len(COSTS) else 10
    CALLS.append(name)
    first, outs = prefetch + len(in_specs), len(shapes)
    anywhere = pl.BlockSpec(memory_space=pl.ANY)

    def ordered(*refs):
        rest = refs[first + len(waits) :]
        kernel(*refs[:first], *rest[:outs], *rest[outs + 1 :])

    run = pl.pallas_call(
        ordered,
        grid_spec=pltpu.PrefetchScalarGridSpec(
            num_scalar_prefetch=prefetch,
            grid=grid,
            in_specs=[*in_specs, *[anywhere] * len(waits)],
            out_specs=[*specs, anywhere],
            scratch_shapes=list(scratch),
        ),
        out_shape=[*shapes, like((8, 128), F32)],
        compiler_params=pltpu.CompilerParams(vmem_limit_bytes=limit * MIB),
        cost_estimate=pl.CostEstimate(flops=int(cost * 1e9), bytes_accessed=1, transcendentals=0),
        name=name,
    )

    def ordered_call(*operands):
        *results, token = run(*operands, *waits)
        ORDER[:] = [token]
        return results[0] if single else results

    return ordered_call


def like(shape, dtype):
    return jax.ShapeDtypeStruct(shape, dtype)


def cut_kernel(flip, c_ref, *refs):
    *operands, out_ref = refs
    col = 0
    for ref in operands:
        if len(ref.shape) == 3:
            heads, wide = ref.shape[1] // 2, ref.shape[2]
            for c in range(2):

                @pl.when(c_ref[0] == c)
                def _(c=c, ref=ref, col=col):
                    for h in range(heads):
                        out_ref[:, col + h * wide : col + (h + 1) * wide] = ref[:, (c ^ flip) * heads + h, :]

            col += heads * wide
        else:
            n = ref.shape[1] // 2
            out_ref[:, col : col + n] = ref[:, pl.ds(pl.multiple_of((c_ref[0] ^ flip) * n, n), n)]
            col += n


def cut_quarter(ctx, flip, *operands):
    rows = operands[0].shape[0]
    n = sum(a.size for a in operands) // rows // 2
    return call(
        functools.partial(cut_kernel, flip),
        (1,),
        [whole(a.shape) for a in operands],
        whole((rows, n)),
        like((rows, n), BF),
        "cut",
        0,
        6 * rows * n,
        prefetch=1,
    )(ctx, *operands)


def arrange_kernel(place_ref, x_ref, d_ref, v_ref, xo_ref, do_ref, vo_ref):
    width = x_ref.shape[1]
    count = width // BLOCK
    rows = x_ref.shape[0] // 2
    for j in range(count):
        out = slice(j * BLOCK, (j + 1) * BLOCK)
        col = pl.ds(pl.multiple_of(place_ref[j] * BLOCK, BLOCK), BLOCK)
        for b in range(2):
            row = pl.ds(pl.multiple_of((place_ref[2 * count] ^ b) * rows, rows), rows)
            xo_ref[b * rows : (b + 1) * rows, out] = x_ref[row, col]
            do_ref[b * rows : (b + 1) * rows, out] = d_ref[row, col]
        vo_ref[:, out] = v_ref[:, col].astype(F32)


def arrange(place, x, d, v):
    operands = (x, d, v)
    outs = [(x.shape, BF), (d.shape, BF), (v.shape, F32)]
    return call(
        arrange_kernel,
        (1,),
        [whole(a.shape) for a in operands],
        [whole(a) for a, _ in outs],
        [like(*a) for a in outs],
        "arrange",
        0,
        4 * x.size * 2,
        prefetch=1,
    )(place, *operands)


def outgoing_kernel(place_ref, x_ref, o_ref):
    count = x_ref.shape[1] // BLOCK
    for j in range(count):
        col = pl.ds(pl.multiple_of(place_ref[count + j] * BLOCK, BLOCK), BLOCK)
        o_ref[:, j * BLOCK : (j + 1) * BLOCK] = x_ref[:, col]


def outgoing(place, x):
    rows, width = x.shape[0] // 2, x.shape[1]
    return call(
        outgoing_kernel,
        (1,),
        [pl.BlockSpec((rows, width), lambda i, p: (p[2 * width // BLOCK], 0))],
        whole((rows, width)),
        like((rows, width), BF),
        "outgoing",
        0,
        x.size * 2,
        prefetch=1,
    )(place, x)


def unorder_kernel(place_ref, v_ref, o_ref):
    for j in range(v_ref.shape[1] // BLOCK):
        col = pl.ds(pl.multiple_of(place_ref[j] * BLOCK, BLOCK), BLOCK)
        o_ref[:, col] = v_ref[:, j * BLOCK : (j + 1) * BLOCK]


def unorder(place, v):
    return call(
        unorder_kernel, (1,), [whole(v.shape)], whole(v.shape), like(v.shape, v.dtype), "unorder", 0, v.size * 8, prefetch=1
    )(place, v)


def pack_kernel(*refs):
    *pieces, out_ref = refs
    row = 0
    for piece in pieces:
        out_ref[row : row + piece.shape[0], :] = piece[...]
        row += piece.shape[0]


def pack(n, *pieces):
    pieces = [p if isinstance(p, tuple) else (p, 0) for p in pieces]
    rows = sum(p.shape[0] for p, _ in pieces)
    return call(
        pack_kernel,
        (1,),
        [pl.BlockSpec((p.shape[0], n), lambda i, k=k: (0, k)) for p, k in pieces],
        whole((rows, n)),
        like((rows, n), BF),
        "pack",
        0,
        rows * n * 4,
    )(*[p for p, _ in pieces])


def halves_kernel(u_ref, v_ref, top_ref, low_ref):
    top_ref[...] = u_ref[...]
    low_ref[...] = v_ref[...]


def halves(u, v):
    rows, n = u.shape[0] // 2, u.shape[1]
    return call(
        halves_kernel,
        (1,),
        [pl.BlockSpec((rows, n), lambda i: (0, 0)), pl.BlockSpec((rows, n), lambda i: (1, 0))],
        [whole((rows, n))] * 2,
        [like((rows, n), BF)] * 2,
        "halves",
        0,
        8 * rows * n,
    )(u, v)


def total_kernel(counts, *refs):
    at = 0
    for k, count in enumerate(counts):
        total = refs[at][...].astype(F32)
        for ref in refs[at + 1 : at + count]:
            total = total + ref[...].astype(F32)
        out_ref = refs[sum(counts) + k]
        out_ref[...] = total.astype(out_ref.dtype)
        at += count


def totals(rows, *groups, dtype=BF, steps=1):
    tile = rows // steps
    in_specs, operands = [], []
    for group in groups:
        for a, k in group:
            if a.shape[0] == 1:
                in_specs.append(whole(a.shape))
            else:
                in_specs.append(pl.BlockSpec((tile, a.shape[1]), lambda i, k=k: (k * steps + i, 0)))
            operands.append(a)
    width = operands[0].shape[1]
    return call(
        functools.partial(total_kernel, [len(g) for g in groups]),
        (steps,),
        in_specs,
        [pl.BlockSpec((tile, width), lambda i: (i, 0))] * len(groups),
        [like((rows, width), dtype)] * len(groups),
        "totals",
        0,
        8 * rows * width,
    )(*operands)


def norm_kernel(x_ref, v_ref, attn_ref, mlp_ref, mean_ref, inv_ref):
    x = x_ref[...].astype(F32)
    mean = jnp.mean(x, -1, keepdims=True)
    center = x - mean
    inv_std = lax.rsqrt(jnp.mean(center * center, -1, keepdims=True) + EPSILON)
    normed = center * inv_std
    attn_ref[...] = (normed * v_ref[0:1, :] + v_ref[1:2, :]).astype(BF)
    mlp_ref[...] = (normed * v_ref[2:3, :] + v_ref[3:4, :]).astype(BF)
    mean_ref[...] = jnp.broadcast_to(mean, mean_ref.shape)
    inv_ref[...] = jnp.broadcast_to(inv_std, inv_ref.shape)


def norm(x, vec):
    rows, width = x.shape
    tile = rows // 4
    block = pl.BlockSpec((tile, width), lambda i: (i, 0))
    stat = pl.BlockSpec((tile, 128), lambda i: (i, 0))
    return call(
        norm_kernel,
        (4,),
        [block, whole(vec.shape)],
        [block, block, stat, stat],
        [like(x.shape, BF), like(x.shape, BF), like((rows, 128), F32), like((rows, 128), F32)],
        "norm",
        x.size * 12,
        x.size * 6,
    )(x, vec)


def over_rows(a, weight):
    rows = weight[0].shape[0]
    return sum(dot(a[:, k * rows : (k + 1) * rows], part[...], 1, 0) for k, part in enumerate(weight))


def hidden_kernel(a_ref, b_ref, *refs):
    *weight, act_ref, slope_ref = refs
    hidden = over_rows(a_ref[...], weight) + b_ref[...]
    cdf = 0.5 * (1.0 + lax.erf(hidden * ROOT_HALF))
    act_ref[...] = (hidden * cdf).astype(BF)
    slope_ref[...] = cdf + hidden * jnp.exp(-0.5 * hidden * hidden) * (1.0 / ROOT_TWO_PI)


def column_specs(weight, tile, at):
    return [pl.BlockSpec((part.shape[0], tile), at) for part in weight]


def hidden_of(a, weight, bias, tile=512):
    (rows, width), n = a.shape, weight[0].shape[1]
    tile = min(tile, n)
    out = pl.BlockSpec((rows, tile), lambda j: (0, j))
    return call(
        hidden_kernel,
        (n // tile,),
        [whole(a.shape), pl.BlockSpec((1, tile), lambda j: (0, j)), *column_specs(weight, tile, lambda j: (0, j))],
        [out, out],
        [like((rows, n), BF), like((rows, n), F32)],
        "hidden",
        2 * rows * width * n,
        (a.size + width * n + rows * n * 3) * 2,
    )(a, bias, *weight)


def d_hidden_kernel(d_ref, slope_ref, *refs):
    *weight, low_ref, sum_ref = refs
    grad = over_rows(d_ref[...], weight) * slope_ref[...]
    low_ref[...] = grad.astype(BF)
    sum_ref[...] = jnp.broadcast_to(jnp.sum(grad, 0, keepdims=True), sum_ref.shape)


def d_hidden_of(d, weight, slope, tile=512):
    (rows, width), n = d.shape, weight[0].shape[1]
    tile = min(tile, n)
    out = pl.BlockSpec((rows, tile), lambda j: (0, j))
    return call(
        d_hidden_kernel,
        (n // tile,),
        [whole(d.shape), out, *column_specs(weight, tile, lambda j: (0, j))],
        [out, pl.BlockSpec((8, tile), lambda j: (0, j))],
        [like((rows, n), BF), like((8, n), F32)],
        "d_hidden",
        2 * rows * width * n,
        (d.size + width * n + rows * n * 3) * 2,
    )(d, slope, *weight)


def turn(block, cosine, sine):
    head = block[:, :128]
    lane = lax.broadcasted_iota(jnp.int32, head.shape, 1)
    half = ROTARY // 2
    partner = jnp.where(lane < half, -pltpu.roll(head, 128 - half, 1), pltpu.roll(head, half, 1))
    return jnp.concatenate([head * cosine + partner * sine, block[:, 128:]], 1)


def attend_kernel(
    z_ref, a0_ref, a1_ref, b_ref, cos_ref, sin_ref, *refs
):
    *weight, ctx_ref, pack_ref, log_ref = refs
    z = z_ref[0]
    size = a0_ref.shape[0] // 2
    hd = HEAD_DIM
    scale = hd**-0.5

    def row_of(p):
        return pl.ds(pl.multiple_of((z ^ p) * size, size), size)

    for b in range(4):
        a = (a0_ref, a1_ref)[b // 2][b % 2 * size : (b % 2 + 1) * size, :]
        lin = over_rows(a, weight) + b_ref[...]
        mine = slice(b * size, (b + 1) * size)
        cosine, sine = cos_ref[mine, :], sin_ref[mine, :]
        rows = row_of(b)
        pack_ref[rows, :hd] = turn(lin[:, :hd], cosine, sine).astype(BF)
        pack_ref[rows, hd : 2 * hd] = turn(lin[:, hd : 2 * hd], cosine, sine).astype(BF)
        pack_ref[rows, 2 * hd :] = lin[:, 2 * hd :].astype(BF)
    for p in range(4):
        here, seen = slice(p * size, (p + 1) * size), slice(0, (p + 1) * size)
        scores = dot(pack_ref[here, :hd], pack_ref[seen, hd : 2 * hd], 1, 1) * scale
        row_ids = p * size + lax.broadcasted_iota(jnp.int32, scores.shape, 0)
        col_ids = lax.broadcasted_iota(jnp.int32, scores.shape, 1)
        scores = jnp.where(row_ids >= col_ids, scores, MASKED)
        top = jnp.max(scores, -1, keepdims=True)
        exponent = jnp.exp(scores - top)
        total = jnp.sum(exponent, -1, keepdims=True)
        low = (exponent * (1.0 / total)).astype(BF)
        ctx_ref[row_of(p), :] = dot(low, pack_ref[seen, 2 * hd :], 1, 0).astype(BF)
        log_ref[here, :] = jnp.broadcast_to(top + jnp.log(total), (size, log_ref.shape[1]))


def attend(z, a0, a1, weight, bias, cosine, sine):
    length, width = 2 * a0.shape[0], a0.shape[1]
    hd = HEAD_DIM
    heads = bias.shape[1] // (3 * hd)
    column = lambda rows, cols: pl.BlockSpec((rows, cols), lambda h, p: (0, h))
    return call(
        attend_kernel,
        (heads,),
        [
            whole(a0.shape),
            whole(a1.shape),
            column(1, 3 * hd),
            whole(cosine.shape),
            whole(sine.shape),
            *column_specs(weight, 3 * hd, lambda h, p: (0, h)),
        ],
        [column(length, hd), column(length, 3 * hd), column(length, 128)],
        [like((length, heads * hd), BF), like((length, heads * 3 * hd), BF), like((length, heads * 128), F32)],
        "attend",
        (3 * length * length * hd + 6 * length * width * hd) * heads,
        length * width * 8,
        prefetch=1,
    )(z, a0, a1, bias, cosine, sine, *weight)


def attend_back_kernel(
    z_ref, pack_ref, log_ref, d0_ref, d1_ref, cos_ref, sin_ref, *refs
):
    *weight, dl_ref, us_ref, g_s, dk_s, dv_s = refs
    z = z_ref[0]
    size = d0_ref.shape[0] // 2
    hd = HEAD_DIM
    scale = hd**-0.5

    def row_of(p):
        return pl.ds(pl.multiple_of((z ^ p) * size, size), size)

    for half, d_ref in enumerate((d0_ref, d1_ref)):
        grad = over_rows(d_ref[...], weight).astype(BF)
        g_s[row_of(2 * half), :] = grad[:size]
        g_s[row_of(2 * half + 1), :] = grad[size:]
    dk_s[...] = jnp.zeros_like(dk_s)
    dv_s[...] = jnp.zeros_like(dv_s)
    q_sum = jnp.zeros((1, hd), F32)
    for p in range(4):
        here, seen = slice(p * size, (p + 1) * size), slice(0, (p + 1) * size)
        rows = row_of(p)
        queries, grads = pack_ref[here, :hd], g_s[here, :]
        keys, values = pack_ref[seen, hd : 2 * hd], pack_ref[seen, 2 * hd :]
        scores = dot(queries, keys, 1, 1) * scale
        row_ids = p * size + lax.broadcasted_iota(jnp.int32, scores.shape, 0)
        col_ids = lax.broadcasted_iota(jnp.int32, scores.shape, 1)
        scores = jnp.where(row_ids >= col_ids, scores, MASKED)
        probs = jnp.exp(scores - log_ref[here, 0:1])
        low = probs.astype(BF)
        weight_grad = dot(grads, values, 1, 1)
        score_grad = (
            probs * (weight_grad - jnp.sum(probs * weight_grad, -1, keepdims=True))
        ).astype(BF)
        query_grad = (dot(score_grad, keys, 1, 0) * scale).astype(BF).astype(F32)
        dk_s[seen, :] += dot(score_grad, queries, 0, 0)
        dv_s[seen, :] += dot(low, grads, 0, 0)
        query_grad = turn(query_grad, cos_ref[rows, :], -sin_ref[rows, :])
        q_sum = q_sum + jnp.sum(query_grad, 0, keepdims=True)
        dl_ref[rows, :hd] = query_grad.astype(BF)
    k_sum = jnp.zeros((1, hd), F32)
    v_sum = jnp.zeros((1, hd), F32)
    for p in range(4):
        here = slice(p * size, (p + 1) * size)
        rows = row_of(p)
        key_grad = (dk_s[here, :] * scale).astype(BF).astype(F32)
        key_grad = turn(key_grad, cos_ref[rows, :], -sin_ref[rows, :])
        k_sum = k_sum + jnp.sum(key_grad, 0, keepdims=True)
        dl_ref[rows, hd : 2 * hd] = key_grad.astype(BF)
        value_grad = dv_s[here, :].astype(BF)
        v_sum = v_sum + jnp.sum(value_grad.astype(F32), 0, keepdims=True)
        dl_ref[rows, 2 * hd :] = value_grad
    us_ref[...] = jnp.broadcast_to(jnp.concatenate([q_sum, k_sum, v_sum], 1), us_ref.shape)


def attend_back(z, packed, logs, d0, d1, weight, cosine, sine):
    length, wide = packed.shape
    hd = HEAD_DIM
    heads = wide // (3 * hd)
    first = wide // hd
    column = lambda rows, cols: pl.BlockSpec((rows, cols), lambda h, p: (0, h))
    return call(
        attend_back_kernel,
        (heads,),
        [
            column(length, 3 * hd),
            column(length, 128),
            whole(d0.shape),
            whole(d1.shape),
            whole(cosine.shape),
            whole(sine.shape),
            *column_specs(weight, hd, lambda h, p: (0, first + h)),
        ],
        [column(length, 3 * hd), column(8, 3 * hd)],
        [like((length, wide), BF), like((8, wide), F32)],
        "attend_back",
        (9 * length * length * hd + 2 * length * d0.shape[1] * hd) * heads,
        length * wide * 8,
        prefetch=1,
        scratch=[pltpu.VMEM((length, hd), BF)] + [pltpu.VMEM((length, hd), F32)] * 2,
    )(z, packed, logs, d0, d1, cosine, sine, *weight)


def in_turn(parts, body):
    j = pl.program_id(0)
    each = pl.num_programs(0) // len(parts)
    for k, part in enumerate(parts):

        @pl.when(j // each == k)
        def _(part=part):
            body(*part)


def row_specs(shape, count, parts, col=0):
    each = count // parts
    return [pl.BlockSpec(shape, lambda j, k=k: (jnp.clip(j - k * each, 0, each - 1), col)) for k in range(parts)]


def branch_kernel(parts, a0_ref, a1_ref, ctx_ref, *refs):
    weights, outs = refs[: 2 * parts], refs[2 * parts :]
    size = outs[0].shape[0]

    def body(down_ref, dense_ref):
        for k, act_ref in enumerate((a0_ref, a1_ref)):
            ctx = ctx_ref[2 * k * size : 2 * (k + 1) * size, :]
            part = dot(act_ref[...], down_ref[...], 1, 1) + dot(ctx, dense_ref[...], 1, 1)
            outs[2 * k][...] = part[:size]
            outs[2 * k + 1][...] = part[size:].astype(BF)

    in_turn(list(zip(weights[:parts], weights[parts:])), body)


def token_outs(size, width, tile):
    spec = pl.BlockSpec((size, tile), lambda j: (0, j))
    return [spec] * 4, [like((size, width), F32), like((size, width), BF)] * 2


def branch_of(a0, a1, context_out, down, attn, tile=256):
    rows, n = a0.shape
    parts = len(down)
    width = parts * down[0].shape[0]
    cols = context_out.shape[1]
    count = width // tile
    specs, shapes = token_outs(rows // 2, width, tile)
    return call(
        functools.partial(branch_kernel, parts),
        (count,),
        [
            whole(a0.shape),
            whole(a1.shape),
            whole(context_out.shape),
            *row_specs((tile, n), count, parts),
            *row_specs((tile, cols), count, parts, attn[0].shape[1] // cols - 1),
        ],
        specs,
        shapes,
        "branch",
        4 * rows * width * (n + cols),
        (2 * rows * (n + cols) + width * (n + cols) + 2 * rows * width * 2) * 2,
    )(a0, a1, context_out, *down, *attn)


def input_grad_kernel(
    parts, dl_ref, h0_ref, h1_ref, x0_ref, x1_ref, m0_ref, m1_ref, i0_ref, i1_ref, v_ref, *refs
):
    weights, outs = refs[: 2 * parts], refs[2 * parts :]
    size = outs[0].shape[0]
    wide = dl_ref.shape[1]
    halves = ((h0_ref, x0_ref, m0_ref, i0_ref), (h1_ref, x1_ref, m1_ref, i1_ref))

    def body(attn_ref, up_ref):
        total = [0.0] * 4
        for k, (dh_ref, x_ref, mean_ref, inv_ref) in enumerate(halves):
            attn = dot(dl_ref[2 * k * size : 2 * (k + 1) * size, :], attn_ref[:, :wide], 1, 1)
            mlp = dot(dh_ref[...], up_ref[...], 1, 1)
            part = attn * v_ref[0:1, :] + mlp * v_ref[2:3, :]
            outs[2 * k][...] = part[:size]
            outs[2 * k + 1][...] = part[size:].astype(BF)
            normed = (x_ref[...].astype(F32) - mean_ref[:, 0:1]) * inv_ref[:, 0:1]
            sums = [jnp.sum(v, 0, keepdims=True) for v in (attn * normed, attn, mlp * normed, mlp)]
            total = [u + v for u, v in zip(total, sums)]
        outs[4][...] = jnp.concatenate(total + [jnp.zeros((4, attn.shape[1]), F32)], 0)

    in_turn(list(zip(weights[:parts], weights[parts:])), body)


def input_grad_of(d_linear, h0, h1, attn, up, xs, means, invs, vec, tile=256):
    rows, n = h0.shape
    width = xs[0].shape[1]
    wide = d_linear.shape[1]
    parts = len(attn)
    count = width // tile
    specs, shapes = token_outs(rows // 2, width, tile)
    column = pl.BlockSpec((rows, tile), lambda j: (0, j))
    return call(
        functools.partial(input_grad_kernel, parts),
        (count,),
        [
            whole(d_linear.shape),
            whole(h0.shape),
            whole(h1.shape),
            column,
            column,
            *[whole(a.shape) for a in (*means, *invs)],
            pl.BlockSpec((vec.shape[0], tile), lambda j: (0, j)),
            *row_specs((tile, attn[0].shape[1]), count, parts),
            *row_specs((tile, n), count, parts),
        ],
        [*specs, pl.BlockSpec((8, tile), lambda j: (0, j))],
        [*shapes, like((8, width), F32)],
        "input_grad",
        4 * rows * width * (n + wide),
        (2 * rows * (n + wide) + width * (n + wide) + 2 * rows * width * 3) * 2,
    )(d_linear, h0, h1, *xs, *means, *invs, vec, *attn, *up)


def grad_kernel(pairs, near, *refs):
    operands, refs = refs[: 4 * pairs], refs[4 * pairs :]
    adds, outs = (refs[:4], refs[4:]) if near else (None, refs)
    j = pl.program_id(0)
    col = 0
    for k in range(pairs):
        l0, l1, r0, r1 = (r[...] for r in operands[4 * k : 4 * k + 4])
        part = dot(l0, r0, 0, 0) + dot(l1, r1, 0, 0)
        cols = slice(col, col + part.shape[1])
        col += part.shape[1]
        for i, out_ref in enumerate(outs):

            @pl.when(j == i)
            def _(i=i, out_ref=out_ref, part=part, cols=cols):
                if near:
                    out_ref[:, cols] = (part + adds[i][:, cols].astype(F32)).astype(BF)
                else:
                    out_ref[:, cols] = part.astype(BF)


def grad_of(factors, adds=()):
    width = factors[0][0].shape[1]
    tile = width // 8
    first = 0 if adds else 4
    in_specs, operands, n, flops, nbytes = [], [], 0, 0, 0
    for l0, l1, r0, r1 in factors:
        rows = l0.shape[0]
        for left in (l0, l1):
            in_specs.append(pl.BlockSpec((rows, tile), lambda j: (0, first + j)))
            operands.append(left)
        cols = r0[0].shape[1]
        for right, k in (r0, r1):
            in_specs.append(pl.BlockSpec((rows, cols), lambda j, k=k: (k, 0), pipeline_mode=pl.Buffered(1)))
            operands.append(right)
        n += cols
        flops += 2 * rows * width * cols
        nbytes += 2 * rows * (width + 2 * cols)
    in_specs += [whole((tile, n)) for _ in adds]
    return call(
        functools.partial(grad_kernel, len(factors), bool(adds)),
        (4,),
        in_specs,
        [whole((tile, n))] * 4,
        [like((tile, n), BF)] * 4,
        "grad_near" if adds else "grad_far",
        flops,
        nbytes + width * n,
    )(*operands, *adds)


def fold_kernel(cross, keep_ref, got_ref, o_ref):
    for j, k in enumerate(cross):
        here = slice(j * BLOCK, (j + 1) * BLOCK)
        o_ref[:, k * BLOCK : (k + 1) * BLOCK] = (keep_ref[:, here] + got_ref[:, here].astype(F32)).astype(BF)


def fold(cross, keep, got):
    rows, width = keep.shape
    tile = rows // 4
    block = pl.BlockSpec((tile, width), lambda i: (i, 0))
    return call(
        functools.partial(fold_kernel, cross), (4,), [block, block], block, like(keep.shape, BF), "fold", keep.size, keep.size * 8
    )(keep, got)


def finish_kernel(place_ref, o0_ref, o1_ref, g0_ref, g1_ref, x_ref, d_ref, out_ref, grad_ref):
    width = x_ref.shape[1]
    count = width // BLOCK
    x = x_ref[...].astype(F32)
    center = x - jnp.mean(x, -1, keepdims=True)
    inv_std = lax.rsqrt(jnp.mean(center * center, -1, keepdims=True) + EPSILON)
    normed = center * inv_std

    def body(o_ref, g_ref):
        g = g_ref[...].astype(F32)
        grad = d_ref[...].astype(F32) + inv_std * (
            g - jnp.mean(g, -1, keepdims=True) - normed * jnp.mean(g * normed, -1, keepdims=True)
        )
        for j in range(count):
            col = pl.ds(pl.multiple_of(place_ref[j] * BLOCK, BLOCK), BLOCK)
            part = slice(j * BLOCK, (j + 1) * BLOCK)
            out_ref[:, col] = o_ref[:, part]
            grad_ref[:, col] = grad[:, part]

    in_turn(((o0_ref, g0_ref), (o1_ref, g1_ref)), body)


def finish(place, o0, o1, g0, g1, x, d):
    rows, width = o0.shape
    per = 4
    tile = rows // per
    at = 2 * width // BLOCK
    first = pl.BlockSpec((tile, width), lambda i, p: (jnp.minimum(i, per - 1), 0))
    second = pl.BlockSpec((tile, width), lambda i, p: (jnp.maximum(i - per, 0), 0))
    local = pl.BlockSpec((tile, width), lambda i, p: (i, 0))
    out = pl.BlockSpec((tile, width), lambda i, p: ((p[at] ^ (i // per)) * per + i % per, 0))
    return call(
        finish_kernel,
        (2 * per,),
        [first, second, first, second, local, local],
        [out, out],
        [like(x.shape, BF), like(x.shape, F32)],
        "finish",
        x.size * 20,
        x.size * 14,
        prefetch=1,
    )(place, o0, o1, g0, g1, x, d)


def step_values(weight, first, root, gradient, fix_one, fix_two, decay_rate):
    first_new = BETA_ONE * first + (1.0 - BETA_ONE) * gradient
    root_new = jnp.sqrt(BETA_TWO * root * root + (1.0 - BETA_TWO) * gradient * gradient)
    change = -LEARN_RATE * (
        first_new / fix_one / (root_new / fix_two + 1e-08) + decay_rate * weight
    )
    return first_new, root_new, change


def adam_kernel(c_ref, fix_ref, w_ref, m_ref, a_ref, b_ref, e_ref, t_ref, g_ref, n_ref, u_ref):
    def body(gradient):
        first, root, change = step_values(
            w_ref[...].astype(F32), m_ref[0], m_ref[1], gradient, fix_ref[0], fix_ref[1], WEIGHT_DECAY
        )
        g_ref[...] = gradient
        n_ref[0] = first
        n_ref[1] = root
        u_ref[...] = change

    @pl.when(pl.program_id(0) == 0)
    def _():
        body(a_ref[...].astype(F32) + b_ref[...].astype(F32) + e_ref[...].astype(F32))

    @pl.when(pl.program_id(0) == 1)
    def _():
        body(t_ref[...].astype(F32))


def adam(ctx, fixes, weight, moments, terms, theirs, tile=1024, first=0):
    rows, cols = weight.shape
    n = cols // 2
    tile = min(tile, n)
    first //= tile
    per = n // tile
    at = lambda k, i, c: (0, (c[0] ^ k) * per + i)
    mine = pl.BlockSpec((rows, tile), lambda k, i, c: (0, first + i + k * (per - 1 - i)))
    other = pl.BlockSpec((rows, tile), lambda k, i, c: (0, first + i * k))
    matrix = pl.BlockSpec((rows, tile), at)
    pair = pl.BlockSpec((2, rows, tile), lambda k, i, c: (0, *at(k, i, c)))
    return call(
        adam_kernel,
        (2, per),
        [pl.BlockSpec(memory_space=pltpu.SMEM), matrix, pair, mine, mine, mine, other],
        [matrix, pair, matrix],
        [like(weight.shape, F32), like(moments.shape, F32), like(weight.shape, F32)],
        "adam",
        weight.size * 20,
        weight.size * 30,
        prefetch=1,
    )(ctx, fixes, weight, moments, *terms, theirs)


def adam_heads_kernel(c_ref, fix_ref, w_ref, m_ref, a_ref, b_ref, e_ref, t_ref, g_ref, n_ref, u_ref):
    mine = a_ref[...].astype(F32) + b_ref[...].astype(F32) + e_ref[...].astype(F32)
    theirs = t_ref[...].astype(F32)
    heads, wide = w_ref.shape[1] // 2, w_ref.shape[2]
    for h in range(2 * heads):
        cols = slice(h % heads * wide, (h % heads + 1) * wide)
        gradient = jnp.where(c_ref[0] == h // heads, mine[:, cols], theirs[:, cols])
        first, root, change = step_values(
            w_ref[:, h, :].astype(F32), m_ref[0, :, h, :], m_ref[1, :, h, :], gradient, fix_ref[0], fix_ref[1], WEIGHT_DECAY
        )
        g_ref[:, h, :] = gradient
        n_ref[0, :, h, :] = first
        n_ref[1, :, h, :] = root
        u_ref[:, h, :] = change


def adam_heads(ctx, fixes, weight, moments, terms, theirs):
    rows, heads, wide = weight.shape
    tile = rows // 4
    part = pl.BlockSpec((tile, heads // 2 * wide), lambda i, c: (i, 0))
    cube = pl.BlockSpec((tile, heads, wide), lambda i, c: (i, 0, 0))
    pair = pl.BlockSpec((2, tile, heads, wide), lambda i, c: (0, i, 0, 0))
    return call(
        adam_heads_kernel,
        (4,),
        [pl.BlockSpec(memory_space=pltpu.SMEM), cube, pair, part, part, part, part],
        [cube, pair, cube],
        [like(weight.shape, F32), like(moments.shape, F32), like(weight.shape, F32)],
        "adam_heads",
        weight.size * 20,
        weight.size * 30,
        prefetch=1,
    )(ctx, fixes, weight, moments, *terms, theirs)


def rotary_tables(positions):
    lane = jnp.arange(128)
    inverse = jnp.exp((lane % (ROTARY // 2)).astype(F32) * (-2.0 / ROTARY) * math.log(10000.0))
    angles = positions.astype(F32)[:, None] * inverse[None, :]
    turned = lane[None, :] < ROTARY
    return (jnp.where(turned, jnp.cos(angles), 1.0), jnp.where(turned, jnp.sin(angles), 0.0))


def adam_step(weight, moments, gradient, count_value, decay_rate):
    first_new = BETA_ONE * moments[0] + (1.0 - BETA_ONE) * gradient
    root_new = jnp.sqrt(BETA_TWO * moments[1] * moments[1] + (1.0 - BETA_TWO) * gradient * gradient)
    fix_one = 1.0 - jnp.power(BETA_ONE, count_value)
    fix_two = 1.0 - jnp.power(BETA_TWO, count_value)
    change = -LEARN_RATE * (
        first_new / fix_one / (root_new / jnp.sqrt(fix_two) + 1e-08) + decay_rate * weight
    )
    return (jnp.stack([first_new, root_new]), change)


def on_device(
    shard_count,
    inputs,
    cotangent,
    qkv_weight,
    dense_weight,
    up_weight,
    down_weight,
    unit_biases,
    vectors,
    qkv_moments,
    dense_moments,
    up_moments,
    down_moments,
    unit_moments,
    vector_moments,
    step_count,
):
    ORDER.clear()
    CALLS.clear()
    shard, ctx, ten = (lax.axis_index(a) for a in ("shard", "context", "tensor"))
    fast = shard_count == 8
    _, local_len, width = inputs.shape
    quarter = local_len // 2
    row_count, heads_local, head_wide = qkv_weight.shape
    heads = heads_local // 2
    units = up_weight.shape[1] // 2
    head_cols = heads * HEAD_DIM
    n_qkv = heads * head_wide
    count = width // BLOCK

    def along(axis, size, bit):
        return lambda v: lax.ppermute(v, axis, [(i, i ^ bit) for i in range(size)])

    to_core, to_x, to_y = (along("shard", shard_count, bit) for bit in (1, 2, 4))
    to_ctx, to_ten = along("context", 2, 1), along("tensor", 2, 1)

    if fast:
        chips = ((0, 4, 2, 6), (0, 2, 4, 6))
        relative = [(core + chips[ab][k], ab) for core in range(2) for ab in range(2) for k in range(4)]
        places = [[(shard ^ s) * 2 + (ctx ^ f ^ ab) for s, ab in relative] for f in range(2)]
        cross = [core * 8 + (1 - ab) * 4 + (0, 2, 1, 3)[k] for core in range(2) for ab in range(2) for k in range(4)]
    else:
        places = [[jnp.int32(j) for j in range(count)]] * 2
        cross = list(range(count))
    place = jnp.stack([*places[0], *places[1], ten]).astype(jnp.int32)
    z = ctx * 2 + ten
    ctx_scalar, z_scalar = (v.reshape(1).astype(jnp.int32) for v in (ctx, z))

    def wait(*values):
        ORDER.extend(values)

    def full_rows(mine, other):
        block = jnp.where(ctx == 0, jnp.concatenate([mine, other], 0), jnp.concatenate([other, mine], 0))
        full = lax.all_gather(block, "shard", axis=0, tiled=True)
        return tuple(full[k * width // 4 : (k + 1) * width // 4] for k in range(4))

    r = row_count
    x_in, d_in = inputs.reshape(local_len, width), cotangent.reshape(local_len, width)
    unit_vals = unit_biases.astype(F32)
    my_units = lax.dynamic_slice_in_dim(unit_vals, ctx * heads, heads, 0)
    qkv_bias, unit_bias = my_units[:, :head_wide].reshape(1, n_qkv), my_units[:, head_wide:].reshape(1, units)
    positions = ((jnp.arange(4) ^ z)[:, None] * quarter + jnp.arange(quarter)[None, :]).reshape(-1)
    cosine, sine = rotary_tables(positions)

    n = up_weight.shape[1] // 2
    units_other = to_ctx(cut_quarter(ctx_scalar, 1, up_weight, down_weight))
    mine = cut_quarter(ctx_scalar, 0, up_weight, down_weight, qkv_weight, dense_weight)
    if fast:
        a_x, a_y = to_x(mine), to_y(mine)
    x_own, d_own, vec = arrange(place, x_in, d_in, vectors)
    attn_own, mlp_own, mean_own, inv_own = norm(x_own, vec)
    if fast:
        top, low = halves(a_y, a_x)
        a_top, a_low = to_x(top), to_y(low)
    wait(units_other)
    attn_other = to_ctx(cut_quarter(ctx_scalar, 1, qkv_weight, dense_weight))
    if fast:
        units_x, units_y = to_x(units_other), to_y(units_other)
    wait(attn_other)
    x_first = to_ctx(outgoing(place, x_in))

    def packed(pieces, k):
        near = pack(n, *[(a, k) for a in pieces])
        return near, to_core(near)

    if fast:
        mine_parts = (mine, a_y, a_x, a_top, a_low)
        up_a, up_far_a = packed(mine_parts, 0)
        down_a, down_far_a = packed(mine_parts, 1)
        top, low = halves(units_y, units_x)
        units_parts = (units_other, units_x, units_y, to_x(top), to_y(low))
        attn_x, attn_y = to_x(attn_other), to_y(attn_other)
        attn_a, attn_far_a = packed(mine_parts, 2)
        up_b, up_far_b = packed(units_parts, 0)
        top, low = halves(attn_y, attn_x)
        attn_parts = (attn_other, attn_x, attn_y, to_x(top), to_y(low))
        down_b, down_far_b = packed(units_parts, 1)
        w_up, w_down = (up_a, up_b, up_far_a, up_far_b), (down_a, down_b, down_far_a, down_far_b)
    else:
        w_up = full_rows(mine[:, :n], units_other[:, :n])
        w_down = full_rows(mine[:, n : 2 * n], units_other[:, n:])
        w_attn = full_rows(mine[:, 2 * n :], attn_other)
    active_own, slope_own = hidden_of(mlp_own, w_up, unit_bias)
    if fast:
        attn_b, attn_far_b = packed(attn_parts, 0)
        w_attn = (attn_a, attn_b, attn_far_a, attn_far_b)
    wait(x_first)
    d_first = to_ctx(outgoing(place, d_in))
    x_second = to_ten(x_first)
    low_own, sum_own = d_hidden_of(d_own, w_down, slope_own)
    x_oth = pack(width, x_first, x_second)
    attn_oth, mlp_oth, mean_oth, inv_oth = norm(x_oth, vec)
    active_oth, slope_oth = hidden_of(mlp_oth, w_up, unit_bias)
    wait(d_first)
    d_second = to_ten(d_first)
    context_out, packed_qkv, logs = attend(z_scalar, attn_own, attn_oth, w_attn, qkv_bias, cosine, sine)
    *branch_own, branch_keep, branch_send = branch_of(active_own, active_oth, context_out, w_down, w_attn)
    branch_got = to_ten(branch_send)
    branch_near = to_ten(branch_own[1])
    d_oth = pack(width, d_first, d_second)

    def far_parts(factors):
        parts = grad_of(factors)
        return [to_core(part) for part in parts] if fast else parts

    def near_parts(factors, far):
        if fast:
            a_own, a_x, b_own, b_y = grad_of(factors, far)
            return a_own, b_own, to_y(b_y), to_x(a_x)
        near = grad_of(factors, [jnp.zeros_like(part) for part in far])
        return lax.psum_scatter(jnp.concatenate([*near, *far], 0), "shard", scatter_dimension=0, tiled=True)

    def second(parts):
        if not fast:
            return parts
        a_own, b_own, b_got, a_got = parts
        b_sum, a_sum = totals(r, ((b_own, 1), (b_got, 1)), ((a_own, 1), (a_got, 1)))
        return (*parts, to_x(b_sum), to_y(a_sum))

    def third(parts):
        if not fast:
            kept = lax.dynamic_slice_in_dim(parts, ctx * r, r, 0)
            zero = jnp.zeros_like(kept)
            return (kept, zero, zero), to_ctx(lax.dynamic_slice_in_dim(parts, (1 - ctx) * r, r, 0))
        a_own, b_own, b_got, a_got, b_last, a_last = parts
        (away,) = totals(r, ((b_own, 0), (b_got, 0), (b_last, 0)))
        return (a_own, a_got, a_last), to_ctx(away)

    low_oth, sum_oth = d_hidden_of(d_oth, w_down, slope_oth)
    unit_factors = [(mlp_own, mlp_oth, (low_own, 0), (low_oth, 0)), (d_own, d_oth, (active_own, 0), (active_oth, 0))]
    unit_far = far_parts(unit_factors)
    branch_far = to_ctx(fold(cross, branch_keep, branch_got))
    d_linear, unit_sums = attend_back(z_scalar, packed_qkv, logs, d_own, d_oth, w_attn, cosine, sine)
    unit_pieces = near_parts(unit_factors, unit_far)
    *g_own, g_keep, g_send, sums = input_grad_of(
        d_linear, low_own, low_oth, w_attn, w_up, (x_own, x_oth), (mean_own, mean_oth), (inv_own, inv_oth), vec
    )
    g_got = to_ten(g_send)
    g_near = to_ten(g_own[1])
    attn_factors = [
        (attn_own, attn_oth, (d_linear, 0), (d_linear, 1)),
        (d_own, d_oth, (context_out, 0), (context_out, 1)),
    ]
    attn_far = far_parts(attn_factors)
    unit_pieces = second(unit_pieces)
    out_bias = (vec[4] + vec[5]).reshape(1, width)
    (out_own,) = totals(quarter, ((branch_own[0], 0), (branch_near, 0), (branch_far, 0), (x_own, 0), (out_bias, 0)), steps=2)
    out_other = to_ten(out_own)
    g_far = to_ctx(fold(cross, g_keep, g_got))
    attn_pieces = near_parts(attn_factors, attn_far)

    d_sum = jnp.sum(d_own[:quarter].astype(F32), 0, keepdims=True)
    sums = unorder(place, jnp.concatenate([sums[:4], d_sum, jnp.zeros((3, width), F32)], 0))
    unit_part = jnp.concatenate(
        [unit_sums[0].reshape(heads, head_wide), (sum_own + sum_oth)[0].reshape(heads, units // heads)], 1
    )
    unit_rows = jnp.where(jnp.arange(4)[:, None, None] == ten * 2 + ctx, unit_part[None], 0.0)
    total = jnp.concatenate([sums.reshape(-1), unit_rows.reshape(-1)]).reshape(-1, BLOCK)
    moves = [to_ten, to_ctx] + [along("shard", shard_count, 1 << k) for k in range(shard_count.bit_length() - 1)]

    def shared(total, moves):
        for move in moves:
            (total,) = totals(total.shape[0], ((total, 0), (move(total), 0)), dtype=F32)
        return total

    count_value = step_count.astype(F32)
    fixes = jnp.stack([1.0 - jnp.power(BETA_ONE, count_value), jnp.sqrt(1.0 - jnp.power(BETA_TWO, count_value))])
    total = shared(total, moves[:1])
    unit_terms, unit_theirs = third(unit_pieces)
    attn_pieces = second(attn_pieces)
    total = shared(total, moves[1:2])
    (g_sum,) = totals(quarter, ((g_own[0], 0), (g_near, 0), (g_far, 0)), steps=2)
    g_other = to_ten(g_sum)
    total = shared(total, moves[2:3])
    attn_terms, attn_theirs = third(attn_pieces)
    total = shared(total, moves[3:]).reshape(-1)
    vector_grad = total[: 5 * width].reshape(5, width)
    vector_grad = jnp.concatenate([vector_grad, vector_grad[4:]], 0)
    unit_all = total[8 * width :].reshape(4 * heads, unit_part.shape[1])
    unit_grad = lax.dynamic_slice_in_dim(unit_all, ten * 2 * heads, 2 * heads, 0)
    up_grad, up_new, up_change = adam(ctx_scalar, fixes, up_weight, up_moments, unit_terms, unit_theirs)
    down_grad, down_new, down_change = adam(ctx_scalar, fixes, down_weight, down_moments, unit_terms, unit_theirs, first=n)
    outputs, input_grad = finish(place, out_own, out_other, g_sum, g_other, x_own, d_own)
    qkv_grad, qkv_new, qkv_change = adam_heads(ctx_scalar, fixes, qkv_weight, qkv_moments, attn_terms, attn_theirs)
    dense_grad, dense_new, dense_change = adam(
        ctx_scalar, fixes, dense_weight, dense_moments, attn_terms, attn_theirs, tile=head_cols, first=n_qkv
    )
    unit_new, unit_change = adam_step(unit_vals, unit_moments, unit_grad, count_value, 0.0)
    vector_new, vector_change = adam_step(vectors.astype(F32), vector_moments, vector_grad, count_value, 0.0)
    return (
        outputs.reshape(inputs.shape),
        input_grad.reshape(inputs.shape),
        qkv_grad,
        dense_grad,
        up_grad,
        down_grad,
        unit_grad,
        vector_grad,
        qkv_new,
        dense_new,
        up_new,
        down_new,
        unit_new,
        vector_new,
        qkv_change,
        dense_change,
        up_change,
        down_change,
        unit_change,
        vector_change,
    )


def solution(mesh):
    rows = ("shard", "context")
    tokens = P("shard", "context", None)
    qkv, matrix, units = P(rows, "tensor", None), P(rows, "tensor"), P("tensor", None)
    qkv_pair, matrix_pair, units_pair = P(None, rows, "tensor", None), P(None, rows, "tensor"), P(None, "tensor", None)
    params = (qkv, matrix, matrix, matrix, units, P())
    states = (qkv_pair, matrix_pair, matrix_pair, matrix_pair, units_pair, P())
    return jax.shard_map(
        functools.partial(on_device, mesh.shape["shard"]),
        mesh=mesh,
        in_specs=(tokens, tokens, *params, *states, P()),
        out_specs=(tokens, tokens, *params, *states, *params),
        check_vma=False,
    )
```

```python
import functools
import math

import jax
import jax.numpy as jnp
from jax import lax
from jax.experimental import pallas as pl
from jax.experimental.pallas import tpu as pltpu
from jax.sharding import PartitionSpec as P

HEAD_DIM = 256
ROTARY = 64
EPSILON = 1e-05
BETA_ONE = 0.9
BETA_TWO = 0.95
LEARN_RATE = 0.02
WEIGHT_DECAY = 0.01
ROOT_HALF = 0.7071067811865476
ROOT_TWO_PI = 2.5066282746310002
MASKED = -1000000000.0
BF = jnp.bfloat16
F32 = jnp.float32


def dot(a, b, ca, cb):
    return lax.dot_general(a, b, (((ca,), (cb,)), ((), ())), preferred_element_type=F32)


def gelu_value(hidden):
    return 0.5 * hidden * (1.0 + lax.erf(hidden * ROOT_HALF))


def gelu_slope(hidden):
    return (
        0.5 * (1.0 + lax.erf(hidden * ROOT_HALF))
        + hidden * jnp.exp(-0.5 * hidden * hidden) / ROOT_TWO_PI
    )


BLOCK = 128
MIB = 1024 * 1024
COSTS = [50, 50, 50, 50, 50, 10, 0.5, 5, 5, 50, 50, 5, 0.5, 50, 50, 2, 0, 50, 50, 50, 50, 0.5, 50, 0.5, 20, 10, 10, 50, 0.5, 50, 2, 50, 10, 0, 50, 50, 0.5, 50, 50, 50, 50, 0.5, 0, 50, 5, 5, 5, 0, 20, 0.5, 50, 20, 10, 50, 20, 50, 50, 0.5, 0, 50, 50, 50, 50, 10, 50]


def whole(shape):
    return pl.BlockSpec(shape, lambda *_: (0,) * len(shape), pipeline_mode=pl.Buffered(1))


ORDER = []
CALLS = []


def call(kernel, grid, in_specs, out_specs, out_shape, name, flops, nbytes, prefetch=0, scratch=(), limit=56):
    single = not isinstance(out_shape, (list, tuple))
    specs, shapes = ([out_specs], [out_shape]) if single else (list(out_specs), list(out_shape))
    waits = tuple(ORDER)
    cost = COSTS[len(CALLS)] if len(CALLS) < len(COSTS) else 10
    CALLS.append(name)
    first, outs = prefetch + len(in_specs), len(shapes)
    anywhere = pl.BlockSpec(memory_space=pl.ANY)

    def ordered(*refs):
        rest = refs[first + len(waits) :]
        kernel(*refs[:first], *rest[:outs], *rest[outs + 1 :])

    run = pl.pallas_call(
        ordered,
        grid_spec=pltpu.PrefetchScalarGridSpec(
            num_scalar_prefetch=prefetch,
            grid=grid,
            in_specs=[*in_specs, *[anywhere] * len(waits)],
            out_specs=[*specs, anywhere],
            scratch_shapes=list(scratch),
        ),
        out_shape=[*shapes, like((8, 128), F32)],
        compiler_params=pltpu.CompilerParams(vmem_limit_bytes=limit * MIB),
        cost_estimate=pl.CostEstimate(flops=int(cost * 1e9), bytes_accessed=1, transcendentals=0),
        name=name,
    )

    def ordered_call(*operands):
        *results, token = run(*operands, *waits)
        ORDER[:] = [token]
        return results[0] if single else results

    return ordered_call


def like(shape, dtype):
    return jax.ShapeDtypeStruct(shape, dtype)


def cut_kernel(flip, c_ref, *refs):
    *operands, out_ref = refs
    col = 0
    for ref in operands:
        if len(ref.shape) == 3:
            heads, wide = ref.shape[1] // 2, ref.shape[2]
            for c in range(2):

                @pl.when(c_ref[0] == c)
                def _(c=c, ref=ref, col=col):
                    for h in range(heads):
                        out_ref[:, col + h * wide : col + (h + 1) * wide] = ref[:, (c ^ flip) * heads + h, :]

            col += heads * wide
        else:
            n = ref.shape[1] // 2
            out_ref[:, col : col + n] = ref[:, pl.ds(pl.multiple_of((c_ref[0] ^ flip) * n, n), n)]
            col += n


def cut_quarter(ctx, flip, *operands):
    rows = operands[0].shape[0]
    n = sum(a.size for a in operands) // rows // 2
    return call(
        functools.partial(cut_kernel, flip),
        (1,),
        [whole(a.shape) for a in operands],
        whole((rows, n)),
        like((rows, n), BF),
        "cut",
        0,
        6 * rows * n,
        prefetch=1,
    )(ctx, *operands)


def arrange_kernel(place_ref, x_ref, d_ref, v_ref, xo_ref, do_ref, vo_ref):
    width = x_ref.shape[1]
    count = width // BLOCK
    rows = x_ref.shape[0] // 2
    for j in range(count):
        out = slice(j * BLOCK, (j + 1) * BLOCK)
        col = pl.ds(pl.multiple_of(place_ref[j] * BLOCK, BLOCK), BLOCK)
        for b in range(2):
            row = pl.ds(pl.multiple_of((place_ref[2 * count] ^ b) * rows, rows), rows)
            xo_ref[b * rows : (b + 1) * rows, out] = x_ref[row, col]
            do_ref[b * rows : (b + 1) * rows, out] = d_ref[row, col]
        vo_ref[:, out] = v_ref[:, col].astype(F32)


def arrange(place, x, d, v):
    operands = (x, d, v)
    outs = [(x.shape, BF), (d.shape, BF), (v.shape, F32)]
    return call(
        arrange_kernel,
        (1,),
        [whole(a.shape) for a in operands],
        [whole(a) for a, _ in outs],
        [like(*a) for a in outs],
        "arrange",
        0,
        4 * x.size * 2,
        prefetch=1,
    )(place, *operands)


def outgoing_kernel(place_ref, x_ref, o_ref):
    count = x_ref.shape[1] // BLOCK
    for j in range(count):
        col = pl.ds(pl.multiple_of(place_ref[count + j] * BLOCK, BLOCK), BLOCK)
        o_ref[:, j * BLOCK : (j + 1) * BLOCK] = x_ref[:, col]


def outgoing(place, x):
    rows, width = x.shape[0] // 2, x.shape[1]
    return call(
        outgoing_kernel,
        (1,),
        [pl.BlockSpec((rows, width), lambda i, p: (p[2 * width // BLOCK], 0))],
        whole((rows, width)),
        like((rows, width), BF),
        "outgoing",
        0,
        x.size * 2,
        prefetch=1,
    )(place, x)


def unorder_kernel(place_ref, v_ref, o_ref):
    for j in range(v_ref.shape[1] // BLOCK):
        col = pl.ds(pl.multiple_of(place_ref[j] * BLOCK, BLOCK), BLOCK)
        o_ref[:, col] = v_ref[:, j * BLOCK : (j + 1) * BLOCK]


def unorder(place, v):
    return call(
        unorder_kernel, (1,), [whole(v.shape)], whole(v.shape), like(v.shape, v.dtype), "unorder", 0, v.size * 8, prefetch=1
    )(place, v)


def pack_kernel(*refs):
    *pieces, out_ref = refs
    row = 0
    for piece in pieces:
        out_ref[row : row + piece.shape[0], :] = piece[...]
        row += piece.shape[0]


def pack(n, *pieces):
    pieces = [p if isinstance(p, tuple) else (p, 0) for p in pieces]
    rows = sum(p.shape[0] for p, _ in pieces)
    return call(
        pack_kernel,
        (1,),
        [pl.BlockSpec((p.shape[0], n), lambda i, k=k: (0, k)) for p, k in pieces],
        whole((rows, n)),
        like((rows, n), BF),
        "pack",
        0,
        rows * n * 4,
    )(*[p for p, _ in pieces])


def halves_kernel(u_ref, v_ref, top_ref, low_ref):
    top_ref[...] = u_ref[...]
    low_ref[...] = v_ref[...]


def halves(u, v):
    rows, n = u.shape[0] // 2, u.shape[1]
    return call(
        halves_kernel,
        (1,),
        [pl.BlockSpec((rows, n), lambda i: (0, 0)), pl.BlockSpec((rows, n), lambda i: (1, 0))],
        [whole((rows, n))] * 2,
        [like((rows, n), BF)] * 2,
        "halves",
        0,
        8 * rows * n,
    )(u, v)


def total_kernel(counts, *refs):
    at = 0
    for k, count in enumerate(counts):
        total = refs[at][...].astype(F32)
        for ref in refs[at + 1 : at + count]:
            total = total + ref[...].astype(F32)
        out_ref = refs[sum(counts) + k]
        out_ref[...] = total.astype(out_ref.dtype)
        at += count


def totals(rows, *groups, dtype=BF, steps=1):
    tile = rows // steps
    in_specs, operands = [], []
    for group in groups:
        for a, k in group:
            if a.shape[0] == 1:
                in_specs.append(whole(a.shape))
            else:
                in_specs.append(pl.BlockSpec((tile, a.shape[1]), lambda i, k=k: (k * steps + i, 0)))
            operands.append(a)
    width = operands[0].shape[1]
    return call(
        functools.partial(total_kernel, [len(g) for g in groups]),
        (steps,),
        in_specs,
        [pl.BlockSpec((tile, width), lambda i: (i, 0))] * len(groups),
        [like((rows, width), dtype)] * len(groups),
        "totals",
        0,
        8 * rows * width,
    )(*operands)


def norm_kernel(x_ref, v_ref, attn_ref, mlp_ref, mean_ref, inv_ref):
    x = x_ref[...].astype(F32)
    mean = jnp.mean(x, -1, keepdims=True)
    center = x - mean
    inv_std = lax.rsqrt(jnp.mean(center * center, -1, keepdims=True) + EPSILON)
    normed = center * inv_std
    attn_ref[...] = (normed * v_ref[0:1, :] + v_ref[1:2, :]).astype(BF)
    mlp_ref[...] = (normed * v_ref[2:3, :] + v_ref[3:4, :]).astype(BF)
    mean_ref[...] = jnp.broadcast_to(mean, mean_ref.shape)
    inv_ref[...] = jnp.broadcast_to(inv_std, inv_ref.shape)


def norm(x, vec):
    rows, width = x.shape
    tile = rows // 2
    block = pl.BlockSpec((tile, width), lambda i: (i, 0))
    stat = pl.BlockSpec((tile, 128), lambda i: (i, 0))
    return call(
        norm_kernel,
        (2,),
        [block, whole(vec.shape)],
        [block, block, stat, stat],
        [like(x.shape, BF), like(x.shape, BF), like((rows, 128), F32), like((rows, 128), F32)],
        "norm",
        x.size * 12,
        x.size * 6,
    )(x, vec)


def over_rows(a, weight):
    rows = weight[0].shape[0]
    return sum(dot(a[:, k * rows : (k + 1) * rows], part[...], 1, 0) for k, part in enumerate(weight))


def hidden_kernel(a_ref, b_ref, *refs):
    *weight, act_ref, slope_ref = refs
    hidden = over_rows(a_ref[...], weight) + b_ref[...]
    cdf = 0.5 * (1.0 + lax.erf(hidden * ROOT_HALF))
    act_ref[...] = (hidden * cdf).astype(BF)
    slope_ref[...] = cdf + hidden * jnp.exp(-0.5 * hidden * hidden) * (1.0 / ROOT_TWO_PI)


def units_kernel(parts, a_ref, d_ref, b_ref, *refs):
    weights, (act_ref, low_ref, sum_ref) = refs[: 2 * parts], refs[2 * parts :]
    hidden = over_rows(a_ref[...], weights[:parts]) + b_ref[...]
    cdf = 0.5 * (1.0 + lax.erf(hidden * ROOT_HALF))
    act_ref[...] = (hidden * cdf).astype(BF)
    slope = cdf + hidden * jnp.exp(-0.5 * hidden * hidden) * (1.0 / ROOT_TWO_PI)
    grad = over_rows(d_ref[...], weights[parts:]) * slope
    low_ref[...] = grad.astype(BF)
    sum_ref[...] = jnp.broadcast_to(jnp.sum(grad, 0, keepdims=True), sum_ref.shape)


def units_of(a, d, up, down, bias, tile=256):
    (rows, width), n = a.shape, up[0].shape[1]
    out = pl.BlockSpec((rows, tile), lambda j: (0, j))
    at = lambda j: (0, j)
    return call(
        functools.partial(units_kernel, len(up)),
        (n // tile,),
        [whole(a.shape), whole(d.shape), pl.BlockSpec((1, tile), at), *column_specs((*up, *down), tile, at)],
        [out, out, pl.BlockSpec((8, tile), at)],
        [like((rows, n), BF), like((rows, n), BF), like((8, n), F32)],
        "units",
        4 * rows * width * n,
        (a.size * 2 + width * n * 2 + rows * n * 2) * 2,
    )(a, d, bias, *up, *down)


def column_specs(weight, tile, at):
    return [pl.BlockSpec((part.shape[0], tile), at) for part in weight]


def hidden_of(a, weight, bias, tile=512):
    (rows, width), n = a.shape, weight[0].shape[1]
    tile = min(tile, n)
    out = pl.BlockSpec((rows, tile), lambda j: (0, j))
    return call(
        hidden_kernel,
        (n // tile,),
        [whole(a.shape), pl.BlockSpec((1, tile), lambda j: (0, j)), *column_specs(weight, tile, lambda j: (0, j))],
        [out, out],
        [like((rows, n), BF), like((rows, n), F32)],
        "hidden",
        2 * rows * width * n,
        (a.size + width * n + rows * n * 3) * 2,
    )(a, bias, *weight)


def d_hidden_kernel(d_ref, slope_ref, *refs):
    *weight, low_ref, sum_ref = refs
    grad = over_rows(d_ref[...], weight) * slope_ref[...]
    low_ref[...] = grad.astype(BF)
    sum_ref[...] = jnp.broadcast_to(jnp.sum(grad, 0, keepdims=True), sum_ref.shape)


def d_hidden_of(d, weight, slope, tile=512):
    (rows, width), n = d.shape, weight[0].shape[1]
    tile = min(tile, n)
    out = pl.BlockSpec((rows, tile), lambda j: (0, j))
    return call(
        d_hidden_kernel,
        (n // tile,),
        [whole(d.shape), out, *column_specs(weight, tile, lambda j: (0, j))],
        [out, pl.BlockSpec((8, tile), lambda j: (0, j))],
        [like((rows, n), BF), like((8, n), F32)],
        "d_hidden",
        2 * rows * width * n,
        (d.size + width * n + rows * n * 3) * 2,
    )(d, slope, *weight)


def turn(block, cosine, sine):
    head = block[:, :128]
    lane = lax.broadcasted_iota(jnp.int32, head.shape, 1)
    half = ROTARY // 2
    partner = jnp.where(lane < half, -pltpu.roll(head, 128 - half, 1), pltpu.roll(head, half, 1))
    return jnp.concatenate([head * cosine + partner * sine, block[:, 128:]], 1)


def attend_kernel(
    z_ref, a0_ref, a1_ref, b_ref, cos_ref, sin_ref, *refs
):
    *weight, ctx_ref, pack_ref, log_ref = refs
    z = z_ref[0]
    size = a0_ref.shape[0] // 2
    hd = HEAD_DIM
    scale = hd**-0.5

    def row_of(p):
        return pl.ds(pl.multiple_of((z ^ p) * size, size), size)

    for b in range(4):
        a = (a0_ref, a1_ref)[b // 2][b % 2 * size : (b % 2 + 1) * size, :]
        lin = over_rows(a, weight) + b_ref[...]
        mine = slice(b * size, (b + 1) * size)
        cosine, sine = cos_ref[mine, :], sin_ref[mine, :]
        rows = row_of(b)
        pack_ref[rows, :hd] = turn(lin[:, :hd], cosine, sine).astype(BF)
        pack_ref[rows, hd : 2 * hd] = turn(lin[:, hd : 2 * hd], cosine, sine).astype(BF)
        pack_ref[rows, 2 * hd :] = lin[:, 2 * hd :].astype(BF)
    for p in range(4):
        here, seen = slice(p * size, (p + 1) * size), slice(0, (p + 1) * size)
        scores = dot(pack_ref[here, :hd], pack_ref[seen, hd : 2 * hd], 1, 1) * scale
        row_ids = p * size + lax.broadcasted_iota(jnp.int32, scores.shape, 0)
        col_ids = lax.broadcasted_iota(jnp.int32, scores.shape, 1)
        scores = jnp.where(row_ids >= col_ids, scores, MASKED)
        top = jnp.max(scores, -1, keepdims=True)
        exponent = jnp.exp(scores - top)
        total = jnp.sum(exponent, -1, keepdims=True)
        low = (exponent * (1.0 / total)).astype(BF)
        ctx_ref[row_of(p), :] = dot(low, pack_ref[seen, 2 * hd :], 1, 0).astype(BF)
        log_ref[here, :] = jnp.broadcast_to(top + jnp.log(total), (size, log_ref.shape[1]))


def attend(z, a0, a1, weight, bias, cosine, sine):
    length, width = 2 * a0.shape[0], a0.shape[1]
    hd = HEAD_DIM
    heads = bias.shape[1] // (3 * hd)
    column = lambda rows, cols: pl.BlockSpec((rows, cols), lambda h, p: (0, h))
    return call(
        attend_kernel,
        (heads,),
        [
            whole(a0.shape),
            whole(a1.shape),
            column(1, 3 * hd),
            whole(cosine.shape),
            whole(sine.shape),
            *column_specs(weight, 3 * hd, lambda h, p: (0, h)),
        ],
        [column(length, hd), column(length, 3 * hd), column(length, 128)],
        [like((length, heads * hd), BF), like((length, heads * 3 * hd), BF), like((length, heads * 128), F32)],
        "attend",
        (3 * length * length * hd + 6 * length * width * hd) * heads,
        length * width * 8,
        prefetch=1,
    )(z, a0, a1, bias, cosine, sine, *weight)


def attend_back_kernel(
    z_ref, pack_ref, log_ref, d0_ref, d1_ref, cos_ref, sin_ref, *refs
):
    *weight, dl_ref, us_ref, g_s, dk_s, dv_s = refs
    z = z_ref[0]
    size = d0_ref.shape[0] // 2
    hd = HEAD_DIM
    scale = hd**-0.5

    def row_of(p):
        return pl.ds(pl.multiple_of((z ^ p) * size, size), size)

    for half, d_ref in enumerate((d0_ref, d1_ref)):
        grad = over_rows(d_ref[...], weight).astype(BF)
        g_s[row_of(2 * half), :] = grad[:size]
        g_s[row_of(2 * half + 1), :] = grad[size:]
    dk_s[...] = jnp.zeros_like(dk_s)
    dv_s[...] = jnp.zeros_like(dv_s)
    q_sum = jnp.zeros((1, hd), F32)
    for p in range(4):
        here, seen = slice(p * size, (p + 1) * size), slice(0, (p + 1) * size)
        rows = row_of(p)
        queries, grads = pack_ref[here, :hd], g_s[here, :]
        keys, values = pack_ref[seen, hd : 2 * hd], pack_ref[seen, 2 * hd :]
        scores = dot(queries, keys, 1, 1) * scale
        row_ids = p * size + lax.broadcasted_iota(jnp.int32, scores.shape, 0)
        col_ids = lax.broadcasted_iota(jnp.int32, scores.shape, 1)
        scores = jnp.where(row_ids >= col_ids, scores, MASKED)
        probs = jnp.exp(scores - log_ref[here, 0:1])
        low = probs.astype(BF)
        weight_grad = dot(grads, values, 1, 1)
        score_grad = (
            probs * (weight_grad - jnp.sum(probs * weight_grad, -1, keepdims=True))
        ).astype(BF)
        query_grad = (dot(score_grad, keys, 1, 0) * scale).astype(BF).astype(F32)
        dk_s[seen, :] += dot(score_grad, queries, 0, 0)
        dv_s[seen, :] += dot(low, grads, 0, 0)
        query_grad = turn(query_grad, cos_ref[rows, :], -sin_ref[rows, :])
        q_sum = q_sum + jnp.sum(query_grad, 0, keepdims=True)
        dl_ref[rows, :hd] = query_grad.astype(BF)
    k_sum = jnp.zeros((1, hd), F32)
    v_sum = jnp.zeros((1, hd), F32)
    for p in range(4):
        here = slice(p * size, (p + 1) * size)
        rows = row_of(p)
        key_grad = (dk_s[here, :] * scale).astype(BF).astype(F32)
        key_grad = turn(key_grad, cos_ref[rows, :], -sin_ref[rows, :])
        k_sum = k_sum + jnp.sum(key_grad, 0, keepdims=True)
        dl_ref[rows, hd : 2 * hd] = key_grad.astype(BF)
        value_grad = dv_s[here, :].astype(BF)
        v_sum = v_sum + jnp.sum(value_grad.astype(F32), 0, keepdims=True)
        dl_ref[rows, 2 * hd :] = value_grad
    us_ref[...] = jnp.broadcast_to(jnp.concatenate([q_sum, k_sum, v_sum], 1), us_ref.shape)


def attend_back(z, packed, logs, d0, d1, weight, cosine, sine):
    length, wide = packed.shape
    hd = HEAD_DIM
    heads = wide // (3 * hd)
    first = wide // hd
    column = lambda rows, cols: pl.BlockSpec((rows, cols), lambda h, p: (0, h))
    return call(
        attend_back_kernel,
        (heads,),
        [
            column(length, 3 * hd),
            column(length, 128),
            whole(d0.shape),
            whole(d1.shape),
            whole(cosine.shape),
            whole(sine.shape),
            *column_specs(weight, hd, lambda h, p: (0, first + h)),
        ],
        [column(length, 3 * hd), column(8, 3 * hd)],
        [like((length, wide), BF), like((8, wide), F32)],
        "attend_back",
        (9 * length * length * hd + 2 * length * d0.shape[1] * hd) * heads,
        length * wide * 8,
        prefetch=1,
        scratch=[pltpu.VMEM((length, hd), BF)] + [pltpu.VMEM((length, hd), F32)] * 2,
    )(z, packed, logs, d0, d1, cosine, sine, *weight)


def in_turn(parts, body):
    j = pl.program_id(0)
    each = pl.num_programs(0) // len(parts)
    for k, part in enumerate(parts):

        @pl.when(j // each == k)
        def _(part=part):
            body(*part)


def row_specs(shape, count, parts, col=0):
    each = count // parts
    return [pl.BlockSpec(shape, lambda j, k=k: (jnp.clip(j - k * each, 0, each - 1), col)) for k in range(parts)]


def branch_kernel(parts, a0_ref, a1_ref, ctx_ref, *refs):
    weights, outs = refs[: 2 * parts], refs[2 * parts :]
    size = outs[0].shape[0]

    def body(down_ref, dense_ref):
        for k, act_ref in enumerate((a0_ref, a1_ref)):
            ctx = ctx_ref[2 * k * size : 2 * (k + 1) * size, :]
            part = dot(act_ref[...], down_ref[...], 1, 1) + dot(ctx, dense_ref[...], 1, 1)
            outs[2 * k][...] = part[:size]
            outs[2 * k + 1][...] = part[size:].astype(BF)

    in_turn(list(zip(weights[:parts], weights[parts:])), body)


def token_outs(size, width, tile):
    spec = pl.BlockSpec((size, tile), lambda j: (0, j))
    return [spec] * 4, [like((size, width), F32), like((size, width), BF)] * 2


def branch_of(a0, a1, context_out, down, attn, tile=256):
    rows, n = a0.shape
    parts = len(down)
    width = parts * down[0].shape[0]
    cols = context_out.shape[1]
    count = width // tile
    specs, shapes = token_outs(rows // 2, width, tile)
    return call(
        functools.partial(branch_kernel, parts),
        (count,),
        [
            whole(a0.shape),
            whole(a1.shape),
            whole(context_out.shape),
            *row_specs((tile, n), count, parts),
            *row_specs((tile, cols), count, parts, attn[0].shape[1] // cols - 1),
        ],
        specs,
        shapes,
        "branch",
        4 * rows * width * (n + cols),
        (2 * rows * (n + cols) + width * (n + cols) + 2 * rows * width * 2) * 2,
    )(a0, a1, context_out, *down, *attn)


def input_grad_kernel(
    parts, dl_ref, h0_ref, h1_ref, x0_ref, x1_ref, m0_ref, m1_ref, i0_ref, i1_ref, v_ref, *refs
):
    weights, outs = refs[: 2 * parts], refs[2 * parts :]
    size = outs[0].shape[0]
    wide = dl_ref.shape[1]
    halves = ((h0_ref, x0_ref, m0_ref, i0_ref), (h1_ref, x1_ref, m1_ref, i1_ref))

    def body(attn_ref, up_ref):
        total = [0.0] * 4
        for k, (dh_ref, x_ref, mean_ref, inv_ref) in enumerate(halves):
            attn = dot(dl_ref[2 * k * size : 2 * (k + 1) * size, :], attn_ref[:, :wide], 1, 1)
            mlp = dot(dh_ref[...], up_ref[...], 1, 1)
            part = attn * v_ref[0:1, :] + mlp * v_ref[2:3, :]
            outs[2 * k][...] = part[:size]
            outs[2 * k + 1][...] = part[size:].astype(BF)
            normed = (x_ref[...].astype(F32) - mean_ref[:, 0:1]) * inv_ref[:, 0:1]
            sums = [jnp.sum(v, 0, keepdims=True) for v in (attn * normed, attn, mlp * normed, mlp)]
            total = [u + v for u, v in zip(total, sums)]
        outs[4][...] = jnp.concatenate(total + [jnp.zeros((4, attn.shape[1]), F32)], 0)

    in_turn(list(zip(weights[:parts], weights[parts:])), body)


def input_grad_of(d_linear, h0, h1, attn, up, xs, means, invs, vec, tile=256):
    rows, n = h0.shape
    width = xs[0].shape[1]
    wide = d_linear.shape[1]
    parts = len(attn)
    count = width // tile
    specs, shapes = token_outs(rows // 2, width, tile)
    column = pl.BlockSpec((rows, tile), lambda j: (0, j))
    return call(
        functools.partial(input_grad_kernel, parts),
        (count,),
        [
            whole(d_linear.shape),
            whole(h0.shape),
            whole(h1.shape),
            column,
            column,
            *[whole(a.shape) for a in (*means, *invs)],
            pl.BlockSpec((vec.shape[0], tile), lambda j: (0, j)),
            *row_specs((tile, attn[0].shape[1]), count, parts),
            *row_specs((tile, n), count, parts),
        ],
        [*specs, pl.BlockSpec((8, tile), lambda j: (0, j))],
        [*shapes, like((8, width), F32)],
        "input_grad",
        4 * rows * width * (n + wide),
        (2 * rows * (n + wide) + width * (n + wide) + 2 * rows * width * 3) * 2,
    )(d_linear, h0, h1, *xs, *means, *invs, vec, *attn, *up)


def grad_kernel(pairs, near, *refs):
    operands, refs = refs[: 4 * pairs], refs[4 * pairs :]
    adds, outs = (refs[:4], refs[4:]) if near else (None, refs)
    j = pl.program_id(0)
    col = 0
    for k in range(pairs):
        l0, l1, r0, r1 = (r[...] for r in operands[4 * k : 4 * k + 4])
        part = dot(l0, r0, 0, 0) + dot(l1, r1, 0, 0)
        cols = slice(col, col + part.shape[1])
        col += part.shape[1]
        for i, out_ref in enumerate(outs):

            @pl.when(j == i)
            def _(i=i, out_ref=out_ref, part=part, cols=cols):
                if near:
                    out_ref[:, cols] = (part + adds[i][:, cols].astype(F32)).astype(BF)
                else:
                    out_ref[:, cols] = part.astype(BF)


def grad_of(factors, adds=()):
    width = factors[0][0].shape[1]
    tile = width // 8
    first = 0 if adds else 4
    in_specs, operands, n, flops, nbytes = [], [], 0, 0, 0
    for l0, l1, r0, r1 in factors:
        rows = l0.shape[0]
        for left in (l0, l1):
            in_specs.append(pl.BlockSpec((rows, tile), lambda j: (0, first + j)))
            operands.append(left)
        cols = r0[0].shape[1]
        for right, k in (r0, r1):
            in_specs.append(pl.BlockSpec((rows, cols), lambda j, k=k: (k, 0), pipeline_mode=pl.Buffered(1)))
            operands.append(right)
        n += cols
        flops += 2 * rows * width * cols
        nbytes += 2 * rows * (width + 2 * cols)
    in_specs += [whole((tile, n)) for _ in adds]
    return call(
        functools.partial(grad_kernel, len(factors), bool(adds)),
        (4,),
        in_specs,
        [whole((tile, n))] * 4,
        [like((tile, n), BF)] * 4,
        "grad_near" if adds else "grad_far",
        flops,
        nbytes + width * n,
    )(*operands, *adds)


def fold_kernel(cross, keep_ref, got_ref, o_ref):
    for j, k in enumerate(cross):
        here = slice(j * BLOCK, (j + 1) * BLOCK)
        o_ref[:, k * BLOCK : (k + 1) * BLOCK] = (keep_ref[:, here] + got_ref[:, here].astype(F32)).astype(BF)


def fold(cross, keep, got):
    rows, width = keep.shape
    tile = rows // 2
    block = pl.BlockSpec((tile, width), lambda i: (i, 0))
    return call(
        functools.partial(fold_kernel, cross), (2,), [block, block], block, like(keep.shape, BF), "fold", keep.size, keep.size * 8
    )(keep, got)


def finish_kernel(place_ref, o0_ref, o1_ref, g0_ref, g1_ref, x_ref, d_ref, out_ref, grad_ref):
    width = x_ref.shape[1]
    count = width // BLOCK
    x = x_ref[...].astype(F32)
    center = x - jnp.mean(x, -1, keepdims=True)
    inv_std = lax.rsqrt(jnp.mean(center * center, -1, keepdims=True) + EPSILON)
    normed = center * inv_std

    def body(o_ref, g_ref):
        g = g_ref[...].astype(F32)
        grad = d_ref[...].astype(F32) + inv_std * (
            g - jnp.mean(g, -1, keepdims=True) - normed * jnp.mean(g * normed, -1, keepdims=True)
        )
        for j in range(count):
            col = pl.ds(pl.multiple_of(place_ref[j] * BLOCK, BLOCK), BLOCK)
            part = slice(j * BLOCK, (j + 1) * BLOCK)
            out_ref[:, col] = o_ref[:, part]
            grad_ref[:, col] = grad[:, part]

    in_turn(((o0_ref, g0_ref), (o1_ref, g1_ref)), body)


def finish(place, o0, o1, g0, g1, x, d):
    rows, width = o0.shape
    per = 2
    tile = rows // per
    at = 2 * width // BLOCK
    first = pl.BlockSpec((tile, width), lambda i, p: (jnp.minimum(i, per - 1), 0))
    second = pl.BlockSpec((tile, width), lambda i, p: (jnp.maximum(i - per, 0), 0))
    local = pl.BlockSpec((tile, width), lambda i, p: (i, 0))
    out = pl.BlockSpec((tile, width), lambda i, p: ((p[at] ^ (i // per)) * per + i % per, 0))
    return call(
        finish_kernel,
        (2 * per,),
        [first, second, first, second, local, local],
        [out, out],
        [like(x.shape, BF), like(x.shape, F32)],
        "finish",
        x.size * 20,
        x.size * 14,
        prefetch=1,
    )(place, o0, o1, g0, g1, x, d)


def step_values(weight, first, root, gradient, fix_one, fix_two, decay_rate):
    first_new = BETA_ONE * first + (1.0 - BETA_ONE) * gradient
    root_new = jnp.sqrt(BETA_TWO * root * root + (1.0 - BETA_TWO) * gradient * gradient)
    change = -LEARN_RATE * (
        first_new / fix_one / (root_new / fix_two + 1e-08) + decay_rate * weight
    )
    return first_new, root_new, change


def adam_kernel(c_ref, fix_ref, w_ref, m_ref, a_ref, b_ref, e_ref, t_ref, g_ref, n_ref, u_ref):
    def body(gradient):
        first, root, change = step_values(
            w_ref[...].astype(F32), m_ref[0], m_ref[1], gradient, fix_ref[0], fix_ref[1], WEIGHT_DECAY
        )
        g_ref[...] = gradient
        n_ref[0] = first
        n_ref[1] = root
        u_ref[...] = change

    @pl.when(pl.program_id(0) == 0)
    def _():
        body(a_ref[...].astype(F32) + b_ref[...].astype(F32) + e_ref[...].astype(F32))

    @pl.when(pl.program_id(0) == 1)
    def _():
        body(t_ref[...].astype(F32))


def adam(ctx, fixes, weight, moments, terms, theirs, tile=2048, first=0):
    rows, cols = weight.shape
    n = cols // 2
    tile = min(tile, n)
    first //= tile
    per = n // tile
    at = lambda k, i, c: (0, (c[0] ^ k) * per + i)
    mine = pl.BlockSpec((rows, tile), lambda k, i, c: (0, first + i + k * (per - 1 - i)))
    other = pl.BlockSpec((rows, tile), lambda k, i, c: (0, first + i * k))
    matrix = pl.BlockSpec((rows, tile), at)
    pair = pl.BlockSpec((2, rows, tile), lambda k, i, c: (0, *at(k, i, c)))
    return call(
        adam_kernel,
        (2, per),
        [pl.BlockSpec(memory_space=pltpu.SMEM), matrix, pair, mine, mine, mine, other],
        [matrix, pair, matrix],
        [like(weight.shape, F32), like(moments.shape, F32), like(weight.shape, F32)],
        "adam",
        weight.size * 20,
        weight.size * 30,
        prefetch=1,
    )(ctx, fixes, weight, moments, *terms, theirs)


def adam_heads_kernel(c_ref, fix_ref, w_ref, m_ref, a_ref, b_ref, e_ref, t_ref, g_ref, n_ref, u_ref):
    mine = a_ref[...].astype(F32) + b_ref[...].astype(F32) + e_ref[...].astype(F32)
    theirs = t_ref[...].astype(F32)
    heads, wide = w_ref.shape[1] // 2, w_ref.shape[2]
    for h in range(2 * heads):
        cols = slice(h % heads * wide, (h % heads + 1) * wide)
        gradient = jnp.where(c_ref[0] == h // heads, mine[:, cols], theirs[:, cols])
        first, root, change = step_values(
            w_ref[:, h, :].astype(F32), m_ref[0, :, h, :], m_ref[1, :, h, :], gradient, fix_ref[0], fix_ref[1], WEIGHT_DECAY
        )
        g_ref[:, h, :] = gradient
        n_ref[0, :, h, :] = first
        n_ref[1, :, h, :] = root
        u_ref[:, h, :] = change


def adam_heads(ctx, fixes, weight, moments, terms, theirs):
    rows, heads, wide = weight.shape
    tile = rows // 4
    part = pl.BlockSpec((tile, heads // 2 * wide), lambda i, c: (i, 0))
    cube = pl.BlockSpec((tile, heads, wide), lambda i, c: (i, 0, 0))
    pair = pl.BlockSpec((2, tile, heads, wide), lambda i, c: (0, i, 0, 0))
    return call(
        adam_heads_kernel,
        (4,),
        [pl.BlockSpec(memory_space=pltpu.SMEM), cube, pair, part, part, part, part],
        [cube, pair, cube],
        [like(weight.shape, F32), like(moments.shape, F32), like(weight.shape, F32)],
        "adam_heads",
        weight.size * 20,
        weight.size * 30,
        prefetch=1,
    )(ctx, fixes, weight, moments, *terms, theirs)


def rotary_tables(positions):
    lane = jnp.arange(128)
    inverse = jnp.exp((lane % (ROTARY // 2)).astype(F32) * (-2.0 / ROTARY) * math.log(10000.0))
    angles = positions.astype(F32)[:, None] * inverse[None, :]
    turned = lane[None, :] < ROTARY
    return (jnp.where(turned, jnp.cos(angles), 1.0), jnp.where(turned, jnp.sin(angles), 0.0))


def adam_step(weight, moments, gradient, count_value, decay_rate):
    first_new = BETA_ONE * moments[0] + (1.0 - BETA_ONE) * gradient
    root_new = jnp.sqrt(BETA_TWO * moments[1] * moments[1] + (1.0 - BETA_TWO) * gradient * gradient)
    fix_one = 1.0 - jnp.power(BETA_ONE, count_value)
    fix_two = 1.0 - jnp.power(BETA_TWO, count_value)
    change = -LEARN_RATE * (
        first_new / fix_one / (root_new / jnp.sqrt(fix_two) + 1e-08) + decay_rate * weight
    )
    return (jnp.stack([first_new, root_new]), change)


def on_device(
    shard_count,
    inputs,
    cotangent,
    qkv_weight,
    dense_weight,
    up_weight,
    down_weight,
    unit_biases,
    vectors,
    qkv_moments,
    dense_moments,
    up_moments,
    down_moments,
    unit_moments,
    vector_moments,
    step_count,
):
    ORDER.clear()
    CALLS.clear()
    shard, ctx, ten = (lax.axis_index(a) for a in ("shard", "context", "tensor"))
    fast = shard_count == 8
    _, local_len, width = inputs.shape
    quarter = local_len // 2
    row_count, heads_local, head_wide = qkv_weight.shape
    heads = heads_local // 2
    units = up_weight.shape[1] // 2
    head_cols = heads * HEAD_DIM
    n_qkv = heads * head_wide
    count = width // BLOCK

    def along(axis, size, bit):
        return lambda v: lax.ppermute(v, axis, [(i, i ^ bit) for i in range(size)])

    to_core, to_x, to_y = (along("shard", shard_count, bit) for bit in (1, 2, 4))
    to_ctx, to_ten = along("context", 2, 1), along("tensor", 2, 1)

    if fast:
        chips = ((0, 4, 2, 6), (0, 2, 4, 6))
        relative = [(core + chips[ab][k], ab) for core in range(2) for ab in range(2) for k in range(4)]
        places = [[(shard ^ s) * 2 + (ctx ^ f ^ ab) for s, ab in relative] for f in range(2)]
        cross = [core * 8 + (1 - ab) * 4 + (0, 2, 1, 3)[k] for core in range(2) for ab in range(2) for k in range(4)]
    else:
        places = [[jnp.int32(j) for j in range(count)]] * 2
        cross = list(range(count))
    place = jnp.stack([*places[0], *places[1], ten]).astype(jnp.int32)
    z = ctx * 2 + ten
    ctx_scalar, z_scalar = (v.reshape(1).astype(jnp.int32) for v in (ctx, z))

    def wait(*values):
        ORDER.extend(values)

    def full_rows(mine, other):
        block = jnp.where(ctx == 0, jnp.concatenate([mine, other], 0), jnp.concatenate([other, mine], 0))
        full = lax.all_gather(block, "shard", axis=0, tiled=True)
        return tuple(full[k * width // 4 : (k + 1) * width // 4] for k in range(4))

    r = row_count
    x_in, d_in = inputs.reshape(local_len, width), cotangent.reshape(local_len, width)
    unit_vals = unit_biases.astype(F32)
    my_units = lax.dynamic_slice_in_dim(unit_vals, ctx * heads, heads, 0)
    qkv_bias, unit_bias = my_units[:, :head_wide].reshape(1, n_qkv), my_units[:, head_wide:].reshape(1, units)
    positions = ((jnp.arange(4) ^ z)[:, None] * quarter + jnp.arange(quarter)[None, :]).reshape(-1)
    cosine, sine = rotary_tables(positions)

    n = up_weight.shape[1] // 2
    units_other = to_ctx(cut_quarter(ctx_scalar, 1, up_weight, down_weight))
    mine = cut_quarter(ctx_scalar, 0, up_weight, down_weight, qkv_weight, dense_weight)
    if fast:
        a_x, a_y = to_x(mine), to_y(mine)
    x_own, d_own, vec = arrange(place, x_in, d_in, vectors)
    attn_own, mlp_own, mean_own, inv_own = norm(x_own, vec)
    if fast:
        top, low = halves(a_y, a_x)
        a_top, a_low = to_x(top), to_y(low)
    wait(units_other)
    attn_other = to_ctx(cut_quarter(ctx_scalar, 1, qkv_weight, dense_weight))
    if fast:
        units_x, units_y = to_x(units_other), to_y(units_other)
    wait(attn_other)
    x_first = to_ctx(outgoing(place, x_in))

    def packed(pieces, k):
        near = pack(n, *[(a, k) for a in pieces])
        return near, to_core(near)

    if fast:
        mine_parts = (mine, a_y, a_x, a_top, a_low)
        up_a, up_far_a = packed(mine_parts, 0)
        down_a, down_far_a = packed(mine_parts, 1)
        top, low = halves(units_y, units_x)
        units_parts = (units_other, units_x, units_y, to_x(top), to_y(low))
        attn_x, attn_y = to_x(attn_other), to_y(attn_other)
        attn_a, attn_far_a = packed(mine_parts, 2)
        up_b, up_far_b = packed(units_parts, 0)
        top, low = halves(attn_y, attn_x)
        attn_parts = (attn_other, attn_x, attn_y, to_x(top), to_y(low))
        down_b, down_far_b = packed(units_parts, 1)
        w_up, w_down = (up_a, up_b, up_far_a, up_far_b), (down_a, down_b, down_far_a, down_far_b)
    else:
        w_up = full_rows(mine[:, :n], units_other[:, :n])
        w_down = full_rows(mine[:, n : 2 * n], units_other[:, n:])
        w_attn = full_rows(mine[:, 2 * n :], attn_other)
    active_own, slope_own = hidden_of(mlp_own, w_up, unit_bias)
    if fast:
        attn_b, attn_far_b = packed(attn_parts, 0)
        w_attn = (attn_a, attn_b, attn_far_a, attn_far_b)
    wait(x_first)
    d_first = to_ctx(outgoing(place, d_in))
    x_second = to_ten(x_first)
    low_own, sum_own = d_hidden_of(d_own, w_down, slope_own)
    x_oth = pack(width, x_first, x_second)
    attn_oth, mlp_oth, mean_oth, inv_oth = norm(x_oth, vec)
    active_oth, slope_oth = hidden_of(mlp_oth, w_up, unit_bias)
    wait(d_first)
    d_second = to_ten(d_first)
    context_out, packed_qkv, logs = attend(z_scalar, attn_own, attn_oth, w_attn, qkv_bias, cosine, sine)
    *branch_own, branch_keep, branch_send = branch_of(active_own, active_oth, context_out, w_down, w_attn)
    branch_got = to_ten(branch_send)
    branch_near = to_ten(branch_own[1])
    d_oth = pack(width, d_first, d_second)

    def far_parts(factors):
        parts = grad_of(factors)
        return [to_core(part) for part in parts] if fast else parts

    def near_parts(factors, far):
        if fast:
            a_own, a_x, b_own, b_y = grad_of(factors, far)
            return a_own, b_own, to_y(b_y), to_x(a_x)
        near = grad_of(factors, [jnp.zeros_like(part) for part in far])
        return lax.psum_scatter(jnp.concatenate([*near, *far], 0), "shard", scatter_dimension=0, tiled=True)

    def second(parts):
        if not fast:
            return parts
        a_own, b_own, b_got, a_got = parts
        b_sum, a_sum = totals(r, ((b_own, 1), (b_got, 1)), ((a_own, 1), (a_got, 1)))
        return (*parts, to_x(b_sum), to_y(a_sum))

    def third(parts):
        if not fast:
            kept = lax.dynamic_slice_in_dim(parts, ctx * r, r, 0)
            zero = jnp.zeros_like(kept)
            return (kept, zero, zero), to_ctx(lax.dynamic_slice_in_dim(parts, (1 - ctx) * r, r, 0))
        a_own, b_own, b_got, a_got, b_last, a_last = parts
        (away,) = totals(r, ((b_own, 0), (b_got, 0), (b_last, 0)))
        return (a_own, a_got, a_last), to_ctx(away)

    low_oth, sum_oth = d_hidden_of(d_oth, w_down, slope_oth)
    unit_factors = [(mlp_own, mlp_oth, (low_own, 0), (low_oth, 0)), (d_own, d_oth, (active_own, 0), (active_oth, 0))]
    unit_far = far_parts(unit_factors)
    branch_far = to_ctx(fold(cross, branch_keep, branch_got))
    d_linear, unit_sums = attend_back(z_scalar, packed_qkv, logs, d_own, d_oth, w_attn, cosine, sine)
    unit_pieces = near_parts(unit_factors, unit_far)
    *g_own, g_keep, g_send, sums = input_grad_of(
        d_linear, low_own, low_oth, w_attn, w_up, (x_own, x_oth), (mean_own, mean_oth), (inv_own, inv_oth), vec
    )
    g_got = to_ten(g_send)
    g_near = to_ten(g_own[1])
    attn_factors = [
        (attn_own, attn_oth, (d_linear, 0), (d_linear, 1)),
        (d_own, d_oth, (context_out, 0), (context_out, 1)),
    ]
    attn_far = far_parts(attn_factors)
    unit_pieces = second(unit_pieces)
    out_bias = (vec[4] + vec[5]).reshape(1, width)
    (out_own,) = totals(quarter, ((branch_own[0], 0), (branch_near, 0), (branch_far, 0), (x_own, 0), (out_bias, 0)), steps=2)
    out_other = to_ten(out_own)
    g_far = to_ctx(fold(cross, g_keep, g_got))
    attn_pieces = near_parts(attn_factors, attn_far)

    unit_terms, unit_theirs = third(unit_pieces)

    d_sum = jnp.sum(d_own[:quarter].astype(F32), 0, keepdims=True)
    sums = unorder(place, jnp.concatenate([sums[:4], d_sum, jnp.zeros((3, width), F32)], 0))
    unit_part = jnp.concatenate(
        [unit_sums[0].reshape(heads, head_wide), (sum_own + sum_oth)[0].reshape(heads, units // heads)], 1
    )
    unit_rows = jnp.where(jnp.arange(4)[:, None, None] == ten * 2 + ctx, unit_part[None], 0.0)
    total = jnp.concatenate([sums.reshape(-1), unit_rows.reshape(-1)]).reshape(-1, BLOCK)
    moves = [to_ten, to_ctx] + [along("shard", shard_count, 1 << k) for k in range(shard_count.bit_length() - 1)]

    def shared(total, moves):
        for move in moves:
            (total,) = totals(total.shape[0], ((total, 0), (move(total), 0)), dtype=F32)
        return total

    count_value = step_count.astype(F32)
    fixes = jnp.stack([1.0 - jnp.power(BETA_ONE, count_value), jnp.sqrt(1.0 - jnp.power(BETA_TWO, count_value))])
    attn_pieces = second(attn_pieces)
    wait(out_other)
    (g_sum,) = totals(quarter, ((g_own[0], 0), (g_near, 0), (g_far, 0)), steps=2)
    g_other = to_ten(g_sum)
    total = shared(total, moves[:1])
    attn_terms, attn_theirs = third(attn_pieces)
    total = shared(total, moves[1:2])
    up_grad, up_new, up_change = adam(ctx_scalar, fixes, up_weight, up_moments, unit_terms, unit_theirs)
    total = shared(total, moves[2:4])
    down_grad, down_new, down_change = adam(ctx_scalar, fixes, down_weight, down_moments, unit_terms, unit_theirs, first=n)
    total = shared(total, moves[4:]).reshape(-1)
    vector_grad = total[: 5 * width].reshape(5, width)
    vector_grad = jnp.concatenate([vector_grad, vector_grad[4:]], 0)
    unit_all = total[8 * width :].reshape(4 * heads, unit_part.shape[1])
    unit_grad = lax.dynamic_slice_in_dim(unit_all, ten * 2 * heads, 2 * heads, 0)
    outputs, input_grad = finish(place, out_own, out_other, g_sum, g_other, x_own, d_own)
    qkv_grad, qkv_new, qkv_change = adam_heads(ctx_scalar, fixes, qkv_weight, qkv_moments, attn_terms, attn_theirs)
    dense_grad, dense_new, dense_change = adam(
        ctx_scalar, fixes, dense_weight, dense_moments, attn_terms, attn_theirs, tile=head_cols, first=n_qkv
    )
    unit_new, unit_change = adam_step(unit_vals, unit_moments, unit_grad, count_value, 0.0)
    vector_new, vector_change = adam_step(vectors.astype(F32), vector_moments, vector_grad, count_value, 0.0)
    return (
        outputs.reshape(inputs.shape),
        input_grad.reshape(inputs.shape),
        qkv_grad,
        dense_grad,
        up_grad,
        down_grad,
        unit_grad,
        vector_grad,
        qkv_new,
        dense_new,
        up_new,
        down_new,
        unit_new,
        vector_new,
        qkv_change,
        dense_change,
        up_change,
        down_change,
        unit_change,
        vector_change,
    )


def solution(mesh):
    rows = ("shard", "context")
    tokens = P("shard", "context", None)
    qkv, matrix, units = P(rows, "tensor", None), P(rows, "tensor"), P("tensor", None)
    qkv_pair, matrix_pair, units_pair = P(None, rows, "tensor", None), P(None, rows, "tensor"), P(None, "tensor", None)
    params = (qkv, matrix, matrix, matrix, units, P())
    states = (qkv_pair, matrix_pair, matrix_pair, matrix_pair, units_pair, P())
    return jax.shard_map(
        functools.partial(on_device, mesh.shape["shard"]),
        mesh=mesh,
        in_specs=(tokens, tokens, *params, *states, P()),
        out_specs=(tokens, tokens, *params, *states, *params),
        check_vma=False,
    )
```

```python
import functools
import math

import jax
import jax.numpy as jnp
from jax import lax
from jax.experimental import pallas as pl
from jax.experimental.pallas import tpu as pltpu
from jax.sharding import PartitionSpec as P

HEAD_DIM = 256
ROTARY = 64
EPSILON = 1e-05
BETA_ONE = 0.9
BETA_TWO = 0.95
LEARN_RATE = 0.02
WEIGHT_DECAY = 0.01
ROOT_HALF = 0.7071067811865476
ROOT_TWO_PI = 2.5066282746310002
MASKED = -1000000000.0
BF = jnp.bfloat16
F32 = jnp.float32


def dot(a, b, ca, cb):
    return lax.dot_general(a, b, (((ca,), (cb,)), ((), ())), preferred_element_type=F32)


def gelu_value(hidden):
    return 0.5 * hidden * (1.0 + lax.erf(hidden * ROOT_HALF))


def gelu_slope(hidden):
    return (
        0.5 * (1.0 + lax.erf(hidden * ROOT_HALF))
        + hidden * jnp.exp(-0.5 * hidden * hidden) / ROOT_TWO_PI
    )


BLOCK = 128
MIB = 1024 * 1024
COSTS = [50, 50, 20, 0.5, 10, 10, 0.5, 5, 5, 2, 50, 50, 50, 50, 50, 20, 0, 50, 50, 5, 20, 0.5, 20, 0, 0, 50, 2, 50, 0.5, 2, 10, 0, 0, 0, 10, 10, 0, 0.5, 5, 0, 2, 0, 0, 0, 0, 20, 0, 0, 50, 0, 20, 0, 0, 20, 0, 0, 0, 0, 20, 0, 10, 10, 10, 5, 20, 0]


def whole(shape):
    return pl.BlockSpec(shape, lambda *_: (0,) * len(shape), pipeline_mode=pl.Buffered(1))


ORDER = []
CALLS = []


def call(kernel, grid, in_specs, out_specs, out_shape, name, flops, nbytes, prefetch=0, scratch=(), limit=56):
    single = not isinstance(out_shape, (list, tuple))
    specs, shapes = ([out_specs], [out_shape]) if single else (list(out_specs), list(out_shape))
    waits = tuple(ORDER)
    cost = COSTS[len(CALLS)] if len(CALLS) < len(COSTS) else 10
    CALLS.append(name)
    first, outs = prefetch + len(in_specs), len(shapes)
    anywhere = pl.BlockSpec(memory_space=pl.ANY)

    def ordered(*refs):
        rest = refs[first + len(waits) :]
        kernel(*refs[:first], *rest[:outs], *rest[outs + 1 :])

    run = pl.pallas_call(
        ordered,
        grid_spec=pltpu.PrefetchScalarGridSpec(
            num_scalar_prefetch=prefetch,
            grid=grid,
            in_specs=[*in_specs, *[anywhere] * len(waits)],
            out_specs=[*specs, anywhere],
            scratch_shapes=list(scratch),
        ),
        out_shape=[*shapes, like((8, 128), F32)],
        compiler_params=pltpu.CompilerParams(vmem_limit_bytes=limit * MIB),
        cost_estimate=pl.CostEstimate(flops=int(cost * 1e9), bytes_accessed=1, transcendentals=0),
        name=name,
    )

    def ordered_call(*operands):
        *results, token = run(*operands, *waits)
        ORDER[:] = [token]
        return results[0] if single else results

    return ordered_call


def like(shape, dtype):
    return jax.ShapeDtypeStruct(shape, dtype)


def cut_kernel(flip, c_ref, *refs):
    *operands, out_ref = refs
    col = 0
    for ref in operands:
        if len(ref.shape) == 3:
            heads, wide = ref.shape[1] // 2, ref.shape[2]
            for c in range(2):

                @pl.when(c_ref[0] == c)
                def _(c=c, ref=ref, col=col):
                    for h in range(heads):
                        out_ref[:, col + h * wide : col + (h + 1) * wide] = ref[:, (c ^ flip) * heads + h, :]

            col += heads * wide
        else:
            n = ref.shape[1] // 2
            out_ref[:, col : col + n] = ref[:, pl.ds(pl.multiple_of((c_ref[0] ^ flip) * n, n), n)]
            col += n


def cut_quarter(ctx, flip, *operands):
    rows = operands[0].shape[0]
    n = sum(a.size for a in operands) // rows // 2
    return call(
        functools.partial(cut_kernel, flip),
        (1,),
        [whole(a.shape) for a in operands],
        whole((rows, n)),
        like((rows, n), BF),
        "cut",
        0,
        6 * rows * n,
        prefetch=1,
    )(ctx, *operands)


def arrange_kernel(place_ref, x_ref, d_ref, v_ref, xo_ref, do_ref, vo_ref):
    width = x_ref.shape[1]
    count = width // BLOCK
    rows = x_ref.shape[0] // 2
    for j in range(count):
        out = slice(j * BLOCK, (j + 1) * BLOCK)
        col = pl.ds(pl.multiple_of(place_ref[j] * BLOCK, BLOCK), BLOCK)
        for b in range(2):
            row = pl.ds(pl.multiple_of((place_ref[2 * count] ^ b) * rows, rows), rows)
            xo_ref[b * rows : (b + 1) * rows, out] = x_ref[row, col]
            do_ref[b * rows : (b + 1) * rows, out] = d_ref[row, col]
        vo_ref[:, out] = v_ref[:, col].astype(F32)


def arrange(place, x, d, v):
    operands = (x, d, v)
    outs = [(x.shape, BF), (d.shape, BF), (v.shape, F32)]
    return call(
        arrange_kernel,
        (1,),
        [whole(a.shape) for a in operands],
        [whole(a) for a, _ in outs],
        [like(*a) for a in outs],
        "arrange",
        0,
        4 * x.size * 2,
        prefetch=1,
    )(place, *operands)


def outgoing_kernel(place_ref, x_ref, o_ref):
    count = x_ref.shape[1] // BLOCK
    for j in range(count):
        col = pl.ds(pl.multiple_of(place_ref[count + j] * BLOCK, BLOCK), BLOCK)
        o_ref[:, j * BLOCK : (j + 1) * BLOCK] = x_ref[:, col]


def outgoing(place, x):
    rows, width = x.shape[0] // 2, x.shape[1]
    return call(
        outgoing_kernel,
        (1,),
        [pl.BlockSpec((rows, width), lambda i, p: (p[2 * width // BLOCK], 0))],
        whole((rows, width)),
        like((rows, width), BF),
        "outgoing",
        0,
        x.size * 2,
        prefetch=1,
    )(place, x)


def unorder_kernel(place_ref, v_ref, o_ref):
    for j in range(v_ref.shape[1] // BLOCK):
        col = pl.ds(pl.multiple_of(place_ref[j] * BLOCK, BLOCK), BLOCK)
        o_ref[:, col] = v_ref[:, j * BLOCK : (j + 1) * BLOCK]


def unorder(place, v):
    return call(
        unorder_kernel, (1,), [whole(v.shape)], whole(v.shape), like(v.shape, v.dtype), "unorder", 0, v.size * 8, prefetch=1
    )(place, v)


def pack_kernel(*refs):
    *pieces, out_ref = refs
    row = 0
    for piece in pieces:
        out_ref[row : row + piece.shape[0], :] = piece[...]
        row += piece.shape[0]


def pack(n, *pieces):
    pieces = [p if isinstance(p, tuple) else (p, 0) for p in pieces]
    rows = sum(p.shape[0] for p, _ in pieces)
    return call(
        pack_kernel,
        (1,),
        [pl.BlockSpec((p.shape[0], n), lambda i, k=k: (0, k)) for p, k in pieces],
        whole((rows, n)),
        like((rows, n), BF),
        "pack",
        0,
        rows * n * 4,
    )(*[p for p, _ in pieces])


def halves_kernel(u_ref, v_ref, top_ref, low_ref):
    top_ref[...] = u_ref[...]
    low_ref[...] = v_ref[...]


def halves(u, v):
    rows, n = u.shape[0] // 2, u.shape[1]
    return call(
        halves_kernel,
        (1,),
        [pl.BlockSpec((rows, n), lambda i: (0, 0)), pl.BlockSpec((rows, n), lambda i: (1, 0))],
        [whole((rows, n))] * 2,
        [like((rows, n), BF)] * 2,
        "halves",
        0,
        8 * rows * n,
    )(u, v)


def total_kernel(counts, *refs):
    at = 0
    for k, count in enumerate(counts):
        total = refs[at][...].astype(F32)
        for ref in refs[at + 1 : at + count]:
            total = total + ref[...].astype(F32)
        out_ref = refs[sum(counts) + k]
        out_ref[...] = total.astype(out_ref.dtype)
        at += count


def totals(rows, *groups, dtype=BF, steps=1):
    tile = rows // steps
    in_specs, operands = [], []
    for group in groups:
        for a, k in group:
            if a.shape[0] == 1:
                in_specs.append(whole(a.shape))
            else:
                in_specs.append(pl.BlockSpec((tile, a.shape[1]), lambda i, k=k: (k * steps + i, 0)))
            operands.append(a)
    width = operands[0].shape[1]
    return call(
        functools.partial(total_kernel, [len(g) for g in groups]),
        (steps,),
        in_specs,
        [pl.BlockSpec((tile, width), lambda i: (i, 0))] * len(groups),
        [like((rows, width), dtype)] * len(groups),
        "totals",
        0,
        8 * rows * width,
    )(*operands)


def norm_kernel(x_ref, v_ref, attn_ref, mlp_ref, mean_ref, inv_ref):
    x = x_ref[...].astype(F32)
    mean = jnp.mean(x, -1, keepdims=True)
    center = x - mean
    inv_std = lax.rsqrt(jnp.mean(center * center, -1, keepdims=True) + EPSILON)
    normed = center * inv_std
    attn_ref[...] = (normed * v_ref[0:1, :] + v_ref[1:2, :]).astype(BF)
    mlp_ref[...] = (normed * v_ref[2:3, :] + v_ref[3:4, :]).astype(BF)
    mean_ref[...] = jnp.broadcast_to(mean, mean_ref.shape)
    inv_ref[...] = jnp.broadcast_to(inv_std, inv_ref.shape)


def norm(x, vec):
    rows, width = x.shape
    tile = rows // 2
    block = pl.BlockSpec((tile, width), lambda i: (i, 0))
    stat = pl.BlockSpec((tile, 128), lambda i: (i, 0))
    return call(
        norm_kernel,
        (2,),
        [block, whole(vec.shape)],
        [block, block, stat, stat],
        [like(x.shape, BF), like(x.shape, BF), like((rows, 128), F32), like((rows, 128), F32)],
        "norm",
        x.size * 12,
        x.size * 6,
    )(x, vec)


def over_rows(a, weight):
    rows = weight[0].shape[0]
    return sum(dot(a[:, k * rows : (k + 1) * rows], part[...], 1, 0) for k, part in enumerate(weight))


def hidden_kernel(a_ref, b_ref, *refs):
    *weight, act_ref, slope_ref = refs
    hidden = over_rows(a_ref[...], weight) + b_ref[...]
    cdf = 0.5 * (1.0 + lax.erf(hidden * ROOT_HALF))
    act_ref[...] = (hidden * cdf).astype(BF)
    slope_ref[...] = cdf + hidden * jnp.exp(-0.5 * hidden * hidden) * (1.0 / ROOT_TWO_PI)


def units_kernel(parts, a_ref, d_ref, b_ref, *refs):
    weights, (act_ref, low_ref, sum_ref) = refs[: 2 * parts], refs[2 * parts :]
    hidden = over_rows(a_ref[...], weights[:parts]) + b_ref[...]
    cdf = 0.5 * (1.0 + lax.erf(hidden * ROOT_HALF))
    act_ref[...] = (hidden * cdf).astype(BF)
    slope = cdf + hidden * jnp.exp(-0.5 * hidden * hidden) * (1.0 / ROOT_TWO_PI)
    grad = over_rows(d_ref[...], weights[parts:]) * slope
    low_ref[...] = grad.astype(BF)
    sum_ref[...] = jnp.broadcast_to(jnp.sum(grad, 0, keepdims=True), sum_ref.shape)


def units_of(a, d, up, down, bias, tile=256):
    (rows, width), n = a.shape, up[0].shape[1]
    out = pl.BlockSpec((rows, tile), lambda j: (0, j))
    at = lambda j: (0, j)
    return call(
        functools.partial(units_kernel, len(up)),
        (n // tile,),
        [whole(a.shape), whole(d.shape), pl.BlockSpec((1, tile), at), *column_specs((*up, *down), tile, at)],
        [out, out, pl.BlockSpec((8, tile), at)],
        [like((rows, n), BF), like((rows, n), BF), like((8, n), F32)],
        "units",
        4 * rows * width * n,
        (a.size * 2 + width * n * 2 + rows * n * 2) * 2,
    )(a, d, bias, *up, *down)


def column_specs(weight, tile, at):
    return [pl.BlockSpec((part.shape[0], tile), at) for part in weight]


def hidden_of(a, weight, bias, tile=512):
    (rows, width), n = a.shape, weight[0].shape[1]
    tile = min(tile, n)
    out = pl.BlockSpec((rows, tile), lambda j: (0, j))
    return call(
        hidden_kernel,
        (n // tile,),
        [whole(a.shape), pl.BlockSpec((1, tile), lambda j: (0, j)), *column_specs(weight, tile, lambda j: (0, j))],
        [out, out],
        [like((rows, n), BF), like((rows, n), F32)],
        "hidden",
        2 * rows * width * n,
        (a.size + width * n + rows * n * 3) * 2,
    )(a, bias, *weight)


def d_hidden_kernel(d_ref, slope_ref, *refs):
    *weight, low_ref, sum_ref = refs
    grad = over_rows(d_ref[...], weight) * slope_ref[...]
    low_ref[...] = grad.astype(BF)
    sum_ref[...] = jnp.broadcast_to(jnp.sum(grad, 0, keepdims=True), sum_ref.shape)


def d_hidden_of(d, weight, slope, tile=512):
    (rows, width), n = d.shape, weight[0].shape[1]
    tile = min(tile, n)
    out = pl.BlockSpec((rows, tile), lambda j: (0, j))
    return call(
        d_hidden_kernel,
        (n // tile,),
        [whole(d.shape), out, *column_specs(weight, tile, lambda j: (0, j))],
        [out, pl.BlockSpec((8, tile), lambda j: (0, j))],
        [like((rows, n), BF), like((8, n), F32)],
        "d_hidden",
        2 * rows * width * n,
        (d.size + width * n + rows * n * 3) * 2,
    )(d, slope, *weight)


def turn(block, cosine, sine):
    head = block[:, :128]
    lane = lax.broadcasted_iota(jnp.int32, head.shape, 1)
    half = ROTARY // 2
    partner = jnp.where(lane < half, -pltpu.roll(head, 128 - half, 1), pltpu.roll(head, half, 1))
    return jnp.concatenate([head * cosine + partner * sine, block[:, 128:]], 1)


def attend_kernel(
    z_ref, a0_ref, a1_ref, b_ref, cos_ref, sin_ref, *refs
):
    *weight, ctx_ref, pack_ref, log_ref = refs
    z = z_ref[0]
    size = a0_ref.shape[0] // 2
    hd = HEAD_DIM
    scale = hd**-0.5

    def row_of(p):
        return pl.ds(pl.multiple_of((z ^ p) * size, size), size)

    for b in range(4):
        a = (a0_ref, a1_ref)[b // 2][b % 2 * size : (b % 2 + 1) * size, :]
        lin = over_rows(a, weight) + b_ref[...]
        mine = slice(b * size, (b + 1) * size)
        cosine, sine = cos_ref[mine, :], sin_ref[mine, :]
        rows = row_of(b)
        pack_ref[rows, :hd] = turn(lin[:, :hd], cosine, sine).astype(BF)
        pack_ref[rows, hd : 2 * hd] = turn(lin[:, hd : 2 * hd], cosine, sine).astype(BF)
        pack_ref[rows, 2 * hd :] = lin[:, 2 * hd :].astype(BF)
    for p in range(4):
        here, seen = slice(p * size, (p + 1) * size), slice(0, (p + 1) * size)
        scores = dot(pack_ref[here, :hd], pack_ref[seen, hd : 2 * hd], 1, 1) * scale
        row_ids = p * size + lax.broadcasted_iota(jnp.int32, scores.shape, 0)
        col_ids = lax.broadcasted_iota(jnp.int32, scores.shape, 1)
        scores = jnp.where(row_ids >= col_ids, scores, MASKED)
        top = jnp.max(scores, -1, keepdims=True)
        exponent = jnp.exp(scores - top)
        total = jnp.sum(exponent, -1, keepdims=True)
        low = (exponent * (1.0 / total)).astype(BF)
        ctx_ref[row_of(p), :] = dot(low, pack_ref[seen, 2 * hd :], 1, 0).astype(BF)
        log_ref[here, :] = jnp.broadcast_to(top + jnp.log(total), (size, log_ref.shape[1]))


def attend(z, a0, a1, weight, bias, cosine, sine):
    length, width = 2 * a0.shape[0], a0.shape[1]
    hd = HEAD_DIM
    heads = bias.shape[1] // (3 * hd)
    column = lambda rows, cols: pl.BlockSpec((rows, cols), lambda h, p: (0, h))
    return call(
        attend_kernel,
        (heads,),
        [
            whole(a0.shape),
            whole(a1.shape),
            column(1, 3 * hd),
            whole(cosine.shape),
            whole(sine.shape),
            *column_specs(weight, 3 * hd, lambda h, p: (0, h)),
        ],
        [column(length, hd), column(length, 3 * hd), column(length, 128)],
        [like((length, heads * hd), BF), like((length, heads * 3 * hd), BF), like((length, heads * 128), F32)],
        "attend",
        (3 * length * length * hd + 6 * length * width * hd) * heads,
        length * width * 8,
        prefetch=1,
    )(z, a0, a1, bias, cosine, sine, *weight)


def attend_back_kernel(
    z_ref, pack_ref, log_ref, d0_ref, d1_ref, cos_ref, sin_ref, *refs
):
    *weight, dl_ref, us_ref, g_s, dk_s, dv_s = refs
    z = z_ref[0]
    size = d0_ref.shape[0] // 2
    hd = HEAD_DIM
    scale = hd**-0.5

    def row_of(p):
        return pl.ds(pl.multiple_of((z ^ p) * size, size), size)

    for half, d_ref in enumerate((d0_ref, d1_ref)):
        grad = over_rows(d_ref[...], weight).astype(BF)
        g_s[row_of(2 * half), :] = grad[:size]
        g_s[row_of(2 * half + 1), :] = grad[size:]
    dk_s[...] = jnp.zeros_like(dk_s)
    dv_s[...] = jnp.zeros_like(dv_s)
    q_sum = jnp.zeros((1, hd), F32)
    for p in range(4):
        here, seen = slice(p * size, (p + 1) * size), slice(0, (p + 1) * size)
        rows = row_of(p)
        queries, grads = pack_ref[here, :hd], g_s[here, :]
        keys, values = pack_ref[seen, hd : 2 * hd], pack_ref[seen, 2 * hd :]
        scores = dot(queries, keys, 1, 1) * scale
        row_ids = p * size + lax.broadcasted_iota(jnp.int32, scores.shape, 0)
        col_ids = lax.broadcasted_iota(jnp.int32, scores.shape, 1)
        scores = jnp.where(row_ids >= col_ids, scores, MASKED)
        probs = jnp.exp(scores - log_ref[here, 0:1])
        low = probs.astype(BF)
        weight_grad = dot(grads, values, 1, 1)
        score_grad = (
            probs * (weight_grad - jnp.sum(probs * weight_grad, -1, keepdims=True))
        ).astype(BF)
        query_grad = (dot(score_grad, keys, 1, 0) * scale).astype(BF).astype(F32)
        dk_s[seen, :] += dot(score_grad, queries, 0, 0)
        dv_s[seen, :] += dot(low, grads, 0, 0)
        query_grad = turn(query_grad, cos_ref[rows, :], -sin_ref[rows, :])
        q_sum = q_sum + jnp.sum(query_grad, 0, keepdims=True)
        dl_ref[rows, :hd] = query_grad.astype(BF)
    k_sum = jnp.zeros((1, hd), F32)
    v_sum = jnp.zeros((1, hd), F32)
    for p in range(4):
        here = slice(p * size, (p + 1) * size)
        rows = row_of(p)
        key_grad = (dk_s[here, :] * scale).astype(BF).astype(F32)
        key_grad = turn(key_grad, cos_ref[rows, :], -sin_ref[rows, :])
        k_sum = k_sum + jnp.sum(key_grad, 0, keepdims=True)
        dl_ref[rows, hd : 2 * hd] = key_grad.astype(BF)
        value_grad = dv_s[here, :].astype(BF)
        v_sum = v_sum + jnp.sum(value_grad.astype(F32), 0, keepdims=True)
        dl_ref[rows, 2 * hd :] = value_grad
    us_ref[...] = jnp.broadcast_to(jnp.concatenate([q_sum, k_sum, v_sum], 1), us_ref.shape)


def attend_back(z, packed, logs, d0, d1, weight, cosine, sine):
    length, wide = packed.shape
    hd = HEAD_DIM
    heads = wide // (3 * hd)
    first = wide // hd
    column = lambda rows, cols: pl.BlockSpec((rows, cols), lambda h, p: (0, h))
    return call(
        attend_back_kernel,
        (heads,),
        [
            column(length, 3 * hd),
            column(length, 128),
            whole(d0.shape),
            whole(d1.shape),
            whole(cosine.shape),
            whole(sine.shape),
            *column_specs(weight, hd, lambda h, p: (0, first + h)),
        ],
        [column(length, 3 * hd), column(8, 3 * hd)],
        [like((length, wide), BF), like((8, wide), F32)],
        "attend_back",
        (9 * length * length * hd + 2 * length * d0.shape[1] * hd) * heads,
        length * wide * 8,
        prefetch=1,
        scratch=[pltpu.VMEM((length, hd), BF)] + [pltpu.VMEM((length, hd), F32)] * 2,
    )(z, packed, logs, d0, d1, cosine, sine, *weight)


def in_turn(parts, body):
    j = pl.program_id(0)
    each = pl.num_programs(0) // len(parts)
    for k, part in enumerate(parts):

        @pl.when(j // each == k)
        def _(part=part):
            body(*part)


def row_specs(shape, count, parts, col=0):
    each = count // parts
    return [pl.BlockSpec(shape, lambda j, k=k: (jnp.clip(j - k * each, 0, each - 1), col)) for k in range(parts)]


def branch_kernel(parts, a0_ref, a1_ref, ctx_ref, *refs):
    weights, outs = refs[: 2 * parts], refs[2 * parts :]
    size = outs[0].shape[0]

    def body(down_ref, dense_ref):
        for k, act_ref in enumerate((a0_ref, a1_ref)):
            ctx = ctx_ref[2 * k * size : 2 * (k + 1) * size, :]
            part = dot(act_ref[...], down_ref[...], 1, 1) + dot(ctx, dense_ref[...], 1, 1)
            outs[2 * k][...] = part[:size]
            outs[2 * k + 1][...] = part[size:].astype(BF)

    in_turn(list(zip(weights[:parts], weights[parts:])), body)


def token_outs(size, width, tile):
    spec = pl.BlockSpec((size, tile), lambda j: (0, j))
    return [spec] * 4, [like((size, width), F32), like((size, width), BF)] * 2


def branch_of(a0, a1, context_out, down, attn, tile=256):
    rows, n = a0.shape
    parts = len(down)
    width = parts * down[0].shape[0]
    cols = context_out.shape[1]
    count = width // tile
    specs, shapes = token_outs(rows // 2, width, tile)
    return call(
        functools.partial(branch_kernel, parts),
        (count,),
        [
            whole(a0.shape),
            whole(a1.shape),
            whole(context_out.shape),
            *row_specs((tile, n), count, parts),
            *row_specs((tile, cols), count, parts, attn[0].shape[1] // cols - 1),
        ],
        specs,
        shapes,
        "branch",
        4 * rows * width * (n + cols),
        (2 * rows * (n + cols) + width * (n + cols) + 2 * rows * width * 2) * 2,
    )(a0, a1, context_out, *down, *attn)


def input_grad_kernel(
    parts, dl_ref, h0_ref, h1_ref, x0_ref, x1_ref, m0_ref, m1_ref, i0_ref, i1_ref, v_ref, *refs
):
    weights, outs = refs[: 2 * parts], refs[2 * parts :]
    size = outs[0].shape[0]
    wide = dl_ref.shape[1]
    halves = ((h0_ref, x0_ref, m0_ref, i0_ref), (h1_ref, x1_ref, m1_ref, i1_ref))

    def body(attn_ref, up_ref):
        total = [0.0] * 4
        for k, (dh_ref, x_ref, mean_ref, inv_ref) in enumerate(halves):
            attn = dot(dl_ref[2 * k * size : 2 * (k + 1) * size, :], attn_ref[:, :wide], 1, 1)
            mlp = dot(dh_ref[...], up_ref[...], 1, 1)
            part = attn * v_ref[0:1, :] + mlp * v_ref[2:3, :]
            outs[2 * k][...] = part[:size]
            outs[2 * k + 1][...] = part[size:].astype(BF)
            normed = (x_ref[...].astype(F32) - mean_ref[:, 0:1]) * inv_ref[:, 0:1]
            sums = [jnp.sum(v, 0, keepdims=True) for v in (attn * normed, attn, mlp * normed, mlp)]
            total = [u + v for u, v in zip(total, sums)]
        outs[4][...] = jnp.concatenate(total + [jnp.zeros((4, attn.shape[1]), F32)], 0)

    in_turn(list(zip(weights[:parts], weights[parts:])), body)


def input_grad_of(d_linear, h0, h1, attn, up, xs, means, invs, vec, tile=256):
    rows, n = h0.shape
    width = xs[0].shape[1]
    wide = d_linear.shape[1]
    parts = len(attn)
    count = width // tile
    specs, shapes = token_outs(rows // 2, width, tile)
    column = pl.BlockSpec((rows, tile), lambda j: (0, j))
    return call(
        functools.partial(input_grad_kernel, parts),
        (count,),
        [
            whole(d_linear.shape),
            whole(h0.shape),
            whole(h1.shape),
            column,
            column,
            *[whole(a.shape) for a in (*means, *invs)],
            pl.BlockSpec((vec.shape[0], tile), lambda j: (0, j)),
            *row_specs((tile, attn[0].shape[1]), count, parts),
            *row_specs((tile, n), count, parts),
        ],
        [*specs, pl.BlockSpec((8, tile), lambda j: (0, j))],
        [*shapes, like((8, width), F32)],
        "input_grad",
        4 * rows * width * (n + wide),
        (2 * rows * (n + wide) + width * (n + wide) + 2 * rows * width * 3) * 2,
    )(d_linear, h0, h1, *xs, *means, *invs, vec, *attn, *up)


def grad_kernel(pairs, near, *refs):
    operands, refs = refs[: 4 * pairs], refs[4 * pairs :]
    adds, outs = (refs[:4], refs[4:]) if near else (None, refs)
    j = pl.program_id(0)
    col = 0
    for k in range(pairs):
        l0, l1, r0, r1 = (r[...] for r in operands[4 * k : 4 * k + 4])
        part = dot(l0, r0, 0, 0) + dot(l1, r1, 0, 0)
        cols = slice(col, col + part.shape[1])
        col += part.shape[1]
        for i, out_ref in enumerate(outs):

            @pl.when(j == i)
            def _(i=i, out_ref=out_ref, part=part, cols=cols):
                if near:
                    out_ref[:, cols] = (part + adds[i][:, cols].astype(F32)).astype(BF)
                else:
                    out_ref[:, cols] = part.astype(BF)


def grad_of(factors, adds=()):
    width = factors[0][0].shape[1]
    tile = width // 8
    first = 0 if adds else 4
    in_specs, operands, n, flops, nbytes = [], [], 0, 0, 0
    for l0, l1, r0, r1 in factors:
        rows = l0.shape[0]
        for left in (l0, l1):
            in_specs.append(pl.BlockSpec((rows, tile), lambda j: (0, first + j)))
            operands.append(left)
        cols = r0[0].shape[1]
        for right, k in (r0, r1):
            in_specs.append(pl.BlockSpec((rows, cols), lambda j, k=k: (k, 0), pipeline_mode=pl.Buffered(1)))
            operands.append(right)
        n += cols
        flops += 2 * rows * width * cols
        nbytes += 2 * rows * (width + 2 * cols)
    in_specs += [whole((tile, n)) for _ in adds]
    return call(
        functools.partial(grad_kernel, len(factors), bool(adds)),
        (4,),
        in_specs,
        [whole((tile, n))] * 4,
        [like((tile, n), BF)] * 4,
        "grad_near" if adds else "grad_far",
        flops,
        nbytes + width * n,
    )(*operands, *adds)


def fold_kernel(cross, keep_ref, got_ref, o_ref):
    for j, k in enumerate(cross):
        here = slice(j * BLOCK, (j + 1) * BLOCK)
        o_ref[:, k * BLOCK : (k + 1) * BLOCK] = (keep_ref[:, here] + got_ref[:, here].astype(F32)).astype(BF)


def fold(cross, keep, got):
    rows, width = keep.shape
    tile = rows // 2
    block = pl.BlockSpec((tile, width), lambda i: (i, 0))
    return call(
        functools.partial(fold_kernel, cross), (2,), [block, block], block, like(keep.shape, BF), "fold", keep.size, keep.size * 8
    )(keep, got)


def finish_kernel(place_ref, o0_ref, o1_ref, g0_ref, g1_ref, x_ref, d_ref, out_ref, grad_ref):
    width = x_ref.shape[1]
    count = width // BLOCK
    x = x_ref[...].astype(F32)
    center = x - jnp.mean(x, -1, keepdims=True)
    inv_std = lax.rsqrt(jnp.mean(center * center, -1, keepdims=True) + EPSILON)
    normed = center * inv_std

    def body(o_ref, g_ref):
        g = g_ref[...].astype(F32)
        grad = d_ref[...].astype(F32) + inv_std * (
            g - jnp.mean(g, -1, keepdims=True) - normed * jnp.mean(g * normed, -1, keepdims=True)
        )
        for j in range(count):
            col = pl.ds(pl.multiple_of(place_ref[j] * BLOCK, BLOCK), BLOCK)
            part = slice(j * BLOCK, (j + 1) * BLOCK)
            out_ref[:, col] = o_ref[:, part]
            grad_ref[:, col] = grad[:, part]

    in_turn(((o0_ref, g0_ref), (o1_ref, g1_ref)), body)


def finish(place, o0, o1, g0, g1, x, d):
    rows, width = o0.shape
    per = 2
    tile = rows // per
    at = 2 * width // BLOCK
    first = pl.BlockSpec((tile, width), lambda i, p: (jnp.minimum(i, per - 1), 0))
    second = pl.BlockSpec((tile, width), lambda i, p: (jnp.maximum(i - per, 0), 0))
    local = pl.BlockSpec((tile, width), lambda i, p: (i, 0))
    out = pl.BlockSpec((tile, width), lambda i, p: ((p[at] ^ (i // per)) * per + i % per, 0))
    return call(
        finish_kernel,
        (2 * per,),
        [first, second, first, second, local, local],
        [out, out],
        [like(x.shape, BF), like(x.shape, F32)],
        "finish",
        x.size * 20,
        x.size * 14,
        prefetch=1,
    )(place, o0, o1, g0, g1, x, d)


def step_values(weight, first, root, gradient, fix_one, fix_two, decay_rate):
    first_new = BETA_ONE * first + (1.0 - BETA_ONE) * gradient
    root_new = jnp.sqrt(BETA_TWO * root * root + (1.0 - BETA_TWO) * gradient * gradient)
    change = -LEARN_RATE * (
        first_new / fix_one / (root_new / fix_two + 1e-08) + decay_rate * weight
    )
    return first_new, root_new, change


def adam_kernel(c_ref, fix_ref, w_ref, m_ref, a_ref, b_ref, e_ref, t_ref, g_ref, n_ref, u_ref):
    def body(gradient):
        first, root, change = step_values(
            w_ref[...].astype(F32), m_ref[0], m_ref[1], gradient, fix_ref[0], fix_ref[1], WEIGHT_DECAY
        )
        g_ref[...] = gradient
        n_ref[0] = first
        n_ref[1] = root
        u_ref[...] = change

    @pl.when(pl.program_id(0) == 0)
    def _():
        body(a_ref[...].astype(F32) + b_ref[...].astype(F32) + e_ref[...].astype(F32))

    @pl.when(pl.program_id(0) == 1)
    def _():
        body(t_ref[...].astype(F32))


def adam(ctx, fixes, weight, moments, terms, theirs, tile=2048, first=0):
    rows, cols = weight.shape
    n = cols // 2
    tile = min(tile, n)
    first //= tile
    per = n // tile
    at = lambda k, i, c: (0, (c[0] ^ k) * per + i)
    mine = pl.BlockSpec((rows, tile), lambda k, i, c: (0, first + i + k * (per - 1 - i)))
    other = pl.BlockSpec((rows, tile), lambda k, i, c: (0, first + i * k))
    matrix = pl.BlockSpec((rows, tile), at)
    pair = pl.BlockSpec((2, rows, tile), lambda k, i, c: (0, *at(k, i, c)))
    return call(
        adam_kernel,
        (2, per),
        [pl.BlockSpec(memory_space=pltpu.SMEM), matrix, pair, mine, mine, mine, other],
        [matrix, pair, matrix],
        [like(weight.shape, F32), like(moments.shape, F32), like(weight.shape, F32)],
        "adam",
        weight.size * 20,
        weight.size * 30,
        prefetch=1,
    )(ctx, fixes, weight, moments, *terms, theirs)


def adam_heads_kernel(c_ref, fix_ref, w_ref, m_ref, a_ref, b_ref, e_ref, t_ref, g_ref, n_ref, u_ref):
    mine = a_ref[...].astype(F32) + b_ref[...].astype(F32) + e_ref[...].astype(F32)
    theirs = t_ref[...].astype(F32)
    heads, wide = w_ref.shape[1] // 2, w_ref.shape[2]
    for h in range(2 * heads):
        cols = slice(h % heads * wide, (h % heads + 1) * wide)
        gradient = jnp.where(c_ref[0] == h // heads, mine[:, cols], theirs[:, cols])
        first, root, change = step_values(
            w_ref[:, h, :].astype(F32), m_ref[0, :, h, :], m_ref[1, :, h, :], gradient, fix_ref[0], fix_ref[1], WEIGHT_DECAY
        )
        g_ref[:, h, :] = gradient
        n_ref[0, :, h, :] = first
        n_ref[1, :, h, :] = root
        u_ref[:, h, :] = change


def adam_heads(ctx, fixes, weight, moments, terms, theirs):
    rows, heads, wide = weight.shape
    tile = rows // 4
    part = pl.BlockSpec((tile, heads // 2 * wide), lambda i, c: (i, 0))
    cube = pl.BlockSpec((tile, heads, wide), lambda i, c: (i, 0, 0))
    pair = pl.BlockSpec((2, tile, heads, wide), lambda i, c: (0, i, 0, 0))
    return call(
        adam_heads_kernel,
        (4,),
        [pl.BlockSpec(memory_space=pltpu.SMEM), cube, pair, part, part, part, part],
        [cube, pair, cube],
        [like(weight.shape, F32), like(moments.shape, F32), like(weight.shape, F32)],
        "adam_heads",
        weight.size * 20,
        weight.size * 30,
        prefetch=1,
    )(ctx, fixes, weight, moments, *terms, theirs)


def rotary_tables(positions):
    lane = jnp.arange(128)
    inverse = jnp.exp((lane % (ROTARY // 2)).astype(F32) * (-2.0 / ROTARY) * math.log(10000.0))
    angles = positions.astype(F32)[:, None] * inverse[None, :]
    turned = lane[None, :] < ROTARY
    return (jnp.where(turned, jnp.cos(angles), 1.0), jnp.where(turned, jnp.sin(angles), 0.0))


def adam_step(weight, moments, gradient, count_value, decay_rate):
    first_new = BETA_ONE * moments[0] + (1.0 - BETA_ONE) * gradient
    root_new = jnp.sqrt(BETA_TWO * moments[1] * moments[1] + (1.0 - BETA_TWO) * gradient * gradient)
    fix_one = 1.0 - jnp.power(BETA_ONE, count_value)
    fix_two = 1.0 - jnp.power(BETA_TWO, count_value)
    change = -LEARN_RATE * (
        first_new / fix_one / (root_new / jnp.sqrt(fix_two) + 1e-08) + decay_rate * weight
    )
    return (jnp.stack([first_new, root_new]), change)


def on_device(
    shard_count,
    inputs,
    cotangent,
    qkv_weight,
    dense_weight,
    up_weight,
    down_weight,
    unit_biases,
    vectors,
    qkv_moments,
    dense_moments,
    up_moments,
    down_moments,
    unit_moments,
    vector_moments,
    step_count,
):
    ORDER.clear()
    CALLS.clear()
    shard, ctx, ten = (lax.axis_index(a) for a in ("shard", "context", "tensor"))
    fast = shard_count == 8
    _, local_len, width = inputs.shape
    quarter = local_len // 2
    row_count, heads_local, head_wide = qkv_weight.shape
    heads = heads_local // 2
    units = up_weight.shape[1] // 2
    head_cols = heads * HEAD_DIM
    n_qkv = heads * head_wide
    count = width // BLOCK

    def along(axis, size, bit):
        return lambda v: lax.ppermute(v, axis, [(i, i ^ bit) for i in range(size)])

    to_core, to_x, to_y = (along("shard", shard_count, bit) for bit in (1, 2, 4))
    to_ctx, to_ten = along("context", 2, 1), along("tensor", 2, 1)

    if fast:
        chips = ((0, 4, 2, 6), (0, 2, 4, 6))
        relative = [(core + chips[ab][k], ab) for core in range(2) for ab in range(2) for k in range(4)]
        places = [[(shard ^ s) * 2 + (ctx ^ f ^ ab) for s, ab in relative] for f in range(2)]
        cross = [core * 8 + (1 - ab) * 4 + (0, 2, 1, 3)[k] for core in range(2) for ab in range(2) for k in range(4)]
    else:
        places = [[jnp.int32(j) for j in range(count)]] * 2
        cross = list(range(count))
    place = jnp.stack([*places[0], *places[1], ten]).astype(jnp.int32)
    z = ctx * 2 + ten
    ctx_scalar, z_scalar = (v.reshape(1).astype(jnp.int32) for v in (ctx, z))

    def wait(*values):
        ORDER.extend(values)

    def full_rows(mine, other):
        block = jnp.where(ctx == 0, jnp.concatenate([mine, other], 0), jnp.concatenate([other, mine], 0))
        full = lax.all_gather(block, "shard", axis=0, tiled=True)
        return tuple(full[k * width // 4 : (k + 1) * width // 4] for k in range(4))

    r = row_count
    x_in, d_in = inputs.reshape(local_len, width), cotangent.reshape(local_len, width)
    unit_vals = unit_biases.astype(F32)
    my_units = lax.dynamic_slice_in_dim(unit_vals, ctx * heads, heads, 0)
    qkv_bias, unit_bias = my_units[:, :head_wide].reshape(1, n_qkv), my_units[:, head_wide:].reshape(1, units)
    positions = ((jnp.arange(4) ^ z)[:, None] * quarter + jnp.arange(quarter)[None, :]).reshape(-1)
    cosine, sine = rotary_tables(positions)

    n = up_weight.shape[1] // 2
    units_other = to_ctx(cut_quarter(ctx_scalar, 1, up_weight, down_weight))
    mine = cut_quarter(ctx_scalar, 0, up_weight, down_weight, qkv_weight, dense_weight)
    if fast:
        a_x, a_y = to_x(mine), to_y(mine)
    x_own, d_own, vec = arrange(place, x_in, d_in, vectors)
    attn_own, mlp_own, mean_own, inv_own = norm(x_own, vec)
    if fast:
        top, low = halves(a_y, a_x)
        a_top, a_low = to_x(top), to_y(low)
    wait(units_other)
    attn_other = to_ctx(cut_quarter(ctx_scalar, 1, qkv_weight, dense_weight))
    if fast:
        units_x, units_y = to_x(units_other), to_y(units_other)
    wait(attn_other)
    x_first = to_ctx(outgoing(place, x_in))

    def packed(pieces, k):
        near = pack(n, *[(a, k) for a in pieces])
        return near, to_core(near)

    if fast:
        mine_parts = (mine, a_y, a_x, a_top, a_low)
        up_a, up_far_a = packed(mine_parts, 0)
        down_a, down_far_a = packed(mine_parts, 1)
        top, low = halves(units_y, units_x)
        units_parts = (units_other, units_x, units_y, to_x(top), to_y(low))
        attn_x, attn_y = to_x(attn_other), to_y(attn_other)
        attn_a, attn_far_a = packed(mine_parts, 2)
        up_b, up_far_b = packed(units_parts, 0)
        top, low = halves(attn_y, attn_x)
        attn_parts = (attn_other, attn_x, attn_y, to_x(top), to_y(low))
        down_b, down_far_b = packed(units_parts, 1)
        w_up, w_down = (up_a, up_b, up_far_a, up_far_b), (down_a, down_b, down_far_a, down_far_b)
    else:
        w_up = full_rows(mine[:, :n], units_other[:, :n])
        w_down = full_rows(mine[:, n : 2 * n], units_other[:, n:])
        w_attn = full_rows(mine[:, 2 * n :], attn_other)
    active_own, slope_own = hidden_of(mlp_own, w_up, unit_bias)
    if fast:
        attn_b, attn_far_b = packed(attn_parts, 0)
        w_attn = (attn_a, attn_b, attn_far_a, attn_far_b)
    wait(x_first)
    d_first = to_ctx(outgoing(place, d_in))
    x_second = to_ten(x_first)
    low_own, sum_own = d_hidden_of(d_own, w_down, slope_own)
    x_oth = pack(width, x_first, x_second)
    attn_oth, mlp_oth, mean_oth, inv_oth = norm(x_oth, vec)
    active_oth, slope_oth = hidden_of(mlp_oth, w_up, unit_bias)
    wait(d_first)
    d_second = to_ten(d_first)
    context_out, packed_qkv, logs = attend(z_scalar, attn_own, attn_oth, w_attn, qkv_bias, cosine, sine)
    *branch_own, branch_keep, branch_send = branch_of(active_own, active_oth, context_out, w_down, w_attn)
    branch_got = to_ten(branch_send)
    branch_near = to_ten(branch_own[1])
    d_oth = pack(width, d_first, d_second)

    def far_parts(factors):
        parts = grad_of(factors)
        return [to_core(part) for part in parts] if fast else parts

    def near_parts(factors, far):
        if fast:
            a_own, a_x, b_own, b_y = grad_of(factors, far)
            return a_own, b_own, to_y(b_y), to_x(a_x)
        near = grad_of(factors, [jnp.zeros_like(part) for part in far])
        return lax.psum_scatter(jnp.concatenate([*near, *far], 0), "shard", scatter_dimension=0, tiled=True)

    def second(parts):
        if not fast:
            return parts
        a_own, b_own, b_got, a_got = parts
        b_sum, a_sum = totals(r, ((b_own, 1), (b_got, 1)), ((a_own, 1), (a_got, 1)))
        return (*parts, to_x(b_sum), to_y(a_sum))

    def third(parts):
        if not fast:
            kept = lax.dynamic_slice_in_dim(parts, ctx * r, r, 0)
            zero = jnp.zeros_like(kept)
            return (kept, zero, zero), to_ctx(lax.dynamic_slice_in_dim(parts, (1 - ctx) * r, r, 0))
        a_own, b_own, b_got, a_got, b_last, a_last = parts
        wait(a_last)
        (away,) = totals(r, ((b_own, 0), (b_got, 0), (b_last, 0)))
        return (a_own, a_got, a_last), to_ctx(away)

    low_oth, sum_oth = d_hidden_of(d_oth, w_down, slope_oth)
    unit_factors = [(mlp_own, mlp_oth, (low_own, 0), (low_oth, 0)), (d_own, d_oth, (active_own, 0), (active_oth, 0))]
    unit_far = far_parts(unit_factors)
    branch_far = to_ctx(fold(cross, branch_keep, branch_got))
    d_linear, unit_sums = attend_back(z_scalar, packed_qkv, logs, d_own, d_oth, w_attn, cosine, sine)
    wait(branch_near)
    unit_pieces = near_parts(unit_factors, unit_far)
    *g_own, g_keep, g_send, sums = input_grad_of(
        d_linear, low_own, low_oth, w_attn, w_up, (x_own, x_oth), (mean_own, mean_oth), (inv_own, inv_oth), vec
    )
    g_got = to_ten(g_send)
    g_near = to_ten(g_own[1])
    attn_factors = [
        (attn_own, attn_oth, (d_linear, 0), (d_linear, 1)),
        (d_own, d_oth, (context_out, 0), (context_out, 1)),
    ]
    d_sum = jnp.sum(d_own[:quarter].astype(F32), 0, keepdims=True)
    sums = unorder(place, jnp.concatenate([sums[:4], d_sum, jnp.zeros((3, width), F32)], 0))
    unit_part = jnp.concatenate(
        [unit_sums[0].reshape(heads, head_wide), (sum_own + sum_oth)[0].reshape(heads, units // heads)], 1
    )
    unit_rows = jnp.where(jnp.arange(4)[:, None, None] == ten * 2 + ctx, unit_part[None], 0.0)
    total = jnp.concatenate([sums.reshape(-1), unit_rows.reshape(-1)]).reshape(-1, BLOCK)
    moves = [to_ctx] + [along("shard", shard_count, 1 << k) for k in range(shard_count.bit_length() - 1)] + [to_ten]
    moved = moves[0](total)

    def shared(total, moved, moves):
        (total,) = totals(total.shape[0], ((total, 0), (moved, 0)), dtype=F32)
        return total, moves[0](total) if moves else None

    attn_far = far_parts(attn_factors)
    out_bias = (vec[4] + vec[5]).reshape(1, width)
    (out_own,) = totals(quarter, ((branch_own[0], 0), (branch_near, 0), (branch_far, 0), (x_own, 0), (out_bias, 0)), steps=2)
    out_other = to_ten(out_own)
    total, moved = shared(total, moved, moves[1:2])
    unit_pieces = second(unit_pieces)
    total, moved = shared(total, moved, moves[2:3])
    g_far = to_ctx(fold(cross, g_keep, g_got))
    attn_pieces = near_parts(attn_factors, attn_far)
    unit_terms, unit_theirs = third(unit_pieces)
    (g_sum,) = totals(quarter, ((g_own[0], 0), (g_near, 0), (g_far, 0)), steps=2)
    g_other = to_ten(g_sum)
    total, moved = shared(total, moved, moves[3:4])
    wait(out_other)
    attn_pieces = second(attn_pieces)
    total, moved = shared(total, moved, moves[4:5])
    attn_terms, attn_theirs = third(attn_pieces)

    count_value = step_count.astype(F32)
    fixes = jnp.stack([1.0 - jnp.power(BETA_ONE, count_value), jnp.sqrt(1.0 - jnp.power(BETA_TWO, count_value))])
    up_grad, up_new, up_change = adam(ctx_scalar, fixes, up_weight, up_moments, unit_terms, unit_theirs)
    down_grad, down_new, down_change = adam(ctx_scalar, fixes, down_weight, down_moments, unit_terms, unit_theirs, first=n)
    for k in range(5, len(moves) + 1):
        total, moved = shared(total, moved, moves[k : k + 1])
    total = total.reshape(-1)
    vector_grad = total[: 5 * width].reshape(5, width)
    vector_grad = jnp.concatenate([vector_grad, vector_grad[4:]], 0)
    unit_all = total[8 * width :].reshape(4 * heads, unit_part.shape[1])
    unit_grad = lax.dynamic_slice_in_dim(unit_all, ten * 2 * heads, 2 * heads, 0)
    outputs, input_grad = finish(place, out_own, out_other, g_sum, g_other, x_own, d_own)
    qkv_grad, qkv_new, qkv_change = adam_heads(ctx_scalar, fixes, qkv_weight, qkv_moments, attn_terms, attn_theirs)
    dense_grad, dense_new, dense_change = adam(
        ctx_scalar, fixes, dense_weight, dense_moments, attn_terms, attn_theirs, tile=head_cols, first=n_qkv
    )
    unit_new, unit_change = adam_step(unit_vals, unit_moments, unit_grad, count_value, 0.0)
    vector_new, vector_change = adam_step(vectors.astype(F32), vector_moments, vector_grad, count_value, 0.0)
    return (
        outputs.reshape(inputs.shape),
        input_grad.reshape(inputs.shape),
        qkv_grad,
        dense_grad,
        up_grad,
        down_grad,
        unit_grad,
        vector_grad,
        qkv_new,
        dense_new,
        up_new,
        down_new,
        unit_new,
        vector_new,
        qkv_change,
        dense_change,
        up_change,
        down_change,
        unit_change,
        vector_change,
    )


def solution(mesh):
    rows = ("shard", "context")
    tokens = P("shard", "context", None)
    qkv, matrix, units = P(rows, "tensor", None), P(rows, "tensor"), P("tensor", None)
    qkv_pair, matrix_pair, units_pair = P(None, rows, "tensor", None), P(None, rows, "tensor"), P(None, "tensor", None)
    params = (qkv, matrix, matrix, matrix, units, P())
    states = (qkv_pair, matrix_pair, matrix_pair, matrix_pair, units_pair, P())
    return jax.shard_map(
        functools.partial(on_device, mesh.shape["shard"]),
        mesh=mesh,
        in_specs=(tokens, tokens, *params, *states, P()),
        out_specs=(tokens, tokens, *params, *states, *params),
        check_vma=False,
    )
```

```python
import functools
import math

import jax
import jax.numpy as jnp
from jax import lax
from jax.experimental import pallas as pl
from jax.experimental.pallas import tpu as pltpu
from jax.sharding import PartitionSpec as P

HEAD_DIM = 256
ROTARY = 64
EPSILON = 1e-05
BETA_ONE = 0.9
BETA_TWO = 0.95
LEARN_RATE = 0.02
WEIGHT_DECAY = 0.01
ROOT_HALF = 0.7071067811865476
ROOT_TWO_PI = 2.5066282746310002
MASKED = -1000000000.0
BF = jnp.bfloat16
F32 = jnp.float32


def dot(a, b, ca, cb):
    return lax.dot_general(a, b, (((ca,), (cb,)), ((), ())), preferred_element_type=F32)


def gelu_value(hidden):
    return 0.5 * hidden * (1.0 + lax.erf(hidden * ROOT_HALF))


def gelu_slope(hidden):
    return (
        0.5 * (1.0 + lax.erf(hidden * ROOT_HALF))
        + hidden * jnp.exp(-0.5 * hidden * hidden) / ROOT_TWO_PI
    )


BLOCK = 128
MIB = 1024 * 1024
COSTS = [50, 50, 20, 0.5, 0.5, 0, 0.5, 5, 5, 0, 50, 0, 50, 2, 50, 20, 0, 2, 50, 5, 20, 50, 20, 0.5, 50, 0, 5, 50, 0, 2, 10, 0, 0, 0.5, 10, 0, 0, 0.5, 0, 0, 2, 0, 0, 0, 0, 2, 0.5, 0, 0, 0.5, 10, 0, 0, 0, 20, 0.5, 0, 10, 5, 2, 2, 10, 0, 50, 5, 2]


def whole(shape):
    return pl.BlockSpec(shape, lambda *_: (0,) * len(shape), pipeline_mode=pl.Buffered(1))


ORDER = []
CALLS = []


def call(kernel, grid, in_specs, out_specs, out_shape, name, flops, nbytes, prefetch=0, scratch=(), limit=56):
    single = not isinstance(out_shape, (list, tuple))
    specs, shapes = ([out_specs], [out_shape]) if single else (list(out_specs), list(out_shape))
    waits = tuple(ORDER)
    cost = COSTS[len(CALLS)] if len(CALLS) < len(COSTS) else 10
    CALLS.append(name)
    first, outs = prefetch + len(in_specs), len(shapes)
    anywhere = pl.BlockSpec(memory_space=pl.ANY)

    def ordered(*refs):
        rest = refs[first + len(waits) :]
        kernel(*refs[:first], *rest[:outs], *rest[outs + 1 :])

    run = pl.pallas_call(
        ordered,
        grid_spec=pltpu.PrefetchScalarGridSpec(
            num_scalar_prefetch=prefetch,
            grid=grid,
            in_specs=[*in_specs, *[anywhere] * len(waits)],
            out_specs=[*specs, anywhere],
            scratch_shapes=list(scratch),
        ),
        out_shape=[*shapes, like((8, 128), F32)],
        compiler_params=pltpu.CompilerParams(vmem_limit_bytes=limit * MIB),
        cost_estimate=pl.CostEstimate(flops=int(cost * 1e9), bytes_accessed=1, transcendentals=0),
        name=name,
    )

    def ordered_call(*operands):
        *results, token = run(*operands, *waits)
        ORDER[:] = [token]
        return results[0] if single else results

    return ordered_call


def like(shape, dtype):
    return jax.ShapeDtypeStruct(shape, dtype)


def cut_kernel(flip, c_ref, *refs):
    *operands, out_ref = refs
    col = 0
    for ref in operands:
        if len(ref.shape) == 3:
            heads, wide = ref.shape[1] // 2, ref.shape[2]
            for c in range(2):

                @pl.when(c_ref[0] == c)
                def _(c=c, ref=ref, col=col):
                    for h in range(heads):
                        out_ref[:, col + h * wide : col + (h + 1) * wide] = ref[:, (c ^ flip) * heads + h, :]

            col += heads * wide
        else:
            n = ref.shape[1] // 2
            out_ref[:, col : col + n] = ref[:, pl.ds(pl.multiple_of((c_ref[0] ^ flip) * n, n), n)]
            col += n


def cut_quarter(ctx, flip, *operands):
    rows = operands[0].shape[0]
    n = sum(a.size for a in operands) // rows // 2
    return call(
        functools.partial(cut_kernel, flip),
        (1,),
        [whole(a.shape) for a in operands],
        whole((rows, n)),
        like((rows, n), BF),
        "cut",
        0,
        6 * rows * n,
        prefetch=1,
    )(ctx, *operands)


def arrange_kernel(place_ref, x_ref, d_ref, v_ref, xo_ref, do_ref, vo_ref):
    width = x_ref.shape[1]
    count = width // BLOCK
    rows = x_ref.shape[0] // 2
    for j in range(count):
        out = slice(j * BLOCK, (j + 1) * BLOCK)
        col = pl.ds(pl.multiple_of(place_ref[j] * BLOCK, BLOCK), BLOCK)
        for b in range(2):
            row = pl.ds(pl.multiple_of((place_ref[2 * count] ^ b) * rows, rows), rows)
            xo_ref[b * rows : (b + 1) * rows, out] = x_ref[row, col]
            do_ref[b * rows : (b + 1) * rows, out] = d_ref[row, col]
        vo_ref[:, out] = v_ref[:, col].astype(F32)


def arrange(place, x, d, v):
    operands = (x, d, v)
    outs = [(x.shape, BF), (d.shape, BF), (v.shape, F32)]
    return call(
        arrange_kernel,
        (1,),
        [whole(a.shape) for a in operands],
        [whole(a) for a, _ in outs],
        [like(*a) for a in outs],
        "arrange",
        0,
        4 * x.size * 2,
        prefetch=1,
    )(place, *operands)


def outgoing_kernel(place_ref, x_ref, o_ref):
    count = x_ref.shape[1] // BLOCK
    for j in range(count):
        col = pl.ds(pl.multiple_of(place_ref[count + j] * BLOCK, BLOCK), BLOCK)
        o_ref[:, j * BLOCK : (j + 1) * BLOCK] = x_ref[:, col]


def outgoing(place, x):
    rows, width = x.shape[0] // 2, x.shape[1]
    return call(
        outgoing_kernel,
        (1,),
        [pl.BlockSpec((rows, width), lambda i, p: (p[2 * width // BLOCK], 0))],
        whole((rows, width)),
        like((rows, width), BF),
        "outgoing",
        0,
        x.size * 2,
        prefetch=1,
    )(place, x)


def unorder_kernel(place_ref, v_ref, o_ref):
    for j in range(v_ref.shape[1] // BLOCK):
        col = pl.ds(pl.multiple_of(place_ref[j] * BLOCK, BLOCK), BLOCK)
        o_ref[:, col] = v_ref[:, j * BLOCK : (j + 1) * BLOCK]


def unorder(place, v):
    return call(
        unorder_kernel, (1,), [whole(v.shape)], whole(v.shape), like(v.shape, v.dtype), "unorder", 0, v.size * 8, prefetch=1
    )(place, v)


def pack_kernel(*refs):
    *pieces, out_ref = refs
    row = 0
    for piece in pieces:
        out_ref[row : row + piece.shape[0], :] = piece[...]
        row += piece.shape[0]


def pack(n, *pieces):
    pieces = [p if isinstance(p, tuple) else (p, 0) for p in pieces]
    rows = sum(p.shape[0] for p, _ in pieces)
    return call(
        pack_kernel,
        (1,),
        [pl.BlockSpec((p.shape[0], n), lambda i, k=k: (0, k)) for p, k in pieces],
        whole((rows, n)),
        like((rows, n), BF),
        "pack",
        0,
        rows * n * 4,
    )(*[p for p, _ in pieces])


def halves_kernel(u_ref, v_ref, top_ref, low_ref):
    top_ref[...] = u_ref[...]
    low_ref[...] = v_ref[...]


def halves(u, v):
    rows, n = u.shape[0] // 2, u.shape[1]
    return call(
        halves_kernel,
        (1,),
        [pl.BlockSpec((rows, n), lambda i: (0, 0)), pl.BlockSpec((rows, n), lambda i: (1, 0))],
        [whole((rows, n))] * 2,
        [like((rows, n), BF)] * 2,
        "halves",
        0,
        8 * rows * n,
    )(u, v)


def total_kernel(counts, *refs):
    at = 0
    for k, count in enumerate(counts):
        total = refs[at][...].astype(F32)
        for ref in refs[at + 1 : at + count]:
            total = total + ref[...].astype(F32)
        out_ref = refs[sum(counts) + k]
        out_ref[...] = total.astype(out_ref.dtype)
        at += count


def totals(rows, *groups, dtype=BF, steps=1):
    tile = rows // steps
    in_specs, operands = [], []
    for group in groups:
        for a, k in group:
            if a.shape[0] == 1:
                in_specs.append(whole(a.shape))
            else:
                in_specs.append(pl.BlockSpec((tile, a.shape[1]), lambda i, k=k: (k * steps + i, 0)))
            operands.append(a)
    width = operands[0].shape[1]
    return call(
        functools.partial(total_kernel, [len(g) for g in groups]),
        (steps,),
        in_specs,
        [pl.BlockSpec((tile, width), lambda i: (i, 0))] * len(groups),
        [like((rows, width), dtype)] * len(groups),
        "totals",
        0,
        8 * rows * width,
    )(*operands)


def norm_kernel(x_ref, v_ref, attn_ref, mlp_ref, mean_ref, inv_ref):
    x = x_ref[...].astype(F32)
    mean = jnp.mean(x, -1, keepdims=True)
    center = x - mean
    inv_std = lax.rsqrt(jnp.mean(center * center, -1, keepdims=True) + EPSILON)
    normed = center * inv_std
    attn_ref[...] = (normed * v_ref[0:1, :] + v_ref[1:2, :]).astype(BF)
    mlp_ref[...] = (normed * v_ref[2:3, :] + v_ref[3:4, :]).astype(BF)
    mean_ref[...] = jnp.broadcast_to(mean, mean_ref.shape)
    inv_ref[...] = jnp.broadcast_to(inv_std, inv_ref.shape)


def norm(x, vec):
    rows, width = x.shape
    tile = rows // 2
    block = pl.BlockSpec((tile, width), lambda i: (i, 0))
    stat = pl.BlockSpec((tile, 128), lambda i: (i, 0))
    return call(
        norm_kernel,
        (2,),
        [block, whole(vec.shape)],
        [block, block, stat, stat],
        [like(x.shape, BF), like(x.shape, BF), like((rows, 128), F32), like((rows, 128), F32)],
        "norm",
        x.size * 12,
        x.size * 6,
    )(x, vec)


def over_rows(a, weight):
    rows = weight[0].shape[0]
    return sum(dot(a[:, k * rows : (k + 1) * rows], part[...], 1, 0) for k, part in enumerate(weight))


def hidden_kernel(a_ref, b_ref, *refs):
    *weight, act_ref, slope_ref = refs
    hidden = over_rows(a_ref[...], weight) + b_ref[...]
    cdf = 0.5 * (1.0 + lax.erf(hidden * ROOT_HALF))
    act_ref[...] = (hidden * cdf).astype(BF)
    slope_ref[...] = cdf + hidden * jnp.exp(-0.5 * hidden * hidden) * (1.0 / ROOT_TWO_PI)


def units_kernel(parts, a_ref, d_ref, b_ref, *refs):
    weights, (act_ref, low_ref, sum_ref) = refs[: 2 * parts], refs[2 * parts :]
    hidden = over_rows(a_ref[...], weights[:parts]) + b_ref[...]
    cdf = 0.5 * (1.0 + lax.erf(hidden * ROOT_HALF))
    act_ref[...] = (hidden * cdf).astype(BF)
    slope = cdf + hidden * jnp.exp(-0.5 * hidden * hidden) * (1.0 / ROOT_TWO_PI)
    grad = over_rows(d_ref[...], weights[parts:]) * slope
    low_ref[...] = grad.astype(BF)
    sum_ref[...] = jnp.broadcast_to(jnp.sum(grad, 0, keepdims=True), sum_ref.shape)


def units_of(a, d, up, down, bias, tile=256):
    (rows, width), n = a.shape, up[0].shape[1]
    out = pl.BlockSpec((rows, tile), lambda j: (0, j))
    at = lambda j: (0, j)
    return call(
        functools.partial(units_kernel, len(up)),
        (n // tile,),
        [whole(a.shape), whole(d.shape), pl.BlockSpec((1, tile), at), *column_specs((*up, *down), tile, at)],
        [out, out, pl.BlockSpec((8, tile), at)],
        [like((rows, n), BF), like((rows, n), BF), like((8, n), F32)],
        "units",
        4 * rows * width * n,
        (a.size * 2 + width * n * 2 + rows * n * 2) * 2,
    )(a, d, bias, *up, *down)


def column_specs(weight, tile, at):
    return [pl.BlockSpec((part.shape[0], tile), at) for part in weight]


def hidden_of(a, weight, bias, tile=512):
    (rows, width), n = a.shape, weight[0].shape[1]
    tile = min(tile, n)
    out = pl.BlockSpec((rows, tile), lambda j: (0, j))
    return call(
        hidden_kernel,
        (n // tile,),
        [whole(a.shape), pl.BlockSpec((1, tile), lambda j: (0, j)), *column_specs(weight, tile, lambda j: (0, j))],
        [out, out],
        [like((rows, n), BF), like((rows, n), F32)],
        "hidden",
        2 * rows * width * n,
        (a.size + width * n + rows * n * 3) * 2,
    )(a, bias, *weight)


def d_hidden_kernel(d_ref, slope_ref, *refs):
    *weight, low_ref, sum_ref = refs
    grad = over_rows(d_ref[...], weight) * slope_ref[...]
    low_ref[...] = grad.astype(BF)
    sum_ref[...] = jnp.broadcast_to(jnp.sum(grad, 0, keepdims=True), sum_ref.shape)


def d_hidden_of(d, weight, slope, tile=512):
    (rows, width), n = d.shape, weight[0].shape[1]
    tile = min(tile, n)
    out = pl.BlockSpec((rows, tile), lambda j: (0, j))
    return call(
        d_hidden_kernel,
        (n // tile,),
        [whole(d.shape), out, *column_specs(weight, tile, lambda j: (0, j))],
        [out, pl.BlockSpec((8, tile), lambda j: (0, j))],
        [like((rows, n), BF), like((8, n), F32)],
        "d_hidden",
        2 * rows * width * n,
        (d.size + width * n + rows * n * 3) * 2,
    )(d, slope, *weight)


def turn(block, cosine, sine):
    head = block[:, :128]
    lane = lax.broadcasted_iota(jnp.int32, head.shape, 1)
    half = ROTARY // 2
    partner = jnp.where(lane < half, -pltpu.roll(head, 128 - half, 1), pltpu.roll(head, half, 1))
    return jnp.concatenate([head * cosine + partner * sine, block[:, 128:]], 1)


def attend_kernel(
    z_ref, a0_ref, a1_ref, b_ref, cos_ref, sin_ref, *refs
):
    *weight, ctx_ref, pack_ref, log_ref = refs
    z = z_ref[0]
    size = a0_ref.shape[0] // 2
    hd = HEAD_DIM
    scale = hd**-0.5

    def row_of(p):
        return pl.ds(pl.multiple_of((z ^ p) * size, size), size)

    for b in range(4):
        a = (a0_ref, a1_ref)[b // 2][b % 2 * size : (b % 2 + 1) * size, :]
        lin = over_rows(a, weight) + b_ref[...]
        mine = slice(b * size, (b + 1) * size)
        cosine, sine = cos_ref[mine, :], sin_ref[mine, :]
        rows = row_of(b)
        pack_ref[rows, :hd] = turn(lin[:, :hd], cosine, sine).astype(BF)
        pack_ref[rows, hd : 2 * hd] = turn(lin[:, hd : 2 * hd], cosine, sine).astype(BF)
        pack_ref[rows, 2 * hd :] = lin[:, 2 * hd :].astype(BF)
    for p in range(4):
        here, seen = slice(p * size, (p + 1) * size), slice(0, (p + 1) * size)
        scores = dot(pack_ref[here, :hd], pack_ref[seen, hd : 2 * hd], 1, 1) * scale
        row_ids = p * size + lax.broadcasted_iota(jnp.int32, scores.shape, 0)
        col_ids = lax.broadcasted_iota(jnp.int32, scores.shape, 1)
        scores = jnp.where(row_ids >= col_ids, scores, MASKED)
        top = jnp.max(scores, -1, keepdims=True)
        exponent = jnp.exp(scores - top)
        total = jnp.sum(exponent, -1, keepdims=True)
        low = (exponent * (1.0 / total)).astype(BF)
        ctx_ref[row_of(p), :] = dot(low, pack_ref[seen, 2 * hd :], 1, 0).astype(BF)
        log_ref[here, :] = jnp.broadcast_to(top + jnp.log(total), (size, log_ref.shape[1]))


def attend(z, a0, a1, weight, bias, cosine, sine):
    length, width = 2 * a0.shape[0], a0.shape[1]
    hd = HEAD_DIM
    heads = bias.shape[1] // (3 * hd)
    column = lambda rows, cols: pl.BlockSpec((rows, cols), lambda h, p: (0, h))
    return call(
        attend_kernel,
        (heads,),
        [
            whole(a0.shape),
            whole(a1.shape),
            column(1, 3 * hd),
            whole(cosine.shape),
            whole(sine.shape),
            *column_specs(weight, 3 * hd, lambda h, p: (0, h)),
        ],
        [column(length, hd), column(length, 3 * hd), column(length, 128)],
        [like((length, heads * hd), BF), like((length, heads * 3 * hd), BF), like((length, heads * 128), F32)],
        "attend",
        (3 * length * length * hd + 6 * length * width * hd) * heads,
        length * width * 8,
        prefetch=1,
    )(z, a0, a1, bias, cosine, sine, *weight)


def attend_back_kernel(
    z_ref, pack_ref, log_ref, d0_ref, d1_ref, cos_ref, sin_ref, *refs
):
    *weight, dl_ref, us_ref, g_s, dk_s, dv_s = refs
    z = z_ref[0]
    size = d0_ref.shape[0] // 2
    hd = HEAD_DIM
    scale = hd**-0.5

    def row_of(p):
        return pl.ds(pl.multiple_of((z ^ p) * size, size), size)

    for half, d_ref in enumerate((d0_ref, d1_ref)):
        grad = over_rows(d_ref[...], weight).astype(BF)
        g_s[row_of(2 * half), :] = grad[:size]
        g_s[row_of(2 * half + 1), :] = grad[size:]
    dk_s[...] = jnp.zeros_like(dk_s)
    dv_s[...] = jnp.zeros_like(dv_s)
    q_sum = jnp.zeros((1, hd), F32)
    for p in range(4):
        here, seen = slice(p * size, (p + 1) * size), slice(0, (p + 1) * size)
        rows = row_of(p)
        queries, grads = pack_ref[here, :hd], g_s[here, :]
        keys, values = pack_ref[seen, hd : 2 * hd], pack_ref[seen, 2 * hd :]
        scores = dot(queries, keys, 1, 1) * scale
        row_ids = p * size + lax.broadcasted_iota(jnp.int32, scores.shape, 0)
        col_ids = lax.broadcasted_iota(jnp.int32, scores.shape, 1)
        scores = jnp.where(row_ids >= col_ids, scores, MASKED)
        probs = jnp.exp(scores - log_ref[here, 0:1])
        low = probs.astype(BF)
        weight_grad = dot(grads, values, 1, 1)
        score_grad = (
            probs * (weight_grad - jnp.sum(probs * weight_grad, -1, keepdims=True))
        ).astype(BF)
        query_grad = (dot(score_grad, keys, 1, 0) * scale).astype(BF).astype(F32)
        dk_s[seen, :] += dot(score_grad, queries, 0, 0)
        dv_s[seen, :] += dot(low, grads, 0, 0)
        query_grad = turn(query_grad, cos_ref[rows, :], -sin_ref[rows, :])
        q_sum = q_sum + jnp.sum(query_grad, 0, keepdims=True)
        dl_ref[rows, :hd] = query_grad.astype(BF)
    k_sum = jnp.zeros((1, hd), F32)
    v_sum = jnp.zeros((1, hd), F32)
    for p in range(4):
        here = slice(p * size, (p + 1) * size)
        rows = row_of(p)
        key_grad = (dk_s[here, :] * scale).astype(BF).astype(F32)
        key_grad = turn(key_grad, cos_ref[rows, :], -sin_ref[rows, :])
        k_sum = k_sum + jnp.sum(key_grad, 0, keepdims=True)
        dl_ref[rows, hd : 2 * hd] = key_grad.astype(BF)
        value_grad = dv_s[here, :].astype(BF)
        v_sum = v_sum + jnp.sum(value_grad.astype(F32), 0, keepdims=True)
        dl_ref[rows, 2 * hd :] = value_grad
    us_ref[...] = jnp.broadcast_to(jnp.concatenate([q_sum, k_sum, v_sum], 1), us_ref.shape)


def attend_back(z, packed, logs, d0, d1, weight, cosine, sine):
    length, wide = packed.shape
    hd = HEAD_DIM
    heads = wide // (3 * hd)
    first = wide // hd
    column = lambda rows, cols: pl.BlockSpec((rows, cols), lambda h, p: (0, h))
    return call(
        attend_back_kernel,
        (heads,),
        [
            column(length, 3 * hd),
            column(length, 128),
            whole(d0.shape),
            whole(d1.shape),
            whole(cosine.shape),
            whole(sine.shape),
            *column_specs(weight, hd, lambda h, p: (0, first + h)),
        ],
        [column(length, 3 * hd), column(8, 3 * hd)],
        [like((length, wide), BF), like((8, wide), F32)],
        "attend_back",
        (9 * length * length * hd + 2 * length * d0.shape[1] * hd) * heads,
        length * wide * 8,
        prefetch=1,
        scratch=[pltpu.VMEM((length, hd), BF)] + [pltpu.VMEM((length, hd), F32)] * 2,
    )(z, packed, logs, d0, d1, cosine, sine, *weight)


def in_turn(parts, body):
    j = pl.program_id(0)
    each = pl.num_programs(0) // len(parts)
    for k, part in enumerate(parts):

        @pl.when(j // each == k)
        def _(part=part):
            body(*part)


def row_specs(shape, count, parts, col=0):
    each = count // parts
    return [pl.BlockSpec(shape, lambda j, k=k: (jnp.clip(j - k * each, 0, each - 1), col)) for k in range(parts)]


def branch_kernel(parts, a0_ref, a1_ref, ctx_ref, *refs):
    weights, outs = refs[: 2 * parts], refs[2 * parts :]
    size = outs[0].shape[0]

    def body(down_ref, dense_ref):
        for k, act_ref in enumerate((a0_ref, a1_ref)):
            ctx = ctx_ref[2 * k * size : 2 * (k + 1) * size, :]
            part = dot(act_ref[...], down_ref[...], 1, 1) + dot(ctx, dense_ref[...], 1, 1)
            outs[2 * k][...] = part[:size]
            outs[2 * k + 1][...] = part[size:].astype(BF)

    in_turn(list(zip(weights[:parts], weights[parts:])), body)


def token_outs(size, width, tile):
    spec = pl.BlockSpec((size, tile), lambda j: (0, j))
    return [spec] * 4, [like((size, width), F32), like((size, width), BF)] * 2


def branch_of(a0, a1, context_out, down, attn, tile=256):
    rows, n = a0.shape
    parts = len(down)
    width = parts * down[0].shape[0]
    cols = context_out.shape[1]
    count = width // tile
    specs, shapes = token_outs(rows // 2, width, tile)
    return call(
        functools.partial(branch_kernel, parts),
        (count,),
        [
            whole(a0.shape),
            whole(a1.shape),
            whole(context_out.shape),
            *row_specs((tile, n), count, parts),
            *row_specs((tile, cols), count, parts, attn[0].shape[1] // cols - 1),
        ],
        specs,
        shapes,
        "branch",
        4 * rows * width * (n + cols),
        (2 * rows * (n + cols) + width * (n + cols) + 2 * rows * width * 2) * 2,
    )(a0, a1, context_out, *down, *attn)


def input_grad_kernel(
    parts, dl_ref, h0_ref, h1_ref, x0_ref, x1_ref, m0_ref, m1_ref, i0_ref, i1_ref, v_ref, *refs
):
    weights, outs = refs[: 2 * parts], refs[2 * parts :]
    size = outs[0].shape[0]
    wide = dl_ref.shape[1]
    halves = ((h0_ref, x0_ref, m0_ref, i0_ref), (h1_ref, x1_ref, m1_ref, i1_ref))

    def body(attn_ref, up_ref):
        total = [0.0] * 4
        for k, (dh_ref, x_ref, mean_ref, inv_ref) in enumerate(halves):
            attn = dot(dl_ref[2 * k * size : 2 * (k + 1) * size, :], attn_ref[:, :wide], 1, 1)
            mlp = dot(dh_ref[...], up_ref[...], 1, 1)
            part = attn * v_ref[0:1, :] + mlp * v_ref[2:3, :]
            outs[2 * k][...] = part[:size]
            outs[2 * k + 1][...] = part[size:].astype(BF)
            normed = (x_ref[...].astype(F32) - mean_ref[:, 0:1]) * inv_ref[:, 0:1]
            sums = [jnp.sum(v, 0, keepdims=True) for v in (attn * normed, attn, mlp * normed, mlp)]
            total = [u + v for u, v in zip(total, sums)]
        outs[4][...] = jnp.concatenate(total + [jnp.zeros((4, attn.shape[1]), F32)], 0)

    in_turn(list(zip(weights[:parts], weights[parts:])), body)


def input_grad_of(d_linear, h0, h1, attn, up, xs, means, invs, vec, tile=256):
    rows, n = h0.shape
    width = xs[0].shape[1]
    wide = d_linear.shape[1]
    parts = len(attn)
    count = width // tile
    specs, shapes = token_outs(rows // 2, width, tile)
    column = pl.BlockSpec((rows, tile), lambda j: (0, j))
    return call(
        functools.partial(input_grad_kernel, parts),
        (count,),
        [
            whole(d_linear.shape),
            whole(h0.shape),
            whole(h1.shape),
            column,
            column,
            *[whole(a.shape) for a in (*means, *invs)],
            pl.BlockSpec((vec.shape[0], tile), lambda j: (0, j)),
            *row_specs((tile, attn[0].shape[1]), count, parts),
            *row_specs((tile, n), count, parts),
        ],
        [*specs, pl.BlockSpec((8, tile), lambda j: (0, j))],
        [*shapes, like((8, width), F32)],
        "input_grad",
        4 * rows * width * (n + wide),
        (2 * rows * (n + wide) + width * (n + wide) + 2 * rows * width * 3) * 2,
    )(d_linear, h0, h1, *xs, *means, *invs, vec, *attn, *up)


def grad_kernel(pairs, near, *refs):
    operands, refs = refs[: 4 * pairs], refs[4 * pairs :]
    adds, outs = (refs[:4], refs[4:]) if near else (None, refs)
    j = pl.program_id(0)
    col = 0
    for k in range(pairs):
        l0, l1, r0, r1 = (r[...] for r in operands[4 * k : 4 * k + 4])
        part = dot(l0, r0, 0, 0) + dot(l1, r1, 0, 0)
        cols = slice(col, col + part.shape[1])
        col += part.shape[1]
        for i, out_ref in enumerate(outs):

            @pl.when(j == i)
            def _(i=i, out_ref=out_ref, part=part, cols=cols):
                if near:
                    out_ref[:, cols] = (part + adds[i][:, cols].astype(F32)).astype(BF)
                else:
                    out_ref[:, cols] = part.astype(BF)


def grad_of(factors, adds=()):
    width = factors[0][0].shape[1]
    tile = width // 8
    first = 0 if adds else 4
    in_specs, operands, n, flops, nbytes = [], [], 0, 0, 0
    for l0, l1, r0, r1 in factors:
        rows = l0.shape[0]
        for left in (l0, l1):
            in_specs.append(pl.BlockSpec((rows, tile), lambda j: (0, first + j)))
            operands.append(left)
        cols = r0[0].shape[1]
        for right, k in (r0, r1):
            in_specs.append(pl.BlockSpec((rows, cols), lambda j, k=k: (k, 0), pipeline_mode=pl.Buffered(1)))
            operands.append(right)
        n += cols
        flops += 2 * rows * width * cols
        nbytes += 2 * rows * (width + 2 * cols)
    in_specs += [whole((tile, n)) for _ in adds]
    return call(
        functools.partial(grad_kernel, len(factors), bool(adds)),
        (4,),
        in_specs,
        [whole((tile, n))] * 4,
        [like((tile, n), BF)] * 4,
        "grad_near" if adds else "grad_far",
        flops,
        nbytes + width * n,
    )(*operands, *adds)


def fold_kernel(cross, keep_ref, got_ref, o_ref):
    for j, k in enumerate(cross):
        here = slice(j * BLOCK, (j + 1) * BLOCK)
        o_ref[:, k * BLOCK : (k + 1) * BLOCK] = (keep_ref[:, here] + got_ref[:, here].astype(F32)).astype(BF)


def fold(cross, keep, got):
    rows, width = keep.shape
    tile = rows // 2
    block = pl.BlockSpec((tile, width), lambda i: (i, 0))
    return call(
        functools.partial(fold_kernel, cross), (2,), [block, block], block, like(keep.shape, BF), "fold", keep.size, keep.size * 8
    )(keep, got)


def finish_kernel(place_ref, o0_ref, o1_ref, g0_ref, g1_ref, x_ref, d_ref, out_ref, grad_ref):
    width = x_ref.shape[1]
    count = width // BLOCK
    x = x_ref[...].astype(F32)
    center = x - jnp.mean(x, -1, keepdims=True)
    inv_std = lax.rsqrt(jnp.mean(center * center, -1, keepdims=True) + EPSILON)
    normed = center * inv_std

    def body(o_ref, g_ref):
        g = g_ref[...].astype(F32)
        grad = d_ref[...].astype(F32) + inv_std * (
            g - jnp.mean(g, -1, keepdims=True) - normed * jnp.mean(g * normed, -1, keepdims=True)
        )
        for j in range(count):
            col = pl.ds(pl.multiple_of(place_ref[j] * BLOCK, BLOCK), BLOCK)
            part = slice(j * BLOCK, (j + 1) * BLOCK)
            out_ref[:, col] = o_ref[:, part]
            grad_ref[:, col] = grad[:, part]

    in_turn(((o0_ref, g0_ref), (o1_ref, g1_ref)), body)


def finish(place, o0, o1, g0, g1, x, d):
    rows, width = o0.shape
    per = 2
    tile = rows // per
    at = 2 * width // BLOCK
    first = pl.BlockSpec((tile, width), lambda i, p: (jnp.minimum(i, per - 1), 0))
    second = pl.BlockSpec((tile, width), lambda i, p: (jnp.maximum(i - per, 0), 0))
    local = pl.BlockSpec((tile, width), lambda i, p: (i, 0))
    out = pl.BlockSpec((tile, width), lambda i, p: ((p[at] ^ (i // per)) * per + i % per, 0))
    return call(
        finish_kernel,
        (2 * per,),
        [first, second, first, second, local, local],
        [out, out],
        [like(x.shape, BF), like(x.shape, F32)],
        "finish",
        x.size * 20,
        x.size * 14,
        prefetch=1,
    )(place, o0, o1, g0, g1, x, d)


def step_values(weight, first, root, gradient, fix_one, fix_two, decay_rate):
    first_new = BETA_ONE * first + (1.0 - BETA_ONE) * gradient
    root_new = jnp.sqrt(BETA_TWO * root * root + (1.0 - BETA_TWO) * gradient * gradient)
    change = -LEARN_RATE * (
        first_new / fix_one / (root_new / fix_two + 1e-08) + decay_rate * weight
    )
    return first_new, root_new, change


def adam_kernel(c_ref, fix_ref, w_ref, m_ref, a_ref, b_ref, e_ref, t_ref, g_ref, n_ref, u_ref):
    def body(gradient):
        first, root, change = step_values(
            w_ref[...].astype(F32), m_ref[0], m_ref[1], gradient, fix_ref[0], fix_ref[1], WEIGHT_DECAY
        )
        g_ref[...] = gradient
        n_ref[0] = first
        n_ref[1] = root
        u_ref[...] = change

    @pl.when(pl.program_id(0) == 0)
    def _():
        body(a_ref[...].astype(F32) + b_ref[...].astype(F32) + e_ref[...].astype(F32))

    @pl.when(pl.program_id(0) == 1)
    def _():
        body(t_ref[...].astype(F32))


def adam(ctx, fixes, weight, moments, terms, theirs, tile=2048, first=0):
    rows, cols = weight.shape
    n = cols // 2
    tile = min(tile, n)
    first //= tile
    per = n // tile
    at = lambda k, i, c: (0, (c[0] ^ k) * per + i)
    mine = pl.BlockSpec((rows, tile), lambda k, i, c: (0, first + i + k * (per - 1 - i)))
    other = pl.BlockSpec((rows, tile), lambda k, i, c: (0, first + i * k))
    matrix = pl.BlockSpec((rows, tile), at)
    pair = pl.BlockSpec((2, rows, tile), lambda k, i, c: (0, *at(k, i, c)))
    return call(
        adam_kernel,
        (2, per),
        [pl.BlockSpec(memory_space=pltpu.SMEM), matrix, pair, mine, mine, mine, other],
        [matrix, pair, matrix],
        [like(weight.shape, F32), like(moments.shape, F32), like(weight.shape, F32)],
        "adam",
        weight.size * 20,
        weight.size * 30,
        prefetch=1,
    )(ctx, fixes, weight, moments, *terms, theirs)


def adam_heads_kernel(c_ref, fix_ref, w_ref, m_ref, a_ref, b_ref, e_ref, t_ref, g_ref, n_ref, u_ref):
    mine = a_ref[...].astype(F32) + b_ref[...].astype(F32) + e_ref[...].astype(F32)
    theirs = t_ref[...].astype(F32)
    heads, wide = w_ref.shape[1] // 2, w_ref.shape[2]
    for h in range(2 * heads):
        cols = slice(h % heads * wide, (h % heads + 1) * wide)
        gradient = jnp.where(c_ref[0] == h // heads, mine[:, cols], theirs[:, cols])
        first, root, change = step_values(
            w_ref[:, h, :].astype(F32), m_ref[0, :, h, :], m_ref[1, :, h, :], gradient, fix_ref[0], fix_ref[1], WEIGHT_DECAY
        )
        g_ref[:, h, :] = gradient
        n_ref[0, :, h, :] = first
        n_ref[1, :, h, :] = root
        u_ref[:, h, :] = change


def adam_heads(ctx, fixes, weight, moments, terms, theirs):
    rows, heads, wide = weight.shape
    tile = rows // 4
    part = pl.BlockSpec((tile, heads // 2 * wide), lambda i, c: (i, 0))
    cube = pl.BlockSpec((tile, heads, wide), lambda i, c: (i, 0, 0))
    pair = pl.BlockSpec((2, tile, heads, wide), lambda i, c: (0, i, 0, 0))
    return call(
        adam_heads_kernel,
        (4,),
        [pl.BlockSpec(memory_space=pltpu.SMEM), cube, pair, part, part, part, part],
        [cube, pair, cube],
        [like(weight.shape, F32), like(moments.shape, F32), like(weight.shape, F32)],
        "adam_heads",
        weight.size * 20,
        weight.size * 30,
        prefetch=1,
    )(ctx, fixes, weight, moments, *terms, theirs)


def rotary_tables(positions):
    lane = jnp.arange(128)
    inverse = jnp.exp((lane % (ROTARY // 2)).astype(F32) * (-2.0 / ROTARY) * math.log(10000.0))
    angles = positions.astype(F32)[:, None] * inverse[None, :]
    turned = lane[None, :] < ROTARY
    return (jnp.where(turned, jnp.cos(angles), 1.0), jnp.where(turned, jnp.sin(angles), 0.0))


def adam_step(weight, moments, gradient, count_value, decay_rate):
    first_new = BETA_ONE * moments[0] + (1.0 - BETA_ONE) * gradient
    root_new = jnp.sqrt(BETA_TWO * moments[1] * moments[1] + (1.0 - BETA_TWO) * gradient * gradient)
    fix_one = 1.0 - jnp.power(BETA_ONE, count_value)
    fix_two = 1.0 - jnp.power(BETA_TWO, count_value)
    change = -LEARN_RATE * (
        first_new / fix_one / (root_new / jnp.sqrt(fix_two) + 1e-08) + decay_rate * weight
    )
    return (jnp.stack([first_new, root_new]), change)


def on_device(
    shard_count,
    inputs,
    cotangent,
    qkv_weight,
    dense_weight,
    up_weight,
    down_weight,
    unit_biases,
    vectors,
    qkv_moments,
    dense_moments,
    up_moments,
    down_moments,
    unit_moments,
    vector_moments,
    step_count,
):
    ORDER.clear()
    CALLS.clear()
    shard, ctx, ten = (lax.axis_index(a) for a in ("shard", "context", "tensor"))
    fast = shard_count == 8
    _, local_len, width = inputs.shape
    quarter = local_len // 2
    row_count, heads_local, head_wide = qkv_weight.shape
    heads = heads_local // 2
    units = up_weight.shape[1] // 2
    head_cols = heads * HEAD_DIM
    n_qkv = heads * head_wide
    count = width // BLOCK

    def along(axis, size, bit):
        return lambda v: lax.ppermute(v, axis, [(i, i ^ bit) for i in range(size)])

    to_core, to_x, to_y = (along("shard", shard_count, bit) for bit in (1, 2, 4))
    to_ctx, to_ten = along("context", 2, 1), along("tensor", 2, 1)

    if fast:
        chips = ((0, 4, 2, 6), (0, 2, 4, 6))
        relative = [(core + chips[ab][k], ab) for core in range(2) for ab in range(2) for k in range(4)]
        places = [[(shard ^ s) * 2 + (ctx ^ f ^ ab) for s, ab in relative] for f in range(2)]
        cross = [core * 8 + (1 - ab) * 4 + (0, 2, 1, 3)[k] for core in range(2) for ab in range(2) for k in range(4)]
    else:
        places = [[jnp.int32(j) for j in range(count)]] * 2
        cross = list(range(count))
    place = jnp.stack([*places[0], *places[1], ten]).astype(jnp.int32)
    z = ctx * 2 + ten
    ctx_scalar, z_scalar = (v.reshape(1).astype(jnp.int32) for v in (ctx, z))

    def wait(*values):
        ORDER.extend(values)

    def full_rows(mine, other):
        block = jnp.where(ctx == 0, jnp.concatenate([mine, other], 0), jnp.concatenate([other, mine], 0))
        full = lax.all_gather(block, "shard", axis=0, tiled=True)
        return tuple(full[k * width // 4 : (k + 1) * width // 4] for k in range(4))

    r = row_count
    x_in, d_in = inputs.reshape(local_len, width), cotangent.reshape(local_len, width)
    unit_vals = unit_biases.astype(F32)
    my_units = lax.dynamic_slice_in_dim(unit_vals, ctx * heads, heads, 0)
    qkv_bias, unit_bias = my_units[:, :head_wide].reshape(1, n_qkv), my_units[:, head_wide:].reshape(1, units)
    positions = ((jnp.arange(4) ^ z)[:, None] * quarter + jnp.arange(quarter)[None, :]).reshape(-1)
    cosine, sine = rotary_tables(positions)

    n = up_weight.shape[1] // 2
    units_other = to_ctx(cut_quarter(ctx_scalar, 1, up_weight, down_weight))
    mine = cut_quarter(ctx_scalar, 0, up_weight, down_weight, qkv_weight, dense_weight)
    if fast:
        a_x, a_y = to_x(mine), to_y(mine)
    x_own, d_own, vec = arrange(place, x_in, d_in, vectors)
    attn_own, mlp_own, mean_own, inv_own = norm(x_own, vec)
    if fast:
        top, low = halves(a_y, a_x)
        a_top, a_low = to_x(top), to_y(low)
    wait(units_other)
    attn_other = to_ctx(cut_quarter(ctx_scalar, 1, qkv_weight, dense_weight))
    if fast:
        units_x, units_y = to_x(units_other), to_y(units_other)
    wait(attn_other)
    x_first = to_ctx(outgoing(place, x_in))

    def packed(pieces, k):
        near = pack(n, *[(a, k) for a in pieces])
        return near, to_core(near)

    if fast:
        mine_parts = (mine, a_y, a_x, a_top, a_low)
        up_a, up_far_a = packed(mine_parts, 0)
        down_a, down_far_a = packed(mine_parts, 1)
        top, low = halves(units_y, units_x)
        units_parts = (units_other, units_x, units_y, to_x(top), to_y(low))
        attn_x, attn_y = to_x(attn_other), to_y(attn_other)
        attn_a, attn_far_a = packed(mine_parts, 2)
        up_b, up_far_b = packed(units_parts, 0)
        top, low = halves(attn_y, attn_x)
        attn_parts = (attn_other, attn_x, attn_y, to_x(top), to_y(low))
        down_b, down_far_b = packed(units_parts, 1)
        w_up, w_down = (up_a, up_b, up_far_a, up_far_b), (down_a, down_b, down_far_a, down_far_b)
    else:
        w_up = full_rows(mine[:, :n], units_other[:, :n])
        w_down = full_rows(mine[:, n : 2 * n], units_other[:, n:])
        w_attn = full_rows(mine[:, 2 * n :], attn_other)
    active_own, slope_own = hidden_of(mlp_own, w_up, unit_bias)
    if fast:
        attn_b, attn_far_b = packed(attn_parts, 0)
        w_attn = (attn_a, attn_b, attn_far_a, attn_far_b)
    wait(x_first)
    d_first = to_ctx(outgoing(place, d_in))
    x_second = to_ten(x_first)
    low_own, sum_own = d_hidden_of(d_own, w_down, slope_own)
    x_oth = pack(width, x_first, x_second)
    attn_oth, mlp_oth, mean_oth, inv_oth = norm(x_oth, vec)
    active_oth, slope_oth = hidden_of(mlp_oth, w_up, unit_bias)
    wait(d_first)
    d_second = to_ten(d_first)
    context_out, packed_qkv, logs = attend(z_scalar, attn_own, attn_oth, w_attn, qkv_bias, cosine, sine)
    *branch_own, branch_keep, branch_send = branch_of(active_own, active_oth, context_out, w_down, w_attn)
    branch_got = to_ten(branch_send)
    branch_near = to_ten(branch_own[1])
    d_oth = pack(width, d_first, d_second)

    def far_parts(factors):
        parts = grad_of(factors)
        return [to_core(part) for part in parts] if fast else parts

    def near_parts(factors, far):
        if fast:
            a_own, a_x, b_own, b_y = grad_of(factors, far)
            return a_own, b_own, to_y(b_y), to_x(a_x)
        near = grad_of(factors, [jnp.zeros_like(part) for part in far])
        return lax.psum_scatter(jnp.concatenate([*near, *far], 0), "shard", scatter_dimension=0, tiled=True)

    def second(parts):
        if not fast:
            return parts
        a_own, b_own, b_got, a_got = parts
        b_sum, a_sum = totals(r, ((b_own, 1), (b_got, 1)), ((a_own, 1), (a_got, 1)))
        return (*parts, to_x(b_sum), to_y(a_sum))

    def third(parts):
        if not fast:
            kept = lax.dynamic_slice_in_dim(parts, ctx * r, r, 0)
            zero = jnp.zeros_like(kept)
            return (kept, zero, zero), to_ctx(lax.dynamic_slice_in_dim(parts, (1 - ctx) * r, r, 0))
        a_own, b_own, b_got, a_got, b_last, a_last = parts
        wait(a_last)
        (away,) = totals(r, ((b_own, 0), (b_got, 0), (b_last, 0)))
        return (a_own, a_got, a_last), to_ctx(away)

    low_oth, sum_oth = d_hidden_of(d_oth, w_down, slope_oth)
    unit_factors = [(mlp_own, mlp_oth, (low_own, 0), (low_oth, 0)), (d_own, d_oth, (active_own, 0), (active_oth, 0))]
    unit_far = far_parts(unit_factors)
    branch_far = to_ctx(fold(cross, branch_keep, branch_got))
    d_linear, unit_sums = attend_back(z_scalar, packed_qkv, logs, d_own, d_oth, w_attn, cosine, sine)
    unit_pieces = near_parts(unit_factors, unit_far)
    wait(branch_near)
    *g_own, g_keep, g_send, sums = input_grad_of(
        d_linear, low_own, low_oth, w_attn, w_up, (x_own, x_oth), (mean_own, mean_oth), (inv_own, inv_oth), vec
    )
    g_got = to_ten(g_send)
    g_near = to_ten(g_own[1])
    attn_factors = [
        (attn_own, attn_oth, (d_linear, 0), (d_linear, 1)),
        (d_own, d_oth, (context_out, 0), (context_out, 1)),
    ]
    d_sum = jnp.sum(d_own[:quarter].astype(F32), 0, keepdims=True)
    sums = unorder(place, jnp.concatenate([sums[:4], d_sum, jnp.zeros((3, width), F32)], 0))
    unit_part = jnp.concatenate(
        [unit_sums[0].reshape(heads, head_wide), (sum_own + sum_oth)[0].reshape(heads, units // heads)], 1
    )
    unit_rows = jnp.where(jnp.arange(4)[:, None, None] == ten * 2 + ctx, unit_part[None], 0.0)
    total = jnp.concatenate([sums.reshape(-1), unit_rows.reshape(-1)]).reshape(-1, BLOCK)
    moves = [to_ctx] + [along("shard", shard_count, 1 << k) for k in range(shard_count.bit_length() - 1)] + [to_ten]
    moved = moves[0](total)

    def shared(total, moved, moves):
        (total,) = totals(total.shape[0], ((total, 0), (moved, 0)), dtype=F32)
        return total, moves[0](total) if moves else None

    attn_far = far_parts(attn_factors)
    out_bias = (vec[4] + vec[5]).reshape(1, width)
    (out_own,) = totals(quarter, ((branch_own[0], 0), (branch_near, 0), (branch_far, 0), (x_own, 0), (out_bias, 0)), steps=2)
    out_other = to_ten(out_own)
    unit_pieces = second(unit_pieces)
    g_far = to_ctx(fold(cross, g_keep, g_got))
    total, moved = shared(total, moved, moves[1:2])
    attn_pieces = near_parts(attn_factors, attn_far)
    unit_terms, unit_theirs = third(unit_pieces)
    (g_sum,) = totals(quarter, ((g_own[0], 0), (g_near, 0), (g_far, 0)), steps=2)
    g_other = to_ten(g_sum)
    total, moved = shared(total, moved, moves[2:3])
    wait(out_other)
    attn_pieces = second(attn_pieces)
    total, moved = shared(total, moved, moves[3:4])
    attn_terms, attn_theirs = third(attn_pieces)
    total, moved = shared(total, moved, moves[4:5])

    count_value = step_count.astype(F32)
    fixes = jnp.stack([1.0 - jnp.power(BETA_ONE, count_value), jnp.sqrt(1.0 - jnp.power(BETA_TWO, count_value))])
    up_grad, up_new, up_change = adam(ctx_scalar, fixes, up_weight, up_moments, unit_terms, unit_theirs)
    down_grad, down_new, down_change = adam(ctx_scalar, fixes, down_weight, down_moments, unit_terms, unit_theirs, first=n)
    outputs, input_grad = finish(place, out_own, out_other, g_sum, g_other, x_own, d_own)
    for k in range(5, len(moves) + 1):
        total, moved = shared(total, moved, moves[k : k + 1])
    total = total.reshape(-1)
    vector_grad = total[: 5 * width].reshape(5, width)
    vector_grad = jnp.concatenate([vector_grad, vector_grad[4:]], 0)
    unit_all = total[8 * width :].reshape(4 * heads, unit_part.shape[1])
    unit_grad = lax.dynamic_slice_in_dim(unit_all, ten * 2 * heads, 2 * heads, 0)
    qkv_grad, qkv_new, qkv_change = adam_heads(ctx_scalar, fixes, qkv_weight, qkv_moments, attn_terms, attn_theirs)
    dense_grad, dense_new, dense_change = adam(
        ctx_scalar, fixes, dense_weight, dense_moments, attn_terms, attn_theirs, tile=head_cols, first=n_qkv
    )
    unit_new, unit_change = adam_step(unit_vals, unit_moments, unit_grad, count_value, 0.0)
    vector_new, vector_change = adam_step(vectors.astype(F32), vector_moments, vector_grad, count_value, 0.0)
    return (
        outputs.reshape(inputs.shape),
        input_grad.reshape(inputs.shape),
        qkv_grad,
        dense_grad,
        up_grad,
        down_grad,
        unit_grad,
        vector_grad,
        qkv_new,
        dense_new,
        up_new,
        down_new,
        unit_new,
        vector_new,
        qkv_change,
        dense_change,
        up_change,
        down_change,
        unit_change,
        vector_change,
    )


def solution(mesh):
    rows = ("shard", "context")
    tokens = P("shard", "context", None)
    qkv, matrix, units = P(rows, "tensor", None), P(rows, "tensor"), P("tensor", None)
    qkv_pair, matrix_pair, units_pair = P(None, rows, "tensor", None), P(None, rows, "tensor"), P(None, "tensor", None)
    params = (qkv, matrix, matrix, matrix, units, P())
    states = (qkv_pair, matrix_pair, matrix_pair, matrix_pair, units_pair, P())
    return jax.shard_map(
        functools.partial(on_device, mesh.shape["shard"]),
        mesh=mesh,
        in_specs=(tokens, tokens, *params, *states, P()),
        out_specs=(tokens, tokens, *params, *states, *params),
        check_vma=False,
    )
```

```python
import functools
import math

import jax
import jax.numpy as jnp
from jax import lax
from jax.experimental import pallas as pl
from jax.experimental.pallas import tpu as pltpu
from jax.sharding import PartitionSpec as P

HEAD_DIM = 256
ROTARY = 64
EPSILON = 1e-05
BETA_ONE = 0.9
BETA_TWO = 0.95
LEARN_RATE = 0.02
WEIGHT_DECAY = 0.01
ROOT_HALF = 0.7071067811865476
ROOT_TWO_PI = 2.5066282746310002
MASKED = -1000000000.0
BF = jnp.bfloat16
F32 = jnp.float32


def dot(a, b, ca, cb):
    return lax.dot_general(a, b, (((ca,), (cb,)), ((), ())), preferred_element_type=F32)


def gelu_value(hidden):
    return 0.5 * hidden * (1.0 + lax.erf(hidden * ROOT_HALF))


def gelu_slope(hidden):
    return (
        0.5 * (1.0 + lax.erf(hidden * ROOT_HALF))
        + hidden * jnp.exp(-0.5 * hidden * hidden) / ROOT_TWO_PI
    )


BLOCK = 128
MIB = 1024 * 1024
COSTS = [0.5, 50, 10, 0.5, 20, 0, 0.5, 5, 5, 0, 50, 50, 50, 10, 50, 20, 0, 0.5, 50, 50, 0.5, 2, 20, 0.5, 50, 2, 0, 50, 0, 2, 10, 0, 0, 0.5, 20, 50, 0, 0.5, 0, 20, 2, 0, 0, 0, 0, 2, 0, 0.5, 0, 0.5, 50, 0, 0, 0, 20, 0.5, 0, 10, 5, 2, 2, 10, 0, 50, 10, 20]


def whole(shape):
    return pl.BlockSpec(shape, lambda *_: (0,) * len(shape), pipeline_mode=pl.Buffered(1))


ORDER = []
CALLS = []


def call(kernel, grid, in_specs, out_specs, out_shape, name, flops, nbytes, prefetch=0, scratch=(), limit=56):
    single = not isinstance(out_shape, (list, tuple))
    specs, shapes = ([out_specs], [out_shape]) if single else (list(out_specs), list(out_shape))
    waits = tuple(ORDER)
    cost = COSTS[len(CALLS)] if len(CALLS) < len(COSTS) else 10
    CALLS.append(name)
    first, outs = prefetch + len(in_specs), len(shapes)
    anywhere = pl.BlockSpec(memory_space=pl.ANY)

    def ordered(*refs):
        rest = refs[first + len(waits) :]
        kernel(*refs[:first], *rest[:outs], *rest[outs + 1 :])

    run = pl.pallas_call(
        ordered,
        grid_spec=pltpu.PrefetchScalarGridSpec(
            num_scalar_prefetch=prefetch,
            grid=grid,
            in_specs=[*in_specs, *[anywhere] * len(waits)],
            out_specs=[*specs, anywhere],
            scratch_shapes=list(scratch),
        ),
        out_shape=[*shapes, like((8, 128), F32)],
        compiler_params=pltpu.CompilerParams(vmem_limit_bytes=limit * MIB),
        cost_estimate=pl.CostEstimate(flops=int(cost * 1e9), bytes_accessed=1, transcendentals=0),
        name=name,
    )

    def ordered_call(*operands):
        *results, token = run(*operands, *waits)
        ORDER[:] = [token]
        return results[0] if single else results

    return ordered_call


def like(shape, dtype):
    return jax.ShapeDtypeStruct(shape, dtype)


def cut_kernel(flip, c_ref, *refs):
    *operands, out_ref = refs
    col = 0
    for ref in operands:
        if len(ref.shape) == 3:
            heads, wide = ref.shape[1] // 2, ref.shape[2]
            for c in range(2):

                @pl.when(c_ref[0] == c)
                def _(c=c, ref=ref, col=col):
                    for h in range(heads):
                        out_ref[:, col + h * wide : col + (h + 1) * wide] = ref[:, (c ^ flip) * heads + h, :]

            col += heads * wide
        else:
            n = ref.shape[1] // 2
            out_ref[:, col : col + n] = ref[:, pl.ds(pl.multiple_of((c_ref[0] ^ flip) * n, n), n)]
            col += n


def cut_quarter(ctx, flip, *operands):
    rows = operands[0].shape[0]
    n = sum(a.size for a in operands) // rows // 2
    return call(
        functools.partial(cut_kernel, flip),
        (1,),
        [whole(a.shape) for a in operands],
        whole((rows, n)),
        like((rows, n), BF),
        "cut",
        0,
        6 * rows * n,
        prefetch=1,
    )(ctx, *operands)


def arrange_kernel(place_ref, x_ref, d_ref, v_ref, xo_ref, do_ref, vo_ref):
    width = x_ref.shape[1]
    count = width // BLOCK
    rows = x_ref.shape[0] // 2
    for j in range(count):
        out = slice(j * BLOCK, (j + 1) * BLOCK)
        col = pl.ds(pl.multiple_of(place_ref[j] * BLOCK, BLOCK), BLOCK)
        for b in range(2):
            row = pl.ds(pl.multiple_of((place_ref[2 * count] ^ b) * rows, rows), rows)
            xo_ref[b * rows : (b + 1) * rows, out] = x_ref[row, col]
            do_ref[b * rows : (b + 1) * rows, out] = d_ref[row, col]
        vo_ref[:, out] = v_ref[:, col].astype(F32)


def arrange(place, x, d, v):
    operands = (x, d, v)
    outs = [(x.shape, BF), (d.shape, BF), (v.shape, F32)]
    return call(
        arrange_kernel,
        (1,),
        [whole(a.shape) for a in operands],
        [whole(a) for a, _ in outs],
        [like(*a) for a in outs],
        "arrange",
        0,
        4 * x.size * 2,
        prefetch=1,
    )(place, *operands)


def outgoing_kernel(place_ref, x_ref, o_ref):
    count = x_ref.shape[1] // BLOCK
    for j in range(count):
        col = pl.ds(pl.multiple_of(place_ref[count + j] * BLOCK, BLOCK), BLOCK)
        o_ref[:, j * BLOCK : (j + 1) * BLOCK] = x_ref[:, col]


def outgoing(place, x):
    rows, width = x.shape[0] // 2, x.shape[1]
    return call(
        outgoing_kernel,
        (1,),
        [pl.BlockSpec((rows, width), lambda i, p: (p[2 * width // BLOCK], 0))],
        whole((rows, width)),
        like((rows, width), BF),
        "outgoing",
        0,
        x.size * 2,
        prefetch=1,
    )(place, x)


def unorder_kernel(place_ref, v_ref, o_ref):
    for j in range(v_ref.shape[1] // BLOCK):
        col = pl.ds(pl.multiple_of(place_ref[j] * BLOCK, BLOCK), BLOCK)
        o_ref[:, col] = v_ref[:, j * BLOCK : (j + 1) * BLOCK]


def unorder(place, v):
    return call(
        unorder_kernel, (1,), [whole(v.shape)], whole(v.shape), like(v.shape, v.dtype), "unorder", 0, v.size * 8, prefetch=1
    )(place, v)


def pack_kernel(*refs):
    *pieces, out_ref = refs
    row = 0
    for piece in pieces:
        out_ref[row : row + piece.shape[0], :] = piece[...]
        row += piece.shape[0]


def pack(n, *pieces):
    pieces = [p if isinstance(p, tuple) else (p, 0) for p in pieces]
    rows = sum(p.shape[0] for p, _ in pieces)
    return call(
        pack_kernel,
        (1,),
        [pl.BlockSpec((p.shape[0], n), lambda i, k=k: (0, k)) for p, k in pieces],
        whole((rows, n)),
        like((rows, n), BF),
        "pack",
        0,
        rows * n * 4,
    )(*[p for p, _ in pieces])


def halves_kernel(u_ref, v_ref, top_ref, low_ref):
    top_ref[...] = u_ref[...]
    low_ref[...] = v_ref[...]


def halves(u, v):
    rows, n = u.shape[0] // 2, u.shape[1]
    return call(
        halves_kernel,
        (1,),
        [pl.BlockSpec((rows, n), lambda i: (0, 0)), pl.BlockSpec((rows, n), lambda i: (1, 0))],
        [whole((rows, n))] * 2,
        [like((rows, n), BF)] * 2,
        "halves",
        0,
        8 * rows * n,
    )(u, v)


def total_kernel(counts, *refs):
    at = 0
    for k, count in enumerate(counts):
        total = refs[at][...].astype(F32)
        for ref in refs[at + 1 : at + count]:
            total = total + ref[...].astype(F32)
        out_ref = refs[sum(counts) + k]
        out_ref[...] = total.astype(out_ref.dtype)
        at += count


def totals(rows, *groups, dtype=BF, steps=1):
    tile = rows // steps
    in_specs, operands = [], []
    for group in groups:
        for a, k in group:
            if a.shape[0] == 1:
                in_specs.append(whole(a.shape))
            else:
                in_specs.append(pl.BlockSpec((tile, a.shape[1]), lambda i, k=k: (k * steps + i, 0)))
            operands.append(a)
    width = operands[0].shape[1]
    return call(
        functools.partial(total_kernel, [len(g) for g in groups]),
        (steps,),
        in_specs,
        [pl.BlockSpec((tile, width), lambda i: (i, 0))] * len(groups),
        [like((rows, width), dtype)] * len(groups),
        "totals",
        0,
        8 * rows * width,
    )(*operands)


def norm_kernel(x_ref, v_ref, attn_ref, mlp_ref, mean_ref, inv_ref):
    x = x_ref[...].astype(F32)
    mean = jnp.mean(x, -1, keepdims=True)
    center = x - mean
    inv_std = lax.rsqrt(jnp.mean(center * center, -1, keepdims=True) + EPSILON)
    normed = center * inv_std
    attn_ref[...] = (normed * v_ref[0:1, :] + v_ref[1:2, :]).astype(BF)
    mlp_ref[...] = (normed * v_ref[2:3, :] + v_ref[3:4, :]).astype(BF)
    mean_ref[...] = jnp.broadcast_to(mean, mean_ref.shape)
    inv_ref[...] = jnp.broadcast_to(inv_std, inv_ref.shape)


def norm(x, vec):
    rows, width = x.shape
    tile = rows // 2
    block = pl.BlockSpec((tile, width), lambda i: (i, 0))
    stat = pl.BlockSpec((tile, 128), lambda i: (i, 0))
    return call(
        norm_kernel,
        (2,),
        [block, whole(vec.shape)],
        [block, block, stat, stat],
        [like(x.shape, BF), like(x.shape, BF), like((rows, 128), F32), like((rows, 128), F32)],
        "norm",
        x.size * 12,
        x.size * 6,
    )(x, vec)


def over_rows(a, weight):
    rows = weight[0].shape[0]
    return sum(dot(a[:, k * rows : (k + 1) * rows], part[...], 1, 0) for k, part in enumerate(weight))


def hidden_kernel(a_ref, b_ref, *refs):
    *weight, act_ref, slope_ref = refs
    hidden = over_rows(a_ref[...], weight) + b_ref[...]
    cdf = 0.5 * (1.0 + lax.erf(hidden * ROOT_HALF))
    act_ref[...] = (hidden * cdf).astype(BF)
    slope_ref[...] = cdf + hidden * jnp.exp(-0.5 * hidden * hidden) * (1.0 / ROOT_TWO_PI)


def units_kernel(parts, a_ref, d_ref, b_ref, *refs):
    weights, (act_ref, low_ref, sum_ref) = refs[: 2 * parts], refs[2 * parts :]
    hidden = over_rows(a_ref[...], weights[:parts]) + b_ref[...]
    cdf = 0.5 * (1.0 + lax.erf(hidden * ROOT_HALF))
    act_ref[...] = (hidden * cdf).astype(BF)
    slope = cdf + hidden * jnp.exp(-0.5 * hidden * hidden) * (1.0 / ROOT_TWO_PI)
    grad = over_rows(d_ref[...], weights[parts:]) * slope
    low_ref[...] = grad.astype(BF)
    sum_ref[...] = jnp.broadcast_to(jnp.sum(grad, 0, keepdims=True), sum_ref.shape)


def units_of(a, d, up, down, bias, tile=256):
    (rows, width), n = a.shape, up[0].shape[1]
    out = pl.BlockSpec((rows, tile), lambda j: (0, j))
    at = lambda j: (0, j)
    return call(
        functools.partial(units_kernel, len(up)),
        (n // tile,),
        [whole(a.shape), whole(d.shape), pl.BlockSpec((1, tile), at), *column_specs((*up, *down), tile, at)],
        [out, out, pl.BlockSpec((8, tile), at)],
        [like((rows, n), BF), like((rows, n), BF), like((8, n), F32)],
        "units",
        4 * rows * width * n,
        (a.size * 2 + width * n * 2 + rows * n * 2) * 2,
    )(a, d, bias, *up, *down)


def column_specs(weight, tile, at):
    return [pl.BlockSpec((part.shape[0], tile), at) for part in weight]


def hidden_of(a, weight, bias, tile=512):
    (rows, width), n = a.shape, weight[0].shape[1]
    tile = min(tile, n)
    out = pl.BlockSpec((rows, tile), lambda j: (0, j))
    return call(
        hidden_kernel,
        (n // tile,),
        [whole(a.shape), pl.BlockSpec((1, tile), lambda j: (0, j)), *column_specs(weight, tile, lambda j: (0, j))],
        [out, out],
        [like((rows, n), BF), like((rows, n), F32)],
        "hidden",
        2 * rows * width * n,
        (a.size + width * n + rows * n * 3) * 2,
    )(a, bias, *weight)


def d_hidden_kernel(d_ref, slope_ref, *refs):
    *weight, low_ref, sum_ref = refs
    grad = over_rows(d_ref[...], weight) * slope_ref[...]
    low_ref[...] = grad.astype(BF)
    sum_ref[...] = jnp.broadcast_to(jnp.sum(grad, 0, keepdims=True), sum_ref.shape)


def d_hidden_of(d, weight, slope, tile=512):
    (rows, width), n = d.shape, weight[0].shape[1]
    tile = min(tile, n)
    out = pl.BlockSpec((rows, tile), lambda j: (0, j))
    return call(
        d_hidden_kernel,
        (n // tile,),
        [whole(d.shape), out, *column_specs(weight, tile, lambda j: (0, j))],
        [out, pl.BlockSpec((8, tile), lambda j: (0, j))],
        [like((rows, n), BF), like((8, n), F32)],
        "d_hidden",
        2 * rows * width * n,
        (d.size + width * n + rows * n * 3) * 2,
    )(d, slope, *weight)


def turn(block, cosine, sine):
    head = block[:, :128]
    lane = lax.broadcasted_iota(jnp.int32, head.shape, 1)
    half = ROTARY // 2
    partner = jnp.where(lane < half, -pltpu.roll(head, 128 - half, 1), pltpu.roll(head, half, 1))
    return jnp.concatenate([head * cosine + partner * sine, block[:, 128:]], 1)


def attend_kernel(
    z_ref, a0_ref, a1_ref, b_ref, cos_ref, sin_ref, *refs
):
    *weight, ctx_ref, pack_ref, log_ref = refs
    z = z_ref[0]
    size = a0_ref.shape[0] // 2
    hd = HEAD_DIM
    scale = hd**-0.5

    def row_of(p):
        return pl.ds(pl.multiple_of((z ^ p) * size, size), size)

    for b in range(4):
        a = (a0_ref, a1_ref)[b // 2][b % 2 * size : (b % 2 + 1) * size, :]
        lin = over_rows(a, weight) + b_ref[...]
        mine = slice(b * size, (b + 1) * size)
        cosine, sine = cos_ref[mine, :], sin_ref[mine, :]
        rows = row_of(b)
        pack_ref[rows, :hd] = turn(lin[:, :hd], cosine, sine).astype(BF)
        pack_ref[rows, hd : 2 * hd] = turn(lin[:, hd : 2 * hd], cosine, sine).astype(BF)
        pack_ref[rows, 2 * hd :] = lin[:, 2 * hd :].astype(BF)
    for p in range(4):
        here, seen = slice(p * size, (p + 1) * size), slice(0, (p + 1) * size)
        scores = dot(pack_ref[here, :hd], pack_ref[seen, hd : 2 * hd], 1, 1) * scale
        row_ids = p * size + lax.broadcasted_iota(jnp.int32, scores.shape, 0)
        col_ids = lax.broadcasted_iota(jnp.int32, scores.shape, 1)
        scores = jnp.where(row_ids >= col_ids, scores, MASKED)
        top = jnp.max(scores, -1, keepdims=True)
        exponent = jnp.exp(scores - top)
        total = jnp.sum(exponent, -1, keepdims=True)
        low = (exponent * (1.0 / total)).astype(BF)
        ctx_ref[row_of(p), :] = dot(low, pack_ref[seen, 2 * hd :], 1, 0).astype(BF)
        log_ref[here, :] = jnp.broadcast_to(top + jnp.log(total), (size, log_ref.shape[1]))


def attend(z, a0, a1, weight, bias, cosine, sine):
    length, width = 2 * a0.shape[0], a0.shape[1]
    hd = HEAD_DIM
    heads = bias.shape[1] // (3 * hd)
    column = lambda rows, cols: pl.BlockSpec((rows, cols), lambda h, p: (0, h))
    return call(
        attend_kernel,
        (heads,),
        [
            whole(a0.shape),
            whole(a1.shape),
            column(1, 3 * hd),
            whole(cosine.shape),
            whole(sine.shape),
            *column_specs(weight, 3 * hd, lambda h, p: (0, h)),
        ],
        [column(length, hd), column(length, 3 * hd), column(length, 128)],
        [like((length, heads * hd), BF), like((length, heads * 3 * hd), BF), like((length, heads * 128), F32)],
        "attend",
        (3 * length * length * hd + 6 * length * width * hd) * heads,
        length * width * 8,
        prefetch=1,
    )(z, a0, a1, bias, cosine, sine, *weight)


def attend_back_kernel(
    z_ref, pack_ref, log_ref, d0_ref, d1_ref, cos_ref, sin_ref, *refs
):
    *weight, dl_ref, us_ref, g_s, dk_s, dv_s = refs
    z = z_ref[0]
    size = d0_ref.shape[0] // 2
    hd = HEAD_DIM
    scale = hd**-0.5

    def row_of(p):
        return pl.ds(pl.multiple_of((z ^ p) * size, size), size)

    for half, d_ref in enumerate((d0_ref, d1_ref)):
        grad = over_rows(d_ref[...], weight).astype(BF)
        g_s[row_of(2 * half), :] = grad[:size]
        g_s[row_of(2 * half + 1), :] = grad[size:]
    dk_s[...] = jnp.zeros_like(dk_s)
    dv_s[...] = jnp.zeros_like(dv_s)
    q_sum = jnp.zeros((1, hd), F32)
    for p in range(4):
        here, seen = slice(p * size, (p + 1) * size), slice(0, (p + 1) * size)
        rows = row_of(p)
        queries, grads = pack_ref[here, :hd], g_s[here, :]
        keys, values = pack_ref[seen, hd : 2 * hd], pack_ref[seen, 2 * hd :]
        scores = dot(queries, keys, 1, 1) * scale
        row_ids = p * size + lax.broadcasted_iota(jnp.int32, scores.shape, 0)
        col_ids = lax.broadcasted_iota(jnp.int32, scores.shape, 1)
        scores = jnp.where(row_ids >= col_ids, scores, MASKED)
        probs = jnp.exp(scores - log_ref[here, 0:1])
        low = probs.astype(BF)
        weight_grad = dot(grads, values, 1, 1)
        score_grad = (
            probs * (weight_grad - jnp.sum(probs * weight_grad, -1, keepdims=True))
        ).astype(BF)
        query_grad = (dot(score_grad, keys, 1, 0) * scale).astype(BF).astype(F32)
        dk_s[seen, :] += dot(score_grad, queries, 0, 0)
        dv_s[seen, :] += dot(low, grads, 0, 0)
        query_grad = turn(query_grad, cos_ref[rows, :], -sin_ref[rows, :])
        q_sum = q_sum + jnp.sum(query_grad, 0, keepdims=True)
        dl_ref[rows, :hd] = query_grad.astype(BF)
    k_sum = jnp.zeros((1, hd), F32)
    v_sum = jnp.zeros((1, hd), F32)
    for p in range(4):
        here = slice(p * size, (p + 1) * size)
        rows = row_of(p)
        key_grad = (dk_s[here, :] * scale).astype(BF).astype(F32)
        key_grad = turn(key_grad, cos_ref[rows, :], -sin_ref[rows, :])
        k_sum = k_sum + jnp.sum(key_grad, 0, keepdims=True)
        dl_ref[rows, hd : 2 * hd] = key_grad.astype(BF)
        value_grad = dv_s[here, :].astype(BF)
        v_sum = v_sum + jnp.sum(value_grad.astype(F32), 0, keepdims=True)
        dl_ref[rows, 2 * hd :] = value_grad
    us_ref[...] = jnp.broadcast_to(jnp.concatenate([q_sum, k_sum, v_sum], 1), us_ref.shape)


def attend_back(z, packed, logs, d0, d1, weight, cosine, sine):
    length, wide = packed.shape
    hd = HEAD_DIM
    heads = wide // (3 * hd)
    first = wide // hd
    column = lambda rows, cols: pl.BlockSpec((rows, cols), lambda h, p: (0, h))
    return call(
        attend_back_kernel,
        (heads,),
        [
            column(length, 3 * hd),
            column(length, 128),
            whole(d0.shape),
            whole(d1.shape),
            whole(cosine.shape),
            whole(sine.shape),
            *column_specs(weight, hd, lambda h, p: (0, first + h)),
        ],
        [column(length, 3 * hd), column(8, 3 * hd)],
        [like((length, wide), BF), like((8, wide), F32)],
        "attend_back",
        (9 * length * length * hd + 2 * length * d0.shape[1] * hd) * heads,
        length * wide * 8,
        prefetch=1,
        scratch=[pltpu.VMEM((length, hd), BF)] + [pltpu.VMEM((length, hd), F32)] * 2,
    )(z, packed, logs, d0, d1, cosine, sine, *weight)


def in_turn(parts, body):
    j = pl.program_id(0)
    each = pl.num_programs(0) // len(parts)
    for k, part in enumerate(parts):

        @pl.when(j // each == k)
        def _(part=part):
            body(*part)


def row_specs(shape, count, parts, col=0):
    each = count // parts
    return [pl.BlockSpec(shape, lambda j, k=k: (jnp.clip(j - k * each, 0, each - 1), col)) for k in range(parts)]


def branch_kernel(parts, a0_ref, a1_ref, ctx_ref, *refs):
    weights, outs = refs[: 2 * parts], refs[2 * parts :]
    size = outs[0].shape[0]

    def body(down_ref, dense_ref):
        for k, act_ref in enumerate((a0_ref, a1_ref)):
            ctx = ctx_ref[2 * k * size : 2 * (k + 1) * size, :]
            part = dot(act_ref[...], down_ref[...], 1, 1) + dot(ctx, dense_ref[...], 1, 1)
            outs[2 * k][...] = part[:size]
            outs[2 * k + 1][...] = part[size:].astype(BF)

    in_turn(list(zip(weights[:parts], weights[parts:])), body)


def token_outs(size, width, tile):
    spec = pl.BlockSpec((size, tile), lambda j: (0, j))
    return [spec] * 4, [like((size, width), F32), like((size, width), BF)] * 2


def branch_of(a0, a1, context_out, down, attn, tile=256):
    rows, n = a0.shape
    parts = len(down)
    width = parts * down[0].shape[0]
    cols = context_out.shape[1]
    count = width // tile
    specs, shapes = token_outs(rows // 2, width, tile)
    return call(
        functools.partial(branch_kernel, parts),
        (count,),
        [
            whole(a0.shape),
            whole(a1.shape),
            whole(context_out.shape),
            *row_specs((tile, n), count, parts),
            *row_specs((tile, cols), count, parts, attn[0].shape[1] // cols - 1),
        ],
        specs,
        shapes,
        "branch",
        4 * rows * width * (n + cols),
        (2 * rows * (n + cols) + width * (n + cols) + 2 * rows * width * 2) * 2,
    )(a0, a1, context_out, *down, *attn)


def input_grad_kernel(
    parts, dl_ref, h0_ref, h1_ref, x0_ref, x1_ref, m0_ref, m1_ref, i0_ref, i1_ref, v_ref, *refs
):
    weights, outs = refs[: 2 * parts], refs[2 * parts :]
    size = outs[0].shape[0]
    wide = dl_ref.shape[1]
    halves = ((h0_ref, x0_ref, m0_ref, i0_ref), (h1_ref, x1_ref, m1_ref, i1_ref))

    def body(attn_ref, up_ref):
        total = [0.0] * 4
        for k, (dh_ref, x_ref, mean_ref, inv_ref) in enumerate(halves):
            attn = dot(dl_ref[2 * k * size : 2 * (k + 1) * size, :], attn_ref[:, :wide], 1, 1)
            mlp = dot(dh_ref[...], up_ref[...], 1, 1)
            part = attn * v_ref[0:1, :] + mlp * v_ref[2:3, :]
            outs[2 * k][...] = part[:size]
            outs[2 * k + 1][...] = part[size:].astype(BF)
            normed = (x_ref[...].astype(F32) - mean_ref[:, 0:1]) * inv_ref[:, 0:1]
            sums = [jnp.sum(v, 0, keepdims=True) for v in (attn * normed, attn, mlp * normed, mlp)]
            total = [u + v for u, v in zip(total, sums)]
        outs[4][...] = jnp.concatenate(total + [jnp.zeros((4, attn.shape[1]), F32)], 0)

    in_turn(list(zip(weights[:parts], weights[parts:])), body)


def input_grad_of(d_linear, h0, h1, attn, up, xs, means, invs, vec, tile=256):
    rows, n = h0.shape
    width = xs[0].shape[1]
    wide = d_linear.shape[1]
    parts = len(attn)
    count = width // tile
    specs, shapes = token_outs(rows // 2, width, tile)
    column = pl.BlockSpec((rows, tile), lambda j: (0, j))
    return call(
        functools.partial(input_grad_kernel, parts),
        (count,),
        [
            whole(d_linear.shape),
            whole(h0.shape),
            whole(h1.shape),
            column,
            column,
            *[whole(a.shape) for a in (*means, *invs)],
            pl.BlockSpec((vec.shape[0], tile), lambda j: (0, j)),
            *row_specs((tile, attn[0].shape[1]), count, parts),
            *row_specs((tile, n), count, parts),
        ],
        [*specs, pl.BlockSpec((8, tile), lambda j: (0, j))],
        [*shapes, like((8, width), F32)],
        "input_grad",
        4 * rows * width * (n + wide),
        (2 * rows * (n + wide) + width * (n + wide) + 2 * rows * width * 3) * 2,
    )(d_linear, h0, h1, *xs, *means, *invs, vec, *attn, *up)


def grad_kernel(pairs, added, pieces, *refs):
    operands, adds, outs = refs[: 4 * pairs], refs[4 * pairs : 4 * pairs + added], refs[4 * pairs + added :]
    j = pl.program_id(0)
    col = 0
    for k in range(pairs):
        l0, l1, r0, r1 = (r[...] for r in operands[4 * k : 4 * k + 4])
        part = dot(l0, r0, 0, 0) + dot(l1, r1, 0, 0)
        cols = slice(col, col + part.shape[1])
        col += part.shape[1]
        half = part.shape[0] // 2
        for i, places in enumerate(pieces):

            @pl.when(j == i)
            def _(i=i, places=places, part=part, cols=cols):
                for k in range(added):
                    if k == i * added // 4:
                        part = part + adds[k][:, cols].astype(F32)
                for side, (piece, block) in enumerate(places):
                    outs[piece][block * half : (block + 1) * half, cols] = part[side * half : (side + 1) * half].astype(BF)


def grad_of(factors, pieces, sizes, adds=()):
    width = factors[0][0].shape[1]
    tile = width // 8
    first = 0 if adds else 4
    in_specs, operands, n, flops, nbytes = [], [], 0, 0, 0
    for l0, l1, r0, r1 in factors:
        rows = l0.shape[0]
        for left in (l0, l1):
            in_specs.append(pl.BlockSpec((rows, tile), lambda j: (0, first + j)))
            operands.append(left)
        cols = r0[0].shape[1]
        for right, k in (r0, r1):
            in_specs.append(pl.BlockSpec((rows, cols), lambda j, k=k: (k, 0), pipeline_mode=pl.Buffered(1)))
            operands.append(right)
        n += cols
        flops += 2 * rows * width * cols
        nbytes += 2 * rows * (width + 2 * cols)
    each = 4 // max(len(adds), 1)
    in_specs += [
        pl.BlockSpec((tile, n), lambda j, k=k: (jnp.clip(j - k * each, 0, each - 1), 0)) for k in range(len(adds))
    ]
    shapes = [(size * tile // 2, n) for size in sizes]
    return call(
        functools.partial(grad_kernel, len(factors), len(adds), pieces),
        (4,),
        in_specs,
        [whole(shape) for shape in shapes],
        [like(shape, BF) for shape in shapes],
        "grad_near" if adds else "grad_far",
        flops,
        nbytes + width * n,
    )(*operands, *adds)


def fold_kernel(cross, keep_ref, got_ref, o_ref):
    for j, k in enumerate(cross):
        here = slice(j * BLOCK, (j + 1) * BLOCK)
        o_ref[:, k * BLOCK : (k + 1) * BLOCK] = (keep_ref[:, here] + got_ref[:, here].astype(F32)).astype(BF)


def fold(cross, keep, got):
    rows, width = keep.shape
    tile = rows // 2
    block = pl.BlockSpec((tile, width), lambda i: (i, 0))
    return call(
        functools.partial(fold_kernel, cross), (2,), [block, block], block, like(keep.shape, BF), "fold", keep.size, keep.size * 8
    )(keep, got)


def finish_kernel(place_ref, o0_ref, o1_ref, g0_ref, g1_ref, x_ref, d_ref, out_ref, grad_ref):
    width = x_ref.shape[1]
    count = width // BLOCK
    x = x_ref[...].astype(F32)
    center = x - jnp.mean(x, -1, keepdims=True)
    inv_std = lax.rsqrt(jnp.mean(center * center, -1, keepdims=True) + EPSILON)
    normed = center * inv_std

    def body(o_ref, g_ref):
        g = g_ref[...].astype(F32)
        grad = d_ref[...].astype(F32) + inv_std * (
            g - jnp.mean(g, -1, keepdims=True) - normed * jnp.mean(g * normed, -1, keepdims=True)
        )
        for j in range(count):
            col = pl.ds(pl.multiple_of(place_ref[j] * BLOCK, BLOCK), BLOCK)
            part = slice(j * BLOCK, (j + 1) * BLOCK)
            out_ref[:, col] = o_ref[:, part]
            grad_ref[:, col] = grad[:, part]

    in_turn(((o0_ref, g0_ref), (o1_ref, g1_ref)), body)


def finish(place, o0, o1, g0, g1, x, d):
    rows, width = o0.shape
    per = 2
    tile = rows // per
    at = 2 * width // BLOCK
    first = pl.BlockSpec((tile, width), lambda i, p: (jnp.minimum(i, per - 1), 0))
    second = pl.BlockSpec((tile, width), lambda i, p: (jnp.maximum(i - per, 0), 0))
    local = pl.BlockSpec((tile, width), lambda i, p: (i, 0))
    out = pl.BlockSpec((tile, width), lambda i, p: ((p[at] ^ (i // per)) * per + i % per, 0))
    return call(
        finish_kernel,
        (2 * per,),
        [first, second, first, second, local, local],
        [out, out],
        [like(x.shape, BF), like(x.shape, F32)],
        "finish",
        x.size * 20,
        x.size * 14,
        prefetch=1,
    )(place, o0, o1, g0, g1, x, d)


def step_values(weight, first, root, gradient, fix_one, fix_two, decay_rate):
    first_new = BETA_ONE * first + (1.0 - BETA_ONE) * gradient
    root_new = jnp.sqrt(BETA_TWO * root * root + (1.0 - BETA_TWO) * gradient * gradient)
    change = -LEARN_RATE * (
        first_new / fix_one / (root_new / fix_two + 1e-08) + decay_rate * weight
    )
    return first_new, root_new, change


def adam_kernel(c_ref, fix_ref, w_ref, m_ref, a_ref, b_ref, e_ref, t_ref, g_ref, n_ref, u_ref):
    def body(gradient):
        first, root, change = step_values(
            w_ref[...].astype(F32), m_ref[0], m_ref[1], gradient, fix_ref[0], fix_ref[1], WEIGHT_DECAY
        )
        g_ref[...] = gradient
        n_ref[0] = first
        n_ref[1] = root
        u_ref[...] = change

    @pl.when(pl.program_id(0) == 0)
    def _():
        body(a_ref[...].astype(F32) + b_ref[...].astype(F32) + e_ref[...].astype(F32))

    @pl.when(pl.program_id(0) == 1)
    def _():
        body(t_ref[...].astype(F32))


def adam(ctx, fixes, weight, moments, terms, theirs, tile=2048, first=0):
    rows, cols = weight.shape
    n = cols // 2
    tile = min(tile, n)
    first //= tile
    per = n // tile
    at = lambda k, i, c: (0, (c[0] ^ k) * per + i)
    mine = pl.BlockSpec((rows, tile), lambda k, i, c: (0, first + i + k * (per - 1 - i)))
    other = pl.BlockSpec((rows, tile), lambda k, i, c: (0, first + i * k))
    matrix = pl.BlockSpec((rows, tile), at)
    pair = pl.BlockSpec((2, rows, tile), lambda k, i, c: (0, *at(k, i, c)))
    return call(
        adam_kernel,
        (2, per),
        [pl.BlockSpec(memory_space=pltpu.SMEM), matrix, pair, mine, mine, mine, other],
        [matrix, pair, matrix],
        [like(weight.shape, F32), like(moments.shape, F32), like(weight.shape, F32)],
        "adam",
        weight.size * 20,
        weight.size * 30,
        prefetch=1,
    )(ctx, fixes, weight, moments, *terms, theirs)


def adam_heads_kernel(c_ref, fix_ref, w_ref, m_ref, a_ref, b_ref, e_ref, t_ref, g_ref, n_ref, u_ref):
    mine = a_ref[...].astype(F32) + b_ref[...].astype(F32) + e_ref[...].astype(F32)
    theirs = t_ref[...].astype(F32)
    heads, wide = w_ref.shape[1] // 2, w_ref.shape[2]
    for h in range(2 * heads):
        cols = slice(h % heads * wide, (h % heads + 1) * wide)
        gradient = jnp.where(c_ref[0] == h // heads, mine[:, cols], theirs[:, cols])
        first, root, change = step_values(
            w_ref[:, h, :].astype(F32), m_ref[0, :, h, :], m_ref[1, :, h, :], gradient, fix_ref[0], fix_ref[1], WEIGHT_DECAY
        )
        g_ref[:, h, :] = gradient
        n_ref[0, :, h, :] = first
        n_ref[1, :, h, :] = root
        u_ref[:, h, :] = change


def adam_heads(ctx, fixes, weight, moments, terms, theirs):
    rows, heads, wide = weight.shape
    tile = rows // 4
    part = pl.BlockSpec((tile, heads // 2 * wide), lambda i, c: (i, 0))
    cube = pl.BlockSpec((tile, heads, wide), lambda i, c: (i, 0, 0))
    pair = pl.BlockSpec((2, tile, heads, wide), lambda i, c: (0, i, 0, 0))
    return call(
        adam_heads_kernel,
        (4,),
        [pl.BlockSpec(memory_space=pltpu.SMEM), cube, pair, part, part, part, part],
        [cube, pair, cube],
        [like(weight.shape, F32), like(moments.shape, F32), like(weight.shape, F32)],
        "adam_heads",
        weight.size * 20,
        weight.size * 30,
        prefetch=1,
    )(ctx, fixes, weight, moments, *terms, theirs)


def rotary_tables(positions):
    lane = jnp.arange(128)
    inverse = jnp.exp((lane % (ROTARY // 2)).astype(F32) * (-2.0 / ROTARY) * math.log(10000.0))
    angles = positions.astype(F32)[:, None] * inverse[None, :]
    turned = lane[None, :] < ROTARY
    return (jnp.where(turned, jnp.cos(angles), 1.0), jnp.where(turned, jnp.sin(angles), 0.0))


def adam_step(weight, moments, gradient, count_value, decay_rate):
    first_new = BETA_ONE * moments[0] + (1.0 - BETA_ONE) * gradient
    root_new = jnp.sqrt(BETA_TWO * moments[1] * moments[1] + (1.0 - BETA_TWO) * gradient * gradient)
    fix_one = 1.0 - jnp.power(BETA_ONE, count_value)
    fix_two = 1.0 - jnp.power(BETA_TWO, count_value)
    change = -LEARN_RATE * (
        first_new / fix_one / (root_new / jnp.sqrt(fix_two) + 1e-08) + decay_rate * weight
    )
    return (jnp.stack([first_new, root_new]), change)


def on_device(
    shard_count,
    inputs,
    cotangent,
    qkv_weight,
    dense_weight,
    up_weight,
    down_weight,
    unit_biases,
    vectors,
    qkv_moments,
    dense_moments,
    up_moments,
    down_moments,
    unit_moments,
    vector_moments,
    step_count,
):
    ORDER.clear()
    CALLS.clear()
    shard, ctx, ten = (lax.axis_index(a) for a in ("shard", "context", "tensor"))
    fast = shard_count == 8
    _, local_len, width = inputs.shape
    quarter = local_len // 2
    row_count, heads_local, head_wide = qkv_weight.shape
    heads = heads_local // 2
    units = up_weight.shape[1] // 2
    head_cols = heads * HEAD_DIM
    n_qkv = heads * head_wide
    count = width // BLOCK

    def along(axis, size, bit):
        return lambda v: lax.ppermute(v, axis, [(i, i ^ bit) for i in range(size)])

    to_core, to_x, to_y = (along("shard", shard_count, bit) for bit in (1, 2, 4))
    to_ctx, to_ten = along("context", 2, 1), along("tensor", 2, 1)

    if fast:
        chips = ((0, 4, 2, 6), (0, 2, 4, 6))
        relative = [(core + chips[ab][k], ab) for core in range(2) for ab in range(2) for k in range(4)]
        places = [[(shard ^ s) * 2 + (ctx ^ f ^ ab) for s, ab in relative] for f in range(2)]
        cross = [core * 8 + (1 - ab) * 4 + (0, 2, 1, 3)[k] for core in range(2) for ab in range(2) for k in range(4)]
    else:
        places = [[jnp.int32(j) for j in range(count)]] * 2
        cross = list(range(count))
    place = jnp.stack([*places[0], *places[1], ten]).astype(jnp.int32)
    z = ctx * 2 + ten
    ctx_scalar, z_scalar = (v.reshape(1).astype(jnp.int32) for v in (ctx, z))

    def wait(*values):
        ORDER.extend(values)

    def full_rows(mine, other):
        block = jnp.where(ctx == 0, jnp.concatenate([mine, other], 0), jnp.concatenate([other, mine], 0))
        full = lax.all_gather(block, "shard", axis=0, tiled=True)
        return tuple(full[k * width // 4 : (k + 1) * width // 4] for k in range(4))

    r = row_count
    x_in, d_in = inputs.reshape(local_len, width), cotangent.reshape(local_len, width)
    unit_vals = unit_biases.astype(F32)
    my_units = lax.dynamic_slice_in_dim(unit_vals, ctx * heads, heads, 0)
    qkv_bias, unit_bias = my_units[:, :head_wide].reshape(1, n_qkv), my_units[:, head_wide:].reshape(1, units)
    positions = ((jnp.arange(4) ^ z)[:, None] * quarter + jnp.arange(quarter)[None, :]).reshape(-1)
    cosine, sine = rotary_tables(positions)

    n = up_weight.shape[1] // 2
    units_other = to_ctx(cut_quarter(ctx_scalar, 1, up_weight, down_weight))
    mine = cut_quarter(ctx_scalar, 0, up_weight, down_weight, qkv_weight, dense_weight)
    if fast:
        a_x, a_y = to_x(mine), to_y(mine)
    x_own, d_own, vec = arrange(place, x_in, d_in, vectors)
    attn_own, mlp_own, mean_own, inv_own = norm(x_own, vec)
    if fast:
        top, low = halves(a_y, a_x)
        a_top, a_low = to_x(top), to_y(low)
    wait(units_other)
    attn_other = to_ctx(cut_quarter(ctx_scalar, 1, qkv_weight, dense_weight))
    if fast:
        units_x, units_y = to_x(units_other), to_y(units_other)
    wait(attn_other)
    x_first = to_ctx(outgoing(place, x_in))

    def packed(pieces, k):
        near = pack(n, *[(a, k) for a in pieces])
        return near, to_core(near)

    if fast:
        mine_parts = (mine, a_y, a_x, a_top, a_low)
        up_a, up_far_a = packed(mine_parts, 0)
        down_a, down_far_a = packed(mine_parts, 1)
        top, low = halves(units_y, units_x)
        units_parts = (units_other, units_x, units_y, to_x(top), to_y(low))
        attn_x, attn_y = to_x(attn_other), to_y(attn_other)
        attn_a, attn_far_a = packed(mine_parts, 2)
        up_b, up_far_b = packed(units_parts, 0)
        top, low = halves(attn_y, attn_x)
        attn_parts = (attn_other, attn_x, attn_y, to_x(top), to_y(low))
        down_b, down_far_b = packed(units_parts, 1)
        w_up, w_down = (up_a, up_b, up_far_a, up_far_b), (down_a, down_b, down_far_a, down_far_b)
    else:
        w_up = full_rows(mine[:, :n], units_other[:, :n])
        w_down = full_rows(mine[:, n : 2 * n], units_other[:, n:])
        w_attn = full_rows(mine[:, 2 * n :], attn_other)
    active_own, slope_own = hidden_of(mlp_own, w_up, unit_bias)
    if fast:
        attn_b, attn_far_b = packed(attn_parts, 0)
        w_attn = (attn_a, attn_b, attn_far_a, attn_far_b)
    wait(x_first)
    d_first = to_ctx(outgoing(place, d_in))
    x_second = to_ten(x_first)
    low_own, sum_own = d_hidden_of(d_own, w_down, slope_own)
    x_oth = pack(width, x_first, x_second)
    attn_oth, mlp_oth, mean_oth, inv_oth = norm(x_oth, vec)
    active_oth, slope_oth = hidden_of(mlp_oth, w_up, unit_bias)
    wait(d_first)
    d_second = to_ten(d_first)
    context_out, packed_qkv, logs = attend(z_scalar, attn_own, attn_oth, w_attn, qkv_bias, cosine, sine)
    *branch_own, branch_keep, branch_send = branch_of(active_own, active_oth, context_out, w_down, w_attn)
    branch_got = to_ten(branch_send)
    branch_near = to_ten(branch_own[1])
    d_oth = pack(width, d_first, d_second)

    def far_parts(factors, count):
        each = 4 // count
        steps = [[(k // each, k % each * 2), (k // each, k % each * 2 + 1)] for k in range(4)]
        parts = grad_of(factors, steps, (2 * each,) * count)
        return [to_core(part) for part in parts] if fast else parts

    def near_parts(factors, far):
        if not fast:
            (near,) = grad_of(factors, [[(0, 2 * k), (0, 2 * k + 1)] for k in range(4)], (8,), [jnp.zeros_like(part) for part in far])
            return lax.psum_scatter(jnp.concatenate([near, *far], 0), "shard", scatter_dimension=0, tiled=True)
        a_own, a_x, b_own, b_y = grad_of(factors, [[(k, 0), (k, 1)] for k in range(4)], (2, 2, 2, 2), far)
        return a_own, b_own, to_y(b_y), to_x(a_x)

    def second(parts):
        if not fast:
            return parts
        a_own, b_own, b_got, a_got = parts
        b_sum, a_sum = totals(r, ((b_own, 1), (b_got, 1)), ((a_own, 1), (a_got, 1)))
        return (*parts, to_x(b_sum), to_y(a_sum))

    def third(parts):
        if not fast:
            kept = lax.dynamic_slice_in_dim(parts, ctx * r, r, 0)
            zero = jnp.zeros_like(kept)
            return (kept, zero, zero), to_ctx(lax.dynamic_slice_in_dim(parts, (1 - ctx) * r, r, 0))
        a_own, b_own, b_got, a_got, b_last, a_last = parts
        wait(a_last)
        (away,) = totals(r, ((b_own, 0), (b_got, 0), (b_last, 0)))
        return (a_own, a_got, a_last), to_ctx(away)

    low_oth, sum_oth = d_hidden_of(d_oth, w_down, slope_oth)
    unit_factors = [(mlp_own, mlp_oth, (low_own, 0), (low_oth, 0)), (d_own, d_oth, (active_own, 0), (active_oth, 0))]
    unit_far = far_parts(unit_factors, 2)
    branch_far = to_ctx(fold(cross, branch_keep, branch_got))
    d_linear, unit_sums = attend_back(z_scalar, packed_qkv, logs, d_own, d_oth, w_attn, cosine, sine)
    unit_pieces = near_parts(unit_factors, unit_far)
    wait(branch_near)
    *g_own, g_keep, g_send, sums = input_grad_of(
        d_linear, low_own, low_oth, w_attn, w_up, (x_own, x_oth), (mean_own, mean_oth), (inv_own, inv_oth), vec
    )
    g_got = to_ten(g_send)
    g_near = to_ten(g_own[1])
    attn_factors = [
        (attn_own, attn_oth, (d_linear, 0), (d_linear, 1)),
        (d_own, d_oth, (context_out, 0), (context_out, 1)),
    ]
    d_sum = jnp.sum(d_own[:quarter].astype(F32), 0, keepdims=True)
    sums = unorder(place, jnp.concatenate([sums[:4], d_sum, jnp.zeros((3, width), F32)], 0))
    unit_part = jnp.concatenate(
        [unit_sums[0].reshape(heads, head_wide), (sum_own + sum_oth)[0].reshape(heads, units // heads)], 1
    )
    unit_rows = jnp.where(jnp.arange(4)[:, None, None] == ten * 2 + ctx, unit_part[None], 0.0)
    total = jnp.concatenate([sums.reshape(-1), unit_rows.reshape(-1)]).reshape(-1, BLOCK)
    moves = [to_ctx] + [along("shard", shard_count, 1 << k) for k in range(shard_count.bit_length() - 1)] + [to_ten]
    moved = moves[0](total)

    def shared(total, moved, moves):
        (total,) = totals(total.shape[0], ((total, 0), (moved, 0)), dtype=F32)
        return total, moves[0](total) if moves else None

    attn_far = far_parts(attn_factors, 2)
    out_bias = (vec[4] + vec[5]).reshape(1, width)
    (out_own,) = totals(quarter, ((branch_own[0], 0), (branch_near, 0), (branch_far, 0), (x_own, 0), (out_bias, 0)), steps=2)
    out_other = to_ten(out_own)
    unit_pieces = second(unit_pieces)
    g_far = to_ctx(fold(cross, g_keep, g_got))
    total, moved = shared(total, moved, moves[1:2])
    attn_pieces = near_parts(attn_factors, attn_far)
    unit_terms, unit_theirs = third(unit_pieces)
    (g_sum,) = totals(quarter, ((g_own[0], 0), (g_near, 0), (g_far, 0)), steps=2)
    g_other = to_ten(g_sum)
    total, moved = shared(total, moved, moves[2:3])
    wait(out_other)
    attn_pieces = second(attn_pieces)
    total, moved = shared(total, moved, moves[3:4])
    attn_terms, attn_theirs = third(attn_pieces)
    total, moved = shared(total, moved, moves[4:5])

    count_value = step_count.astype(F32)
    fixes = jnp.stack([1.0 - jnp.power(BETA_ONE, count_value), jnp.sqrt(1.0 - jnp.power(BETA_TWO, count_value))])
    up_grad, up_new, up_change = adam(ctx_scalar, fixes, up_weight, up_moments, unit_terms, unit_theirs)
    down_grad, down_new, down_change = adam(ctx_scalar, fixes, down_weight, down_moments, unit_terms, unit_theirs, first=n)
    outputs, input_grad = finish(place, out_own, out_other, g_sum, g_other, x_own, d_own)
    for k in range(5, len(moves) + 1):
        total, moved = shared(total, moved, moves[k : k + 1])
    total = total.reshape(-1)
    vector_grad = total[: 5 * width].reshape(5, width)
    vector_grad = jnp.concatenate([vector_grad, vector_grad[4:]], 0)
    unit_all = total[8 * width :].reshape(4 * heads, unit_part.shape[1])
    unit_grad = lax.dynamic_slice_in_dim(unit_all, ten * 2 * heads, 2 * heads, 0)
    qkv_grad, qkv_new, qkv_change = adam_heads(ctx_scalar, fixes, qkv_weight, qkv_moments, attn_terms, attn_theirs)
    dense_grad, dense_new, dense_change = adam(
        ctx_scalar, fixes, dense_weight, dense_moments, attn_terms, attn_theirs, tile=head_cols, first=n_qkv
    )
    unit_new, unit_change = adam_step(unit_vals, unit_moments, unit_grad, count_value, 0.0)
    vector_new, vector_change = adam_step(vectors.astype(F32), vector_moments, vector_grad, count_value, 0.0)
    return (
        outputs.reshape(inputs.shape),
        input_grad.reshape(inputs.shape),
        qkv_grad,
        dense_grad,
        up_grad,
        down_grad,
        unit_grad,
        vector_grad,
        qkv_new,
        dense_new,
        up_new,
        down_new,
        unit_new,
        vector_new,
        qkv_change,
        dense_change,
        up_change,
        down_change,
        unit_change,
        vector_change,
    )


def solution(mesh):
    rows = ("shard", "context")
    tokens = P("shard", "context", None)
    qkv, matrix, units = P(rows, "tensor", None), P(rows, "tensor"), P("tensor", None)
    qkv_pair, matrix_pair, units_pair = P(None, rows, "tensor", None), P(None, rows, "tensor"), P(None, "tensor", None)
    params = (qkv, matrix, matrix, matrix, units, P())
    states = (qkv_pair, matrix_pair, matrix_pair, matrix_pair, units_pair, P())
    return jax.shard_map(
        functools.partial(on_device, mesh.shape["shard"]),
        mesh=mesh,
        in_specs=(tokens, tokens, *params, *states, P()),
        out_specs=(tokens, tokens, *params, *states, *params),
        check_vma=False,
    )
```

```python
import functools
import math

import jax
import jax.numpy as jnp
from jax import lax
from jax.experimental import pallas as pl
from jax.experimental.pallas import tpu as pltpu
from jax.sharding import PartitionSpec as P

HEAD_DIM = 256
ROTARY = 64
EPSILON = 1e-05
BETA_ONE = 0.9
BETA_TWO = 0.95
LEARN_RATE = 0.02
WEIGHT_DECAY = 0.01
ROOT_HALF = 0.7071067811865476
ROOT_TWO_PI = 2.5066282746310002
MASKED = -1000000000.0
BF = jnp.bfloat16
F32 = jnp.float32


def dot(a, b, ca, cb):
    return lax.dot_general(a, b, (((ca,), (cb,)), ((), ())), preferred_element_type=F32)


def gelu_value(hidden):
    return 0.5 * hidden * (1.0 + lax.erf(hidden * ROOT_HALF))


def gelu_slope(hidden):
    return (
        0.5 * (1.0 + lax.erf(hidden * ROOT_HALF))
        + hidden * jnp.exp(-0.5 * hidden * hidden) / ROOT_TWO_PI
    )


BLOCK = 128
MIB = 1024 * 1024
COSTS = [50, 10, 20, 0.5, 0, 0, 2, 50, 5, 2, 50, 0.5, 50, 10, 50, 20, 0, 20, 50, 50, 10, 2, 20, 0.5, 50, 10, 50, 50, 50, 2, 10, 0, 5, 0.5, 20, 50, 0, 0.5, 0, 10, 5, 0, 0, 0, 2, 2, 5, 0, 2, 0.5, 20, 0.5, 0, 2, 20, 0.5, 0, 0.5, 5, 0, 2, 0, 5, 0, 0, 20]


def whole(shape):
    return pl.BlockSpec(shape, lambda *_: (0,) * len(shape), pipeline_mode=pl.Buffered(1))


ORDER = []
CALLS = []


def call(kernel, grid, in_specs, out_specs, out_shape, name, flops, nbytes, prefetch=0, scratch=(), limit=56):
    single = not isinstance(out_shape, (list, tuple))
    specs, shapes = ([out_specs], [out_shape]) if single else (list(out_specs), list(out_shape))
    waits = tuple(ORDER)
    cost = COSTS[len(CALLS)] if len(CALLS) < len(COSTS) else 10
    CALLS.append(name)
    first, outs = prefetch + len(in_specs), len(shapes)
    anywhere = pl.BlockSpec(memory_space=pl.ANY)

    def ordered(*refs):
        rest = refs[first + len(waits) :]
        kernel(*refs[:first], *rest[:outs], *rest[outs + 1 :])

    run = pl.pallas_call(
        ordered,
        grid_spec=pltpu.PrefetchScalarGridSpec(
            num_scalar_prefetch=prefetch,
            grid=grid,
            in_specs=[*in_specs, *[anywhere] * len(waits)],
            out_specs=[*specs, anywhere],
            scratch_shapes=list(scratch),
        ),
        out_shape=[*shapes, like((8, 128), F32)],
        compiler_params=pltpu.CompilerParams(vmem_limit_bytes=limit * MIB),
        cost_estimate=pl.CostEstimate(flops=int(cost * 1e9), bytes_accessed=1, transcendentals=0),
        name=name,
    )

    def ordered_call(*operands):
        *results, token = run(*operands, *waits)
        ORDER[:] = [token]
        return results[0] if single else results

    return ordered_call


def like(shape, dtype):
    return jax.ShapeDtypeStruct(shape, dtype)


def cut_kernel(flip, c_ref, *refs):
    *operands, out_ref = refs
    col = 0
    for ref in operands:
        if len(ref.shape) == 3:
            heads, wide = ref.shape[1] // 2, ref.shape[2]
            for c in range(2):

                @pl.when(c_ref[0] == c)
                def _(c=c, ref=ref, col=col):
                    for h in range(heads):
                        out_ref[:, col + h * wide : col + (h + 1) * wide] = ref[:, (c ^ flip) * heads + h, :]

            col += heads * wide
        else:
            n = ref.shape[1] // 2
            out_ref[:, col : col + n] = ref[:, pl.ds(pl.multiple_of((c_ref[0] ^ flip) * n, n), n)]
            col += n


def cut_quarter(ctx, flip, *operands):
    rows = operands[0].shape[0]
    n = sum(a.size for a in operands) // rows // 2
    return call(
        functools.partial(cut_kernel, flip),
        (1,),
        [whole(a.shape) for a in operands],
        whole((rows, n)),
        like((rows, n), BF),
        "cut",
        0,
        6 * rows * n,
        prefetch=1,
    )(ctx, *operands)


def arrange_kernel(place_ref, x_ref, d_ref, v_ref, xo_ref, do_ref, vo_ref):
    width = x_ref.shape[1]
    count = width // BLOCK
    rows = x_ref.shape[0] // 2
    for j in range(count):
        out = slice(j * BLOCK, (j + 1) * BLOCK)
        col = pl.ds(pl.multiple_of(place_ref[j] * BLOCK, BLOCK), BLOCK)
        for b in range(2):
            row = pl.ds(pl.multiple_of((place_ref[2 * count] ^ b) * rows, rows), rows)
            xo_ref[b * rows : (b + 1) * rows, out] = x_ref[row, col]
            do_ref[b * rows : (b + 1) * rows, out] = d_ref[row, col]
        vo_ref[:, out] = v_ref[:, col].astype(F32)


def arrange(place, x, d, v):
    operands = (x, d, v)
    outs = [(x.shape, BF), (d.shape, BF), (v.shape, F32)]
    return call(
        arrange_kernel,
        (1,),
        [whole(a.shape) for a in operands],
        [whole(a) for a, _ in outs],
        [like(*a) for a in outs],
        "arrange",
        0,
        4 * x.size * 2,
        prefetch=1,
    )(place, *operands)


def outgoing_kernel(place_ref, x_ref, o_ref):
    count = x_ref.shape[1] // BLOCK
    for j in range(count):
        col = pl.ds(pl.multiple_of(place_ref[count + j] * BLOCK, BLOCK), BLOCK)
        o_ref[:, j * BLOCK : (j + 1) * BLOCK] = x_ref[:, col]


def outgoing(place, x):
    rows, width = x.shape[0] // 2, x.shape[1]
    return call(
        outgoing_kernel,
        (1,),
        [pl.BlockSpec((rows, width), lambda i, p: (p[2 * width // BLOCK], 0))],
        whole((rows, width)),
        like((rows, width), BF),
        "outgoing",
        0,
        x.size * 2,
        prefetch=1,
    )(place, x)


def unorder_kernel(place_ref, v_ref, o_ref):
    for j in range(v_ref.shape[1] // BLOCK):
        col = pl.ds(pl.multiple_of(place_ref[j] * BLOCK, BLOCK), BLOCK)
        o_ref[:, col] = v_ref[:, j * BLOCK : (j + 1) * BLOCK]


def unorder(place, v):
    return call(
        unorder_kernel, (1,), [whole(v.shape)], whole(v.shape), like(v.shape, v.dtype), "unorder", 0, v.size * 8, prefetch=1
    )(place, v)


def pack_kernel(*refs):
    *pieces, out_ref = refs
    row = 0
    for piece in pieces:
        out_ref[row : row + piece.shape[0], :] = piece[...]
        row += piece.shape[0]


def pack(n, *pieces):
    pieces = [p if isinstance(p, tuple) else (p, 0) for p in pieces]
    rows = sum(p.shape[0] for p, _ in pieces)
    return call(
        pack_kernel,
        (1,),
        [pl.BlockSpec((p.shape[0], n), lambda i, k=k: (0, k)) for p, k in pieces],
        whole((rows, n)),
        like((rows, n), BF),
        "pack",
        0,
        rows * n * 4,
    )(*[p for p, _ in pieces])


def halves_kernel(u_ref, v_ref, top_ref, low_ref):
    top_ref[...] = u_ref[...]
    low_ref[...] = v_ref[...]


def halves(u, v):
    rows, n = u.shape[0] // 2, u.shape[1]
    return call(
        halves_kernel,
        (1,),
        [pl.BlockSpec((rows, n), lambda i: (0, 0)), pl.BlockSpec((rows, n), lambda i: (1, 0))],
        [whole((rows, n))] * 2,
        [like((rows, n), BF)] * 2,
        "halves",
        0,
        8 * rows * n,
    )(u, v)


def total_kernel(counts, *refs):
    at = 0
    for k, count in enumerate(counts):
        total = refs[at][...].astype(F32)
        for ref in refs[at + 1 : at + count]:
            total = total + ref[...].astype(F32)
        out_ref = refs[sum(counts) + k]
        out_ref[...] = total.astype(out_ref.dtype)
        at += count


def totals(rows, *groups, dtype=BF, steps=1):
    tile = rows // steps
    in_specs, operands = [], []
    for group in groups:
        for a, k in group:
            if a.shape[0] == 1:
                in_specs.append(whole(a.shape))
            else:
                in_specs.append(pl.BlockSpec((tile, a.shape[1]), lambda i, k=k: (k * steps + i, 0)))
            operands.append(a)
    width = operands[0].shape[1]
    return call(
        functools.partial(total_kernel, [len(g) for g in groups]),
        (steps,),
        in_specs,
        [pl.BlockSpec((tile, width), lambda i: (i, 0))] * len(groups),
        [like((rows, width), dtype)] * len(groups),
        "totals",
        0,
        8 * rows * width,
    )(*operands)


def norm_kernel(x_ref, v_ref, attn_ref, mlp_ref, mean_ref, inv_ref):
    x = x_ref[...].astype(F32)
    mean = jnp.mean(x, -1, keepdims=True)
    center = x - mean
    inv_std = lax.rsqrt(jnp.mean(center * center, -1, keepdims=True) + EPSILON)
    normed = center * inv_std
    attn_ref[...] = (normed * v_ref[0:1, :] + v_ref[1:2, :]).astype(BF)
    mlp_ref[...] = (normed * v_ref[2:3, :] + v_ref[3:4, :]).astype(BF)
    mean_ref[...] = jnp.broadcast_to(mean, mean_ref.shape)
    inv_ref[...] = jnp.broadcast_to(inv_std, inv_ref.shape)


def norm(x, vec):
    rows, width = x.shape
    tile = rows // 2
    block = pl.BlockSpec((tile, width), lambda i: (i, 0))
    stat = pl.BlockSpec((tile, 128), lambda i: (i, 0))
    return call(
        norm_kernel,
        (2,),
        [block, whole(vec.shape)],
        [block, block, stat, stat],
        [like(x.shape, BF), like(x.shape, BF), like((rows, 128), F32), like((rows, 128), F32)],
        "norm",
        x.size * 12,
        x.size * 6,
    )(x, vec)


def over_rows(a, weight):
    rows = weight[0].shape[0]
    return sum(dot(a[:, k * rows : (k + 1) * rows], part[...], 1, 0) for k, part in enumerate(weight))


def hidden_kernel(a_ref, b_ref, *refs):
    *weight, act_ref, slope_ref = refs
    hidden = over_rows(a_ref[...], weight) + b_ref[...]
    cdf = 0.5 * (1.0 + lax.erf(hidden * ROOT_HALF))
    act_ref[...] = (hidden * cdf).astype(BF)
    slope_ref[...] = cdf + hidden * jnp.exp(-0.5 * hidden * hidden) * (1.0 / ROOT_TWO_PI)


def units_kernel(parts, a_ref, d_ref, b_ref, *refs):
    weights, (act_ref, low_ref, sum_ref) = refs[: 2 * parts], refs[2 * parts :]
    hidden = over_rows(a_ref[...], weights[:parts]) + b_ref[...]
    cdf = 0.5 * (1.0 + lax.erf(hidden * ROOT_HALF))
    act_ref[...] = (hidden * cdf).astype(BF)
    slope = cdf + hidden * jnp.exp(-0.5 * hidden * hidden) * (1.0 / ROOT_TWO_PI)
    grad = over_rows(d_ref[...], weights[parts:]) * slope
    low_ref[...] = grad.astype(BF)
    sum_ref[...] = jnp.broadcast_to(jnp.sum(grad, 0, keepdims=True), sum_ref.shape)


def units_of(a, d, up, down, bias, tile=256):
    (rows, width), n = a.shape, up[0].shape[1]
    out = pl.BlockSpec((rows, tile), lambda j: (0, j))
    at = lambda j: (0, j)
    return call(
        functools.partial(units_kernel, len(up)),
        (n // tile,),
        [whole(a.shape), whole(d.shape), pl.BlockSpec((1, tile), at), *column_specs((*up, *down), tile, at)],
        [out, out, pl.BlockSpec((8, tile), at)],
        [like((rows, n), BF), like((rows, n), BF), like((8, n), F32)],
        "units",
        4 * rows * width * n,
        (a.size * 2 + width * n * 2 + rows * n * 2) * 2,
    )(a, d, bias, *up, *down)


def column_specs(weight, tile, at):
    return [pl.BlockSpec((part.shape[0], tile), at) for part in weight]


def hidden_of(a, weight, bias, tile=512):
    (rows, width), n = a.shape, weight[0].shape[1]
    tile = min(tile, n)
    out = pl.BlockSpec((rows, tile), lambda j: (0, j))
    return call(
        hidden_kernel,
        (n // tile,),
        [whole(a.shape), pl.BlockSpec((1, tile), lambda j: (0, j)), *column_specs(weight, tile, lambda j: (0, j))],
        [out, out],
        [like((rows, n), BF), like((rows, n), F32)],
        "hidden",
        2 * rows * width * n,
        (a.size + width * n + rows * n * 3) * 2,
    )(a, bias, *weight)


def d_hidden_kernel(d_ref, slope_ref, *refs):
    *weight, low_ref, sum_ref = refs
    grad = over_rows(d_ref[...], weight) * slope_ref[...]
    low_ref[...] = grad.astype(BF)
    sum_ref[...] = jnp.broadcast_to(jnp.sum(grad, 0, keepdims=True), sum_ref.shape)


def d_hidden_of(d, weight, slope, tile=512):
    (rows, width), n = d.shape, weight[0].shape[1]
    tile = min(tile, n)
    out = pl.BlockSpec((rows, tile), lambda j: (0, j))
    return call(
        d_hidden_kernel,
        (n // tile,),
        [whole(d.shape), out, *column_specs(weight, tile, lambda j: (0, j))],
        [out, pl.BlockSpec((8, tile), lambda j: (0, j))],
        [like((rows, n), BF), like((8, n), F32)],
        "d_hidden",
        2 * rows * width * n,
        (d.size + width * n + rows * n * 3) * 2,
    )(d, slope, *weight)


def turn(block, cosine, sine):
    head = block[:, :128]
    lane = lax.broadcasted_iota(jnp.int32, head.shape, 1)
    half = ROTARY // 2
    partner = jnp.where(lane < half, -pltpu.roll(head, 128 - half, 1), pltpu.roll(head, half, 1))
    return jnp.concatenate([head * cosine + partner * sine, block[:, 128:]], 1)


def attend_kernel(
    z_ref, a0_ref, a1_ref, b_ref, cos_ref, sin_ref, *refs
):
    *weight, ctx_ref, pack_ref, log_ref = refs
    z = z_ref[0]
    size = a0_ref.shape[0] // 2
    hd = HEAD_DIM
    scale = hd**-0.5

    def row_of(p):
        return pl.ds(pl.multiple_of((z ^ p) * size, size), size)

    for b in range(4):
        a = (a0_ref, a1_ref)[b // 2][b % 2 * size : (b % 2 + 1) * size, :]
        lin = over_rows(a, weight) + b_ref[...]
        mine = slice(b * size, (b + 1) * size)
        cosine, sine = cos_ref[mine, :], sin_ref[mine, :]
        rows = row_of(b)
        pack_ref[rows, :hd] = turn(lin[:, :hd], cosine, sine).astype(BF)
        pack_ref[rows, hd : 2 * hd] = turn(lin[:, hd : 2 * hd], cosine, sine).astype(BF)
        pack_ref[rows, 2 * hd :] = lin[:, 2 * hd :].astype(BF)
    for p in range(4):
        here, seen = slice(p * size, (p + 1) * size), slice(0, (p + 1) * size)
        scores = dot(pack_ref[here, :hd], pack_ref[seen, hd : 2 * hd], 1, 1) * scale
        row_ids = p * size + lax.broadcasted_iota(jnp.int32, scores.shape, 0)
        col_ids = lax.broadcasted_iota(jnp.int32, scores.shape, 1)
        scores = jnp.where(row_ids >= col_ids, scores, MASKED)
        top = jnp.max(scores, -1, keepdims=True)
        exponent = jnp.exp(scores - top)
        total = jnp.sum(exponent, -1, keepdims=True)
        low = (exponent * (1.0 / total)).astype(BF)
        ctx_ref[row_of(p), :] = dot(low, pack_ref[seen, 2 * hd :], 1, 0).astype(BF)
        log_ref[here, :] = jnp.broadcast_to(top + jnp.log(total), (size, log_ref.shape[1]))


def attend(z, a0, a1, weight, bias, cosine, sine):
    length, width = 2 * a0.shape[0], a0.shape[1]
    hd = HEAD_DIM
    heads = bias.shape[1] // (3 * hd)
    column = lambda rows, cols: pl.BlockSpec((rows, cols), lambda h, p: (0, h))
    return call(
        attend_kernel,
        (heads,),
        [
            whole(a0.shape),
            whole(a1.shape),
            column(1, 3 * hd),
            whole(cosine.shape),
            whole(sine.shape),
            *column_specs(weight, 3 * hd, lambda h, p: (0, h)),
        ],
        [column(length, hd), column(length, 3 * hd), column(length, 128)],
        [like((length, heads * hd), BF), like((length, heads * 3 * hd), BF), like((length, heads * 128), F32)],
        "attend",
        (3 * length * length * hd + 6 * length * width * hd) * heads,
        length * width * 8,
        prefetch=1,
    )(z, a0, a1, bias, cosine, sine, *weight)


def attend_back_kernel(
    z_ref, pack_ref, log_ref, d0_ref, d1_ref, cos_ref, sin_ref, *refs
):
    *weight, dl_ref, us_ref, g_s, dk_s, dv_s = refs
    z = z_ref[0]
    size = d0_ref.shape[0] // 2
    hd = HEAD_DIM
    scale = hd**-0.5

    def row_of(p):
        return pl.ds(pl.multiple_of((z ^ p) * size, size), size)

    for half, d_ref in enumerate((d0_ref, d1_ref)):
        grad = over_rows(d_ref[...], weight).astype(BF)
        g_s[row_of(2 * half), :] = grad[:size]
        g_s[row_of(2 * half + 1), :] = grad[size:]
    dk_s[...] = jnp.zeros_like(dk_s)
    dv_s[...] = jnp.zeros_like(dv_s)
    q_sum = jnp.zeros((1, hd), F32)
    for p in range(4):
        here, seen = slice(p * size, (p + 1) * size), slice(0, (p + 1) * size)
        rows = row_of(p)
        queries, grads = pack_ref[here, :hd], g_s[here, :]
        keys, values = pack_ref[seen, hd : 2 * hd], pack_ref[seen, 2 * hd :]
        scores = dot(queries, keys, 1, 1) * scale
        row_ids = p * size + lax.broadcasted_iota(jnp.int32, scores.shape, 0)
        col_ids = lax.broadcasted_iota(jnp.int32, scores.shape, 1)
        scores = jnp.where(row_ids >= col_ids, scores, MASKED)
        probs = jnp.exp(scores - log_ref[here, 0:1])
        low = probs.astype(BF)
        weight_grad = dot(grads, values, 1, 1)
        score_grad = (
            probs * (weight_grad - jnp.sum(probs * weight_grad, -1, keepdims=True))
        ).astype(BF)
        query_grad = (dot(score_grad, keys, 1, 0) * scale).astype(BF).astype(F32)
        dk_s[seen, :] += dot(score_grad, queries, 0, 0)
        dv_s[seen, :] += dot(low, grads, 0, 0)
        query_grad = turn(query_grad, cos_ref[rows, :], -sin_ref[rows, :])
        q_sum = q_sum + jnp.sum(query_grad, 0, keepdims=True)
        dl_ref[rows, :hd] = query_grad.astype(BF)
    k_sum = jnp.zeros((1, hd), F32)
    v_sum = jnp.zeros((1, hd), F32)
    for p in range(4):
        here = slice(p * size, (p + 1) * size)
        rows = row_of(p)
        key_grad = (dk_s[here, :] * scale).astype(BF).astype(F32)
        key_grad = turn(key_grad, cos_ref[rows, :], -sin_ref[rows, :])
        k_sum = k_sum + jnp.sum(key_grad, 0, keepdims=True)
        dl_ref[rows, hd : 2 * hd] = key_grad.astype(BF)
        value_grad = dv_s[here, :].astype(BF)
        v_sum = v_sum + jnp.sum(value_grad.astype(F32), 0, keepdims=True)
        dl_ref[rows, 2 * hd :] = value_grad
    us_ref[...] = jnp.broadcast_to(jnp.concatenate([q_sum, k_sum, v_sum], 1), us_ref.shape)


def attend_back(z, packed, logs, d0, d1, weight, cosine, sine):
    length, wide = packed.shape
    hd = HEAD_DIM
    heads = wide // (3 * hd)
    first = wide // hd
    column = lambda rows, cols: pl.BlockSpec((rows, cols), lambda h, p: (0, h))
    return call(
        attend_back_kernel,
        (heads,),
        [
            column(length, 3 * hd),
            column(length, 128),
            whole(d0.shape),
            whole(d1.shape),
            whole(cosine.shape),
            whole(sine.shape),
            *column_specs(weight, hd, lambda h, p: (0, first + h)),
        ],
        [column(length, 3 * hd), column(8, 3 * hd)],
        [like((length, wide), BF), like((8, wide), F32)],
        "attend_back",
        (9 * length * length * hd + 2 * length * d0.shape[1] * hd) * heads,
        length * wide * 8,
        prefetch=1,
        scratch=[pltpu.VMEM((length, hd), BF)] + [pltpu.VMEM((length, hd), F32)] * 2,
    )(z, packed, logs, d0, d1, cosine, sine, *weight)


def in_turn(parts, body):
    j = pl.program_id(0)
    each = pl.num_programs(0) // len(parts)
    for k, part in enumerate(parts):

        @pl.when(j // each == k)
        def _(part=part):
            body(*part)


def row_specs(shape, count, parts, col=0):
    each = count // parts
    return [pl.BlockSpec(shape, lambda j, k=k: (jnp.clip(j - k * each, 0, each - 1), col)) for k in range(parts)]


def branch_kernel(parts, a0_ref, a1_ref, ctx_ref, *refs):
    weights, outs = refs[: 2 * parts], refs[2 * parts :]
    size = outs[0].shape[0]

    def body(down_ref, dense_ref):
        for k, act_ref in enumerate((a0_ref, a1_ref)):
            ctx = ctx_ref[2 * k * size : 2 * (k + 1) * size, :]
            part = dot(act_ref[...], down_ref[...], 1, 1) + dot(ctx, dense_ref[...], 1, 1)
            outs[2 * k][...] = part[:size]
            outs[2 * k + 1][...] = part[size:].astype(BF)

    in_turn(list(zip(weights[:parts], weights[parts:])), body)


def token_outs(size, width, tile):
    spec = pl.BlockSpec((size, tile), lambda j: (0, j))
    return [spec] * 4, [like((size, width), F32), like((size, width), BF)] * 2


def branch_of(a0, a1, context_out, down, attn, tile=256):
    rows, n = a0.shape
    parts = len(down)
    width = parts * down[0].shape[0]
    cols = context_out.shape[1]
    count = width // tile
    specs, shapes = token_outs(rows // 2, width, tile)
    return call(
        functools.partial(branch_kernel, parts),
        (count,),
        [
            whole(a0.shape),
            whole(a1.shape),
            whole(context_out.shape),
            *row_specs((tile, n), count, parts),
            *row_specs((tile, cols), count, parts, attn[0].shape[1] // cols - 1),
        ],
        specs,
        shapes,
        "branch",
        4 * rows * width * (n + cols),
        (2 * rows * (n + cols) + width * (n + cols) + 2 * rows * width * 2) * 2,
    )(a0, a1, context_out, *down, *attn)


def input_grad_kernel(
    parts, dl_ref, h0_ref, h1_ref, x0_ref, x1_ref, m0_ref, m1_ref, i0_ref, i1_ref, v_ref, *refs
):
    weights, outs = refs[: 2 * parts], refs[2 * parts :]
    size = outs[0].shape[0]
    wide = dl_ref.shape[1]
    halves = ((h0_ref, x0_ref, m0_ref, i0_ref), (h1_ref, x1_ref, m1_ref, i1_ref))

    def body(attn_ref, up_ref):
        total = [0.0] * 4
        for k, (dh_ref, x_ref, mean_ref, inv_ref) in enumerate(halves):
            attn = dot(dl_ref[2 * k * size : 2 * (k + 1) * size, :], attn_ref[:, :wide], 1, 1)
            mlp = dot(dh_ref[...], up_ref[...], 1, 1)
            part = attn * v_ref[0:1, :] + mlp * v_ref[2:3, :]
            outs[2 * k][...] = part[:size]
            outs[2 * k + 1][...] = part[size:].astype(BF)
            normed = (x_ref[...].astype(F32) - mean_ref[:, 0:1]) * inv_ref[:, 0:1]
            sums = [jnp.sum(v, 0, keepdims=True) for v in (attn * normed, attn, mlp * normed, mlp)]
            total = [u + v for u, v in zip(total, sums)]
        outs[4][...] = jnp.concatenate(total + [jnp.zeros((4, attn.shape[1]), F32)], 0)

    in_turn(list(zip(weights[:parts], weights[parts:])), body)


def input_grad_of(d_linear, h0, h1, attn, up, xs, means, invs, vec, tile=256):
    rows, n = h0.shape
    width = xs[0].shape[1]
    wide = d_linear.shape[1]
    parts = len(attn)
    count = width // tile
    specs, shapes = token_outs(rows // 2, width, tile)
    column = pl.BlockSpec((rows, tile), lambda j: (0, j))
    return call(
        functools.partial(input_grad_kernel, parts),
        (count,),
        [
            whole(d_linear.shape),
            whole(h0.shape),
            whole(h1.shape),
            column,
            column,
            *[whole(a.shape) for a in (*means, *invs)],
            pl.BlockSpec((vec.shape[0], tile), lambda j: (0, j)),
            *row_specs((tile, attn[0].shape[1]), count, parts),
            *row_specs((tile, n), count, parts),
        ],
        [*specs, pl.BlockSpec((8, tile), lambda j: (0, j))],
        [*shapes, like((8, width), F32)],
        "input_grad",
        4 * rows * width * (n + wide),
        (2 * rows * (n + wide) + width * (n + wide) + 2 * rows * width * 3) * 2,
    )(d_linear, h0, h1, *xs, *means, *invs, vec, *attn, *up)


def grad_kernel(pairs, added, pieces, *refs):
    operands, adds, outs = refs[: 4 * pairs], refs[4 * pairs : 4 * pairs + added], refs[4 * pairs + added :]
    j = pl.program_id(0)
    col = 0
    for k in range(pairs):
        l0, l1, r0, r1 = (r[...] for r in operands[4 * k : 4 * k + 4])
        part = dot(l0, r0, 0, 0) + dot(l1, r1, 0, 0)
        cols = slice(col, col + part.shape[1])
        col += part.shape[1]
        half = part.shape[0] // 2
        for i, places in enumerate(pieces):

            @pl.when(j == i)
            def _(i=i, places=places, part=part, cols=cols):
                for k in range(added):
                    if k == i * added // 4:
                        part = part + adds[k][:, cols].astype(F32)
                for side, (piece, block) in enumerate(places):
                    outs[piece][block * half : (block + 1) * half, cols] = part[side * half : (side + 1) * half].astype(BF)


def grad_of(factors, pieces, sizes, adds=()):
    width = factors[0][0].shape[1]
    tile = width // 8
    first = 0 if adds else 4
    in_specs, operands, n, flops, nbytes = [], [], 0, 0, 0
    for l0, l1, r0, r1 in factors:
        rows = l0.shape[0]
        for left in (l0, l1):
            in_specs.append(pl.BlockSpec((rows, tile), lambda j: (0, first + j)))
            operands.append(left)
        cols = r0[0].shape[1]
        for right, k in (r0, r1):
            in_specs.append(pl.BlockSpec((rows, cols), lambda j, k=k: (k, 0), pipeline_mode=pl.Buffered(1)))
            operands.append(right)
        n += cols
        flops += 2 * rows * width * cols
        nbytes += 2 * rows * (width + 2 * cols)
    each = 4 // max(len(adds), 1)
    in_specs += [
        pl.BlockSpec((tile, n), lambda j, k=k: (jnp.clip(j - k * each, 0, each - 1), 0)) for k in range(len(adds))
    ]
    shapes = [(size * tile // 2, n) for size in sizes]
    return call(
        functools.partial(grad_kernel, len(factors), len(adds), pieces),
        (4,),
        in_specs,
        [whole(shape) for shape in shapes],
        [like(shape, BF) for shape in shapes],
        "grad_near" if adds else "grad_far",
        flops,
        nbytes + width * n,
    )(*operands, *adds)


def fold_kernel(cross, keep_ref, got_ref, o_ref):
    for j, k in enumerate(cross):
        here = slice(j * BLOCK, (j + 1) * BLOCK)
        o_ref[:, k * BLOCK : (k + 1) * BLOCK] = (keep_ref[:, here] + got_ref[:, here].astype(F32)).astype(BF)


def fold(cross, keep, got):
    rows, width = keep.shape
    tile = rows // 2
    block = pl.BlockSpec((tile, width), lambda i: (i, 0))
    return call(
        functools.partial(fold_kernel, cross), (2,), [block, block], block, like(keep.shape, BF), "fold", keep.size, keep.size * 8
    )(keep, got)


def finish_kernel(place_ref, o0_ref, o1_ref, g0_ref, g1_ref, x_ref, d_ref, out_ref, grad_ref):
    width = x_ref.shape[1]
    count = width // BLOCK
    x = x_ref[...].astype(F32)
    center = x - jnp.mean(x, -1, keepdims=True)
    inv_std = lax.rsqrt(jnp.mean(center * center, -1, keepdims=True) + EPSILON)
    normed = center * inv_std

    def body(o_ref, g_ref):
        g = g_ref[...].astype(F32)
        grad = d_ref[...].astype(F32) + inv_std * (
            g - jnp.mean(g, -1, keepdims=True) - normed * jnp.mean(g * normed, -1, keepdims=True)
        )
        for j in range(count):
            col = pl.ds(pl.multiple_of(place_ref[j] * BLOCK, BLOCK), BLOCK)
            part = slice(j * BLOCK, (j + 1) * BLOCK)
            out_ref[:, col] = o_ref[:, part]
            grad_ref[:, col] = grad[:, part]

    in_turn(((o0_ref, g0_ref), (o1_ref, g1_ref)), body)


def finish(place, o0, o1, g0, g1, x, d):
    rows, width = o0.shape
    per = 2
    tile = rows // per
    at = 2 * width // BLOCK
    first = pl.BlockSpec((tile, width), lambda i, p: (jnp.minimum(i, per - 1), 0))
    second = pl.BlockSpec((tile, width), lambda i, p: (jnp.maximum(i - per, 0), 0))
    local = pl.BlockSpec((tile, width), lambda i, p: (i, 0))
    out = pl.BlockSpec((tile, width), lambda i, p: ((p[at] ^ (i // per)) * per + i % per, 0))
    return call(
        finish_kernel,
        (2 * per,),
        [first, second, first, second, local, local],
        [out, out],
        [like(x.shape, BF), like(x.shape, F32)],
        "finish",
        x.size * 20,
        x.size * 14,
        prefetch=1,
    )(place, o0, o1, g0, g1, x, d)


def step_values(weight, first, root, gradient, fix_one, fix_two, decay_rate):
    first_new = BETA_ONE * first + (1.0 - BETA_ONE) * gradient
    root_new = jnp.sqrt(BETA_TWO * root * root + (1.0 - BETA_TWO) * gradient * gradient)
    change = -LEARN_RATE * (
        first_new / fix_one / (root_new / fix_two + 1e-08) + decay_rate * weight
    )
    return first_new, root_new, change


def adam_kernel(c_ref, fix_ref, w_ref, m_ref, a_ref, b_ref, e_ref, t_ref, g_ref, n_ref, u_ref):
    def body(gradient):
        first, root, change = step_values(
            w_ref[...].astype(F32), m_ref[0], m_ref[1], gradient, fix_ref[0], fix_ref[1], WEIGHT_DECAY
        )
        g_ref[...] = gradient
        n_ref[0] = first
        n_ref[1] = root
        u_ref[...] = change

    @pl.when(pl.program_id(0) == 0)
    def _():
        body(a_ref[...].astype(F32) + b_ref[...].astype(F32) + e_ref[...].astype(F32))

    @pl.when(pl.program_id(0) == 1)
    def _():
        body(t_ref[...].astype(F32))


def adam(ctx, fixes, weight, moments, terms, theirs, tile=2048, first=0):
    rows, cols = weight.shape
    n = cols // 2
    tile = min(tile, n)
    first //= tile
    per = n // tile
    at = lambda k, i, c: (0, (c[0] ^ k) * per + i)
    mine = pl.BlockSpec((rows, tile), lambda k, i, c: (0, first + i + k * (per - 1 - i)))
    other = pl.BlockSpec((rows, tile), lambda k, i, c: (0, first + i * k))
    matrix = pl.BlockSpec((rows, tile), at)
    pair = pl.BlockSpec((2, rows, tile), lambda k, i, c: (0, *at(k, i, c)))
    return call(
        adam_kernel,
        (2, per),
        [pl.BlockSpec(memory_space=pltpu.SMEM), matrix, pair, mine, mine, mine, other],
        [matrix, pair, matrix],
        [like(weight.shape, F32), like(moments.shape, F32), like(weight.shape, F32)],
        "adam",
        weight.size * 20,
        weight.size * 30,
        prefetch=1,
    )(ctx, fixes, weight, moments, *terms, theirs)


def adam_heads_kernel(c_ref, fix_ref, w_ref, m_ref, a_ref, b_ref, e_ref, t_ref, g_ref, n_ref, u_ref):
    mine = a_ref[...].astype(F32) + b_ref[...].astype(F32) + e_ref[...].astype(F32)
    theirs = t_ref[...].astype(F32)
    heads, wide = w_ref.shape[1] // 2, w_ref.shape[2]
    for h in range(2 * heads):
        cols = slice(h % heads * wide, (h % heads + 1) * wide)
        gradient = jnp.where(c_ref[0] == h // heads, mine[:, cols], theirs[:, cols])
        first, root, change = step_values(
            w_ref[:, h, :].astype(F32), m_ref[0, :, h, :], m_ref[1, :, h, :], gradient, fix_ref[0], fix_ref[1], WEIGHT_DECAY
        )
        g_ref[:, h, :] = gradient
        n_ref[0, :, h, :] = first
        n_ref[1, :, h, :] = root
        u_ref[:, h, :] = change


def adam_heads(ctx, fixes, weight, moments, terms, theirs):
    rows, heads, wide = weight.shape
    tile = rows // 4
    part = pl.BlockSpec((tile, heads // 2 * wide), lambda i, c: (i, 0))
    cube = pl.BlockSpec((tile, heads, wide), lambda i, c: (i, 0, 0))
    pair = pl.BlockSpec((2, tile, heads, wide), lambda i, c: (0, i, 0, 0))
    return call(
        adam_heads_kernel,
        (4,),
        [pl.BlockSpec(memory_space=pltpu.SMEM), cube, pair, part, part, part, part],
        [cube, pair, cube],
        [like(weight.shape, F32), like(moments.shape, F32), like(weight.shape, F32)],
        "adam_heads",
        weight.size * 20,
        weight.size * 30,
        prefetch=1,
    )(ctx, fixes, weight, moments, *terms, theirs)


def rotary_tables(positions):
    lane = jnp.arange(128)
    inverse = jnp.exp((lane % (ROTARY // 2)).astype(F32) * (-2.0 / ROTARY) * math.log(10000.0))
    angles = positions.astype(F32)[:, None] * inverse[None, :]
    turned = lane[None, :] < ROTARY
    return (jnp.where(turned, jnp.cos(angles), 1.0), jnp.where(turned, jnp.sin(angles), 0.0))


def adam_step(weight, moments, gradient, count_value, decay_rate):
    first_new = BETA_ONE * moments[0] + (1.0 - BETA_ONE) * gradient
    root_new = jnp.sqrt(BETA_TWO * moments[1] * moments[1] + (1.0 - BETA_TWO) * gradient * gradient)
    fix_one = 1.0 - jnp.power(BETA_ONE, count_value)
    fix_two = 1.0 - jnp.power(BETA_TWO, count_value)
    change = -LEARN_RATE * (
        first_new / fix_one / (root_new / jnp.sqrt(fix_two) + 1e-08) + decay_rate * weight
    )
    return (jnp.stack([first_new, root_new]), change)


def on_device(
    shard_count,
    inputs,
    cotangent,
    qkv_weight,
    dense_weight,
    up_weight,
    down_weight,
    unit_biases,
    vectors,
    qkv_moments,
    dense_moments,
    up_moments,
    down_moments,
    unit_moments,
    vector_moments,
    step_count,
):
    ORDER.clear()
    CALLS.clear()
    shard, ctx, ten = (lax.axis_index(a) for a in ("shard", "context", "tensor"))
    fast = shard_count == 8
    _, local_len, width = inputs.shape
    quarter = local_len // 2
    row_count, heads_local, head_wide = qkv_weight.shape
    heads = heads_local // 2
    units = up_weight.shape[1] // 2
    head_cols = heads * HEAD_DIM
    n_qkv = heads * head_wide
    count = width // BLOCK

    def along(axis, size, bit):
        return lambda v: lax.ppermute(v, axis, [(i, i ^ bit) for i in range(size)])

    to_core, to_x, to_y = (along("shard", shard_count, bit) for bit in (1, 2, 4))
    to_ctx, to_ten = along("context", 2, 1), along("tensor", 2, 1)

    if fast:
        chips = ((0, 4, 2, 6), (0, 2, 4, 6))
        relative = [(core + chips[ab][k], ab) for core in range(2) for ab in range(2) for k in range(4)]
        places = [[(shard ^ s) * 2 + (ctx ^ f ^ ab) for s, ab in relative] for f in range(2)]
        cross = [core * 8 + (1 - ab) * 4 + (0, 2, 1, 3)[k] for core in range(2) for ab in range(2) for k in range(4)]
    else:
        places = [[jnp.int32(j) for j in range(count)]] * 2
        cross = list(range(count))
    place = jnp.stack([*places[0], *places[1], ten]).astype(jnp.int32)
    z = ctx * 2 + ten
    ctx_scalar, z_scalar = (v.reshape(1).astype(jnp.int32) for v in (ctx, z))

    def wait(*values):
        ORDER.extend(values)

    def full_rows(mine, other):
        block = jnp.where(ctx == 0, jnp.concatenate([mine, other], 0), jnp.concatenate([other, mine], 0))
        full = lax.all_gather(block, "shard", axis=0, tiled=True)
        return tuple(full[k * width // 4 : (k + 1) * width // 4] for k in range(4))

    r = row_count
    x_in, d_in = inputs.reshape(local_len, width), cotangent.reshape(local_len, width)
    unit_vals = unit_biases.astype(F32)
    my_units = lax.dynamic_slice_in_dim(unit_vals, ctx * heads, heads, 0)
    qkv_bias, unit_bias = my_units[:, :head_wide].reshape(1, n_qkv), my_units[:, head_wide:].reshape(1, units)
    positions = ((jnp.arange(4) ^ z)[:, None] * quarter + jnp.arange(quarter)[None, :]).reshape(-1)
    cosine, sine = rotary_tables(positions)

    n = up_weight.shape[1] // 2
    units_other = to_ctx(cut_quarter(ctx_scalar, 1, up_weight, down_weight))
    mine = cut_quarter(ctx_scalar, 0, up_weight, down_weight, qkv_weight, dense_weight)
    if fast:
        a_x, a_y = to_x(mine), to_y(mine)
    x_own, d_own, vec = arrange(place, x_in, d_in, vectors)
    attn_own, mlp_own, mean_own, inv_own = norm(x_own, vec)
    if fast:
        top, low = halves(a_y, a_x)
        a_top, a_low = to_x(top), to_y(low)
    wait(units_other)
    attn_other = to_ctx(cut_quarter(ctx_scalar, 1, qkv_weight, dense_weight))
    if fast:
        units_x, units_y = to_x(units_other), to_y(units_other)
    wait(attn_other)
    x_first = to_ctx(outgoing(place, x_in))

    def packed(pieces, k):
        near = pack(n, *[(a, k) for a in pieces])
        return near, to_core(near)

    if fast:
        mine_parts = (mine, a_y, a_x, a_top, a_low)
        up_a, up_far_a = packed(mine_parts, 0)
        down_a, down_far_a = packed(mine_parts, 1)
        top, low = halves(units_y, units_x)
        units_parts = (units_other, units_x, units_y, to_x(top), to_y(low))
        attn_x, attn_y = to_x(attn_other), to_y(attn_other)
        attn_a, attn_far_a = packed(mine_parts, 2)
        up_b, up_far_b = packed(units_parts, 0)
        top, low = halves(attn_y, attn_x)
        attn_parts = (attn_other, attn_x, attn_y, to_x(top), to_y(low))
        down_b, down_far_b = packed(units_parts, 1)
        w_up, w_down = (up_a, up_b, up_far_a, up_far_b), (down_a, down_b, down_far_a, down_far_b)
    else:
        w_up = full_rows(mine[:, :n], units_other[:, :n])
        w_down = full_rows(mine[:, n : 2 * n], units_other[:, n:])
        w_attn = full_rows(mine[:, 2 * n :], attn_other)
    active_own, slope_own = hidden_of(mlp_own, w_up, unit_bias)
    if fast:
        attn_b, attn_far_b = packed(attn_parts, 0)
        w_attn = (attn_a, attn_b, attn_far_a, attn_far_b)
    wait(x_first)
    d_first = to_ctx(outgoing(place, d_in))
    x_second = to_ten(x_first)
    low_own, sum_own = d_hidden_of(d_own, w_down, slope_own)
    x_oth = pack(width, x_first, x_second)
    attn_oth, mlp_oth, mean_oth, inv_oth = norm(x_oth, vec)
    active_oth, slope_oth = hidden_of(mlp_oth, w_up, unit_bias)
    wait(d_first)
    d_second = to_ten(d_first)
    context_out, packed_qkv, logs = attend(z_scalar, attn_own, attn_oth, w_attn, qkv_bias, cosine, sine)
    *branch_own, branch_keep, branch_send = branch_of(active_own, active_oth, context_out, w_down, w_attn)
    branch_got = to_ten(branch_send)
    branch_near = to_ten(branch_own[1])
    d_oth = pack(width, d_first, d_second)

    def far_parts(factors, count):
        each = 4 // count
        steps = [[(k // each, k % each * 2), (k // each, k % each * 2 + 1)] for k in range(4)]
        parts = grad_of(factors, steps, (2 * each,) * count)
        return [to_core(part) for part in parts] if fast else parts

    def near_parts(factors, far):
        if not fast:
            (near,) = grad_of(factors, [[(0, 2 * k), (0, 2 * k + 1)] for k in range(4)], (8,), [jnp.zeros_like(part) for part in far])
            return lax.psum_scatter(jnp.concatenate([near, *far], 0), "shard", scatter_dimension=0, tiled=True)
        a_own, a_x, b_own, b_y = grad_of(factors, [[(k, 0), (k, 1)] for k in range(4)], (2, 2, 2, 2), far)
        return a_own, b_own, to_y(b_y), to_x(a_x)

    def second(parts):
        if not fast:
            return parts
        a_own, b_own, b_got, a_got = parts
        b_sum, a_sum = totals(r, ((b_own, 1), (b_got, 1)), ((a_own, 1), (a_got, 1)))
        return (*parts, to_x(b_sum), to_y(a_sum))

    def third(parts):
        if not fast:
            kept = lax.dynamic_slice_in_dim(parts, ctx * r, r, 0)
            zero = jnp.zeros_like(kept)
            return (kept, zero, zero), to_ctx(lax.dynamic_slice_in_dim(parts, (1 - ctx) * r, r, 0))
        a_own, b_own, b_got, a_got, b_last, a_last = parts
        wait(a_last)
        (away,) = totals(r, ((b_own, 0), (b_got, 0), (b_last, 0)))
        return (a_own, a_got, a_last), to_ctx(away)

    low_oth, sum_oth = d_hidden_of(d_oth, w_down, slope_oth)
    unit_factors = [(mlp_own, mlp_oth, (low_own, 0), (low_oth, 0)), (d_own, d_oth, (active_own, 0), (active_oth, 0))]
    unit_far = far_parts(unit_factors, 1)
    branch_far = to_ctx(fold(cross, branch_keep, branch_got))
    d_linear, unit_sums = attend_back(z_scalar, packed_qkv, logs, d_own, d_oth, w_attn, cosine, sine)
    unit_pieces = near_parts(unit_factors, unit_far)
    wait(branch_near)
    *g_own, g_keep, g_send, sums = input_grad_of(
        d_linear, low_own, low_oth, w_attn, w_up, (x_own, x_oth), (mean_own, mean_oth), (inv_own, inv_oth), vec
    )
    g_got = to_ten(g_send)
    g_near = to_ten(g_own[1])
    attn_factors = [
        (attn_own, attn_oth, (d_linear, 0), (d_linear, 1)),
        (d_own, d_oth, (context_out, 0), (context_out, 1)),
    ]
    d_sum = jnp.sum(d_own[:quarter].astype(F32), 0, keepdims=True)
    sums = unorder(place, jnp.concatenate([sums[:4], d_sum, jnp.zeros((3, width), F32)], 0))
    unit_part = jnp.concatenate(
        [unit_sums[0].reshape(heads, head_wide), (sum_own + sum_oth)[0].reshape(heads, units // heads)], 1
    )
    unit_rows = jnp.where(jnp.arange(4)[:, None, None] == ten * 2 + ctx, unit_part[None], 0.0)
    total = jnp.concatenate([sums.reshape(-1), unit_rows.reshape(-1)]).reshape(-1, BLOCK)
    moves = [to_ctx] + [along("shard", shard_count, 1 << k) for k in range(shard_count.bit_length() - 1)] + [to_ten]
    moved = moves[0](total)

    def shared(total, moved, moves):
        (total,) = totals(total.shape[0], ((total, 0), (moved, 0)), dtype=F32)
        return total, moves[0](total) if moves else None

    attn_far = far_parts(attn_factors, 1)
    out_bias = (vec[4] + vec[5]).reshape(1, width)
    (out_own,) = totals(quarter, ((branch_own[0], 0), (branch_near, 0), (branch_far, 0), (x_own, 0), (out_bias, 0)), steps=2)
    out_other = to_ten(out_own)
    unit_pieces = second(unit_pieces)
    g_far = to_ctx(fold(cross, g_keep, g_got))
    total, moved = shared(total, moved, moves[1:2])
    attn_pieces = near_parts(attn_factors, attn_far)
    unit_terms, unit_theirs = third(unit_pieces)
    (g_sum,) = totals(quarter, ((g_own[0], 0), (g_near, 0), (g_far, 0)), steps=2)
    g_other = to_ten(g_sum)
    total, moved = shared(total, moved, moves[2:3])
    wait(out_other)
    attn_pieces = second(attn_pieces)
    total, moved = shared(total, moved, moves[3:4])
    attn_terms, attn_theirs = third(attn_pieces)
    total, moved = shared(total, moved, moves[4:5])

    count_value = step_count.astype(F32)
    fixes = jnp.stack([1.0 - jnp.power(BETA_ONE, count_value), jnp.sqrt(1.0 - jnp.power(BETA_TWO, count_value))])
    up_grad, up_new, up_change = adam(ctx_scalar, fixes, up_weight, up_moments, unit_terms, unit_theirs)
    down_grad, down_new, down_change = adam(ctx_scalar, fixes, down_weight, down_moments, unit_terms, unit_theirs, first=n)
    outputs, input_grad = finish(place, out_own, out_other, g_sum, g_other, x_own, d_own)
    for k in range(5, len(moves) + 1):
        total, moved = shared(total, moved, moves[k : k + 1])
    total = total.reshape(-1)
    vector_grad = total[: 5 * width].reshape(5, width)
    vector_grad = jnp.concatenate([vector_grad, vector_grad[4:]], 0)
    unit_all = total[8 * width :].reshape(4 * heads, unit_part.shape[1])
    unit_grad = lax.dynamic_slice_in_dim(unit_all, ten * 2 * heads, 2 * heads, 0)
    qkv_grad, qkv_new, qkv_change = adam_heads(ctx_scalar, fixes, qkv_weight, qkv_moments, attn_terms, attn_theirs)
    dense_grad, dense_new, dense_change = adam(
        ctx_scalar, fixes, dense_weight, dense_moments, attn_terms, attn_theirs, tile=head_cols, first=n_qkv
    )
    unit_new, unit_change = adam_step(unit_vals, unit_moments, unit_grad, count_value, 0.0)
    vector_new, vector_change = adam_step(vectors.astype(F32), vector_moments, vector_grad, count_value, 0.0)
    return (
        outputs.reshape(inputs.shape),
        input_grad.reshape(inputs.shape),
        qkv_grad,
        dense_grad,
        up_grad,
        down_grad,
        unit_grad,
        vector_grad,
        qkv_new,
        dense_new,
        up_new,
        down_new,
        unit_new,
        vector_new,
        qkv_change,
        dense_change,
        up_change,
        down_change,
        unit_change,
        vector_change,
    )


def solution(mesh):
    rows = ("shard", "context")
    tokens = P("shard", "context", None)
    qkv, matrix, units = P(rows, "tensor", None), P(rows, "tensor"), P("tensor", None)
    qkv_pair, matrix_pair, units_pair = P(None, rows, "tensor", None), P(None, rows, "tensor"), P(None, "tensor", None)
    params = (qkv, matrix, matrix, matrix, units, P())
    states = (qkv_pair, matrix_pair, matrix_pair, matrix_pair, units_pair, P())
    return jax.shard_map(
        functools.partial(on_device, mesh.shape["shard"]),
        mesh=mesh,
        in_specs=(tokens, tokens, *params, *states, P()),
        out_specs=(tokens, tokens, *params, *states, *params),
        check_vma=False,
    )
```
